32 devices in a mesh: tgt: 16 (over z, y, core), sup: 2 (over x).
Axes of the slice: x: 2, y: 2, z: 4, core: 2. Of those that a mesh axis runs over, the one named last changes fastest.
Arguments:
- targets: bfloat16 [3584, 12288], P('tgt', 'sup'), may hold values from -6 to 6, as said below
- support: bfloat16 [128, 12288], P('sup'), may hold values from -6 to 6, as said below
- label_weights: bfloat16 [128, 1000], P('sup'), may hold values from -0.00390625 to 0.00390625
- labels: int32 [3584], P('tgt'), may hold values from 0 to 999
- first_moment: float32 [128, 12288], P('sup', 'tgt'), may hold values from -0.6 to 0.6
- second_moment: float32 [128, 12288], P('sup', 'tgt'), may hold values from 0.001 to 0.1
Outputs:
- new_support: bfloat16 [128, 12288], P('sup')
- new_first: float32 [128, 12288], P('sup', 'tgt')
- new_second: float32 [128, 12288], P('sup', 'tgt')
The draws below stay inside these ranges and needn't reach their ends.
Inputs may be any that keep to these rules, and one draw needn't show every extreme that they name: `targets`: image pixel values. `support`: image pixel values.
All inputs are finite; a program needn't handle non-finite values.
Results may differ from the reference program's by a relative error of at most 0.0028.
Values may be sent and summed in bfloat16 or wider, within the bound.
A program may use at most 64 MiB of HBM per device.

```python
import math
import jax
import jax.numpy as jnp
from jax import lax

P_SIZE = 12288
C = 1000
DEPTH = 3
NT = 3584
NS = 128


pattern_count = 256


def image_rows(key, count_rows, salt):
    patterns = jax.random.randint(jax.random.fold_in(key, 101), (pattern_count, P_SIZE), -4, 5).astype(jnp.float32)
    mixing = jax.random.randint(jax.random.fold_in(key, salt), (count_rows, pattern_count), -3, 4).astype(jnp.float32)
    shared = jnp.dot(mixing, patterns, precision=lax.Precision.HIGHEST) / math.sqrt(pattern_count * 60.0 / 9.0 * 4.0)
    ramp = jnp.exp(jnp.linspace(math.log(0.5), math.log(1.6), P_SIZE, dtype=jnp.float32))
    rough = jax.random.uniform(jax.random.fold_in(key, 102), (P_SIZE,), jnp.float32, 0.8, 1.2)
    noise = 0.5 * jax.random.normal(jax.random.fold_in(key, salt + 1), (count_rows, P_SIZE), jnp.float32)
    images = shared + noise
    return jnp.clip(images * (ramp * rough)[None, :], -6.0, 6.0)


def draw_targets(key, part):
    return image_rows(key, NT, 7).astype(jnp.bfloat16)


def draw_support(key, part):
    return image_rows(key, NS, 17).astype(jnp.bfloat16)


def set_ends(drawn, stream_key, least, largest):
    place = [jax.random.randint(jax.random.fold_in(stream_key, axis), (), 0, length) for axis, length in enumerate(drawn.shape)]
    main_axis = drawn.shape.index(max(drawn.shape))
    next_to = place[:main_axis] + [(place[main_axis] + 1) % drawn.shape[main_axis]] + place[main_axis + 1:]
    return drawn.at[tuple(place)].set(least).at[tuple(next_to)].set(largest)


def level_of(key, dims, pieces, least, largest):
    gain = 1.0
    for position, shards_of in pieces:
        draws = jax.random.uniform(jax.random.fold_in(jax.random.fold_in(key, 6), position), (shards_of,), jnp.float32, least / len(pieces), largest / len(pieces))
        gain = gain * jnp.repeat(jnp.exp(draws), dims[position] // shards_of).reshape((-1,) + (1,) * (len(dims) - 1 - position))
    return gain


def bell_draw(own_key, extent, width, bound, pieces=(), kind=jnp.bfloat16):
    result = width * jax.random.normal(own_key, extent, jnp.float32)
    if pieces:
        result = result * level_of(own_key, extent, pieces, -0.22, 0.18)
    return jnp.clip(result, -bound, bound).astype(kind)


def setup_inputs(seed: int = 0) -> dict:
    keys = jax.random.split(jax.random.key(seed), 7)
    targets = draw_targets(jax.random.fold_in(keys[6], 71), 0)
    support = draw_support(jax.random.fold_in(keys[6], 71), 0)
    label_weights = bell_draw(keys[2], (NS, C), (16 * C * NS) ** -0.5, 0.00390625, ((0, 2),))
    labels = set_ends(jax.random.randint(keys[3], (NT,), 0, C), jax.random.fold_in(keys[3], 1), 0, C - 1).astype(jnp.int32)
    first_moment = bell_draw(keys[4], (NS, P_SIZE), 0.1, 0.6, ((0, 2), (1, 16)), jnp.float32)
    second_moment = jnp.clip(jnp.exp(math.log(0.1) - 4.6051702 * jax.random.uniform(keys[5], (NS, P_SIZE), jnp.float32) ** level_of(keys[5], (NS, P_SIZE), ((0, 2), (1, 16)), -0.2, 0.2)), 0.001, 0.1)
    return dict(targets=targets, support=support, label_weights=label_weights, labels=labels, first_moment=first_moment, second_moment=second_moment)


bias_var = 0.1
learning_rate = 0.05
first_decay = 0.9
second_decay = 0.99
first_fix = 1.0 - 0.9 ** 10
second_fix = 1.0 - 0.99 ** 10
adam_eps = 1e-08

def tangent_kernel(cross, target_diag, support_diag):
    tangent = cross
    current = cross
    left_diag = target_diag
    right_diag = support_diag
    for _ in range(DEPTH):
        product = (1.0 + 2.0 * left_diag)[:, None] * (1.0 + 2.0 * right_diag)[None, :]
        slope = 4.0 / math.pi / jnp.sqrt(product - 4.0 * current * current)
        current = 2.0 / math.pi * jnp.arcsin(2.0 * current / jnp.sqrt(product)) + bias_var
        tangent = current + slope * tangent
        left_diag = 2.0 / math.pi * jnp.arcsin(2.0 * left_diag / (1.0 + 2.0 * left_diag)) + bias_var
        right_diag = 2.0 / math.pi * jnp.arcsin(2.0 * right_diag / (1.0 + 2.0 * right_diag)) + bias_var
    return tangent

def reference(targets, support, label_weights, labels, first_moment, second_moment):
    cross = jnp.dot(targets, support.T, preferred_element_type=jnp.float32) / P_SIZE + bias_var
    target_diag = lax.optimization_barrier(jnp.sum(jnp.square(targets.astype(jnp.float32)), axis=1)) / P_SIZE + bias_var
    support_diag = lax.optimization_barrier(jnp.sum(jnp.square(support.astype(jnp.float32)), axis=1)) / P_SIZE + bias_var

    def kernel_of(cross_in, diag_in):
        return tangent_kernel(cross_in, target_diag, diag_in)
    kernel, pullback = jax.vjp(kernel_of, cross, support_diag)
    predicted = jnp.dot(kernel.astype(jnp.bfloat16), label_weights, preferred_element_type=jnp.float32)
    classes = jnp.arange(C, dtype=jnp.int32)
    onehot = (labels[:, None] == classes[None, :]).astype(jnp.float32)
    residual = (predicted - onehot).astype(jnp.bfloat16)
    loss_scale = 4.0 * P_SIZE * math.sqrt(C * NS / NT)
    kernel_grad = jnp.dot(residual, label_weights.T, preferred_element_type=jnp.float32) * loss_scale
    cross_grad, norm_grad = pullback(kernel_grad)
    cross_low = cross_grad.astype(jnp.bfloat16)
    gradient = (jnp.dot(cross_low.T, targets, preferred_element_type=jnp.float32) + 2.0 * norm_grad[:, None] * support.astype(jnp.float32)) / P_SIZE
    new_first = first_decay * first_moment + (1.0 - first_decay) * gradient
    new_second = second_decay * second_moment + (1.0 - second_decay) * gradient * gradient
    update = learning_rate * (new_first / first_fix) / (jnp.sqrt(new_second / second_fix) + adam_eps)
    new_support = (support.astype(jnp.float32) - update).astype(jnp.bfloat16)
    return (new_support, new_first, new_second)
```

```python
import functools
import math

import jax
import jax.numpy as jnp
from jax import lax
from jax.experimental import pallas as pl
from jax.experimental.pallas import tpu as pltpu
from jax.sharding import PartitionSpec as P

DEPTH = 3


bias_var = 0.1
learning_rate = 0.05
first_decay = 0.9
second_decay = 0.99
first_fix = 1.0 - 0.9**10
second_fix = 1.0 - 0.99**10
adam_eps = 1e-08


def tangent_kernel(cross, target_diag, support_diag):
    tangent = cross
    current = cross
    left_diag = target_diag
    right_diag = support_diag
    for _ in range(DEPTH):
        product = (1.0 + 2.0 * left_diag)[:, None] * (1.0 + 2.0 * right_diag)[None, :]
        slope = 4.0 / math.pi / jnp.sqrt(product - 4.0 * current * current)
        current = 2.0 / math.pi * jnp.arcsin(2.0 * current / jnp.sqrt(product)) + bias_var
        tangent = current + slope * tangent
        left_diag = 2.0 / math.pi * jnp.arcsin(2.0 * left_diag / (1.0 + 2.0 * left_diag)) + bias_var
        right_diag = (
            2.0 / math.pi * jnp.arcsin(2.0 * right_diag / (1.0 + 2.0 * right_diag)) + bias_var
        )
    return tangent


def row_squares(images):
    return jnp.sum(jnp.square(images.astype(jnp.float32)), axis=1)


def shards(targets, support, label_weights, labels, first_moment, second_moment):
    pixels = support.shape[1]
    target_count = targets.shape[0] * lax.axis_size("tgt")
    support_count = support.shape[0] * lax.axis_size("sup")
    class_count = label_weights.shape[1]
    support_diag = row_squares(support) / pixels + bias_var
    slabs = lax.all_to_all(support, "sup", split_axis=1, concat_axis=0, tiled=True)
    partial_cross = lax.dot_general(
        targets, slabs, (((1,), (1,)), ((), ())), preferred_element_type=jnp.float32
    )
    cross = (
        lax.psum_scatter(
            partial_cross.astype(jnp.bfloat16), "sup", scatter_dimension=1, tiled=True
        ).astype(jnp.float32)
        / pixels
        + bias_var
    )
    target_diag = lax.psum(row_squares(targets), "sup") / pixels + bias_var

    def kernel_of(cross_in, diag_in):
        return tangent_kernel(cross_in, target_diag, diag_in)

    kernel, pullback = jax.vjp(kernel_of, cross, support_diag)
    partial_pred = jnp.dot(
        kernel.astype(jnp.bfloat16), label_weights, preferred_element_type=jnp.float32
    )
    predicted = lax.psum(partial_pred.astype(jnp.bfloat16), "sup").astype(jnp.float32)
    classes = jnp.arange(class_count, dtype=jnp.int32)
    onehot = (labels[:, None] == classes[None, :]).astype(jnp.float32)
    residual = (predicted - onehot).astype(jnp.bfloat16)
    kernel_grad = lax.dot_general(
        residual, label_weights, (((1,), (1,)), ((), ())), preferred_element_type=jnp.float32
    )
    kernel_grad = kernel_grad * (
        4.0 * pixels * math.sqrt(class_count * support_count / target_count)
    )
    cross_grad, norm_grad = pullback(kernel_grad)
    cross_low = cross_grad.astype(jnp.bfloat16)
    all_grads = lax.all_gather(cross_low, "sup", axis=1, tiled=True)
    slab_grad = lax.dot_general(
        all_grads, targets, (((0,), (0,)), ((), ())), preferred_element_type=jnp.float32
    )
    image_grad = lax.all_to_all(
        slab_grad.astype(jnp.bfloat16), "sup", split_axis=0, concat_axis=1, tiled=True
    ).astype(slab_grad.dtype)
    gradient = (image_grad + 2.0 * norm_grad[:, None] * support.astype(jnp.float32)) / pixels
    shares = lax.psum_scatter(gradient, "tgt", scatter_dimension=1, tiled=True)
    slab_width = shares.shape[1]
    own_pixels = lax.dynamic_slice_in_dim(
        support, lax.axis_index("tgt") * slab_width, slab_width, 1
    ).astype(jnp.float32)
    new_first = first_decay * first_moment + (1.0 - first_decay) * shares
    new_second = second_decay * second_moment + (1.0 - second_decay) * shares * shares
    update = (
        learning_rate * (new_first / first_fix) / (jnp.sqrt(new_second / second_fix) + adam_eps)
    )
    new_slab = (own_pixels - update).astype(jnp.bfloat16)
    new_support = lax.all_gather(new_slab, "tgt", axis=1, tiled=True)
    return (new_support, new_first, new_second)


MESH = pl.DeviceIdType.MESH
f32 = jnp.float32
bf16 = jnp.bfloat16


@jax.custom_jvp
def arcsine(x):
    a = jnp.abs(x)
    big = a > 0.5
    z = jnp.where(big, 0.5 * (1.0 - a), a * a)
    s = jnp.where(big, jnp.sqrt(z), a)
    p = 4.2163199048e-2 * z + 2.4181311049e-2
    p = p * z + 4.5470025998e-2
    p = p * z + 7.4953002686e-2
    p = p * z + 1.6666752422e-1
    p = p * z * s + s
    r = jnp.where(big, math.pi / 2.0 - 2.0 * p, p)
    return jnp.where(x < 0.0, -r, r)


@arcsine.defjvp
def arcsine_jvp(primals, tangents):
    (x,) = primals
    (t,) = tangents
    return arcsine(x), t * lax.rsqrt(1.0 - x * x)


def tangent_tile(cross, target_diag, support_diag):
    tangent = cross
    current = cross
    left = target_diag
    right = support_diag
    for _ in range(DEPTH):
        product = (1.0 + 2.0 * left) * (1.0 + 2.0 * right)
        slope = 4.0 / math.pi * lax.rsqrt(product - 4.0 * current * current)
        current = 2.0 / math.pi * arcsine(2.0 * current * lax.rsqrt(product)) + bias_var
        tangent = current + slope * tangent
        left = 2.0 / math.pi * arcsine(2.0 * left / (1.0 + 2.0 * left)) + bias_var
        right = 2.0 / math.pi * arcsine(2.0 * right / (1.0 + 2.0 * right)) + bias_var
    return tangent


def to_row(col, offset, lanes):
    shape = (col.shape[0], lanes)
    hit = lax.broadcasted_iota(jnp.int32, shape, 1) == lax.broadcasted_iota(jnp.int32, shape, 0) + offset
    return jnp.sum(jnp.where(hit, col, 0.0), axis=0, keepdims=True)


def to_col(row, count, offset=0):
    shape = (count, row.shape[1])
    hit = lax.broadcasted_iota(jnp.int32, shape, 1) == lax.broadcasted_iota(jnp.int32, shape, 0) + offset
    return jnp.sum(jnp.where(hit, row, 0.0), axis=1, keepdims=True)


SLAB, FWD, DIAG, CROSS, WEIGHTS, LOW, NORM = 0, 4, 8, 9, 10, 11, 12
PAIR, HALF_Y, HALF_Z, LATE_Z, LATE_Y, LAST_X, LAST_Z, LAST_A = 13, 17, 19, 21, 22, 23, 24, 25
GAT = 26
MESSAGES = 51


def step_kernel(
    scale, pixels,
    t_hbm, s_hbm, w_hbm, labels_hbm, m1_hbm, m2_hbm,
    out_hbm, n1_ref, n2_ref,
    t_v, slab, sup_v, lw, tacc, dmsg_s, dmsg_r, cacc, cmsg_s, cmsg_r, low, nmsg_s, nmsg_r,
    s1, keep, r1, s2y, s2z, r2y, r2z, s3, r3, own, s4, r4, ns, labels_ref, m1_ref, m2_ref,
    send_sem, recv_sem, local_sem, out_sem,
):
    tgt = lax.axis_index("tgt")
    x = lax.axis_index("sup")
    core = lax.rem(tgt, 2)
    yy = lax.rem(tgt // 2, 2)
    z0 = lax.rem(tgt // 4, 2)
    z1 = tgt // 8
    sib_t = tgt + 1 - 2 * core
    y_t = tgt + 2 - 4 * yy
    z0_t = tgt + 4 - 8 * z0
    z1_t = tgt + 8 - 16 * z1
    SIB, YP, ZP, ZF, XP, AN = (sib_t, x), (y_t, x), (z0_t, x), (z1_t, x), (tgt, 1 - x), (z1_t, 1 - x)

    images, width = n1_ref.shape
    rows, half = t_v.shape
    mine_rows = rows // 2
    lanes = slab.shape[0]

    def remote(src, dst, number, device):
        return pltpu.make_async_remote_copy(
            src_ref=src, dst_ref=dst, send_sem=send_sem.at[number], recv_sem=recv_sem.at[number],
            device_id=device, device_id_type=MESH,
        )

    started = []

    def send(src, dst, number, device):
        copy = remote(src, dst, number, device)
        copy.start()
        started.append(copy)

    def arrived(dst, number, device):
        remote(dst, dst, number, device).wait_recv()

    def aligned(value, by):
        return pl.multiple_of(value, by)

    my_row = aligned(x * images, images)
    peer_row = aligned((1 - x) * images, images)

    load_t = pltpu.make_async_copy(t_hbm, t_v, local_sem.at[0])
    load_s = pltpu.make_async_copy(s_hbm, sup_v, local_sem.at[1])
    load_o = pltpu.make_async_copy(
        s_hbm.at[:, pl.ds(aligned(x * half, width), half)], slab.at[pl.ds(my_row, images), :], local_sem.at[2]
    )
    load_w = pltpu.make_async_copy(w_hbm, lw.at[pl.ds(my_row, images), :], local_sem.at[3])
    load_t.start()
    load_s.start()
    load_o.start()
    load_w.start()
    load_l = pltpu.make_async_copy(labels_hbm, labels_ref, local_sem.at[4])
    load_1 = pltpu.make_async_copy(m1_hbm, m1_ref, local_sem.at[5])
    load_2 = pltpu.make_async_copy(m2_hbm, m2_ref, local_sem.at[6])
    load_l.start()
    load_1.start()
    load_2.start()

    barrier = pltpu.get_barrier_semaphore()
    for device in (SIB, YP, ZP, ZF, XP, AN):
        pl.semaphore_signal(barrier, inc=1, device_id=device, device_id_type=MESH)
    pl.semaphore_wait(barrier, 6)

    def piece(which, index):
        return aligned((which * 4 + index) * width, width)

    seat = 2 * yy + z0
    turn = (seat, 3 - seat, seat + 2 - 4 * yy, seat + 1 - 2 * z0)
    source = (XP, XP, YP, ZP)
    for p in range(2):
        send(
            s_hbm.at[:, pl.ds(aligned((1 - x) * half + (core * 4 + turn[p]) * width, width), width)],
            slab.at[pl.ds(my_row, images), pl.ds(aligned((core * 4 + turn[p]) * width, width), width)],
            SLAB + p, XP,
        )
    send(w_hbm, lw.at[pl.ds(my_row, images), :], WEIGHTS, XP)

    load_s.wait()

    def support_squares(i, acc):
        block = sup_v[:, pl.ds(aligned(i * width, width), width)].astype(f32)
        block = block * block
        for k in range(width // 128):
            acc = acc + block[:, k * 128 : (k + 1) * 128]
        return acc

    sacc = lax.fori_loop(0, pixels // width, support_squares, jnp.zeros((images, 128), f32))
    s_row = to_row(jnp.sum(sacc, axis=1, keepdims=True), x * images, lanes)
    load_t.wait()
    tacc[...] = jnp.zeros_like(tacc)

    def target_squares(i, carry):
        block = t_v[:, pl.ds(aligned(i * width, width), width)].astype(f32)
        block = block * block
        acc = tacc[...]
        for k in range(width // 128):
            acc = acc + block[:, k * 128 : (k + 1) * 128]
        tacc[...] = acc
        return carry

    lax.fori_loop(0, half // width, target_squares, 0)
    peer_first = aligned((1 - x) * mine_rows, mine_rows)
    my_first = aligned(x * mine_rows, mine_rows)
    peer_sq = jnp.sum(tacc[pl.ds(peer_first, mine_rows), :], axis=1, keepdims=True)
    my_sq = jnp.sum(tacc[pl.ds(my_first, mine_rows), :], axis=1, keepdims=True)
    load_l.wait()
    label_col = to_col(labels_ref[...].astype(f32), mine_rows, x * mine_rows)
    dmsg_s[0:8, :] = jnp.broadcast_to(to_row(peer_sq, 0, lanes), (8, lanes))
    dmsg_s[8:16, :] = jnp.broadcast_to(s_row, (8, lanes))
    send(dmsg_s, dmsg_r, DIAG, XP)

    load_o.wait()
    cacc[...] = jnp.zeros_like(cacc)

    def cross_piece(column):
        cacc[...] += lax.dot_general(
            t_v[:, pl.ds(column, width)], slab[:, pl.ds(column, width)], (((1,), (1,)), ((), ())),
            preferred_element_type=f32,
        )

    for p in range(4):
        here = slab.at[pl.ds(peer_row, images), pl.ds(piece(core, turn[p]), width)]
        arrived(here, SLAB + p, source[p])
        if p == 0:
            send(here, here, SLAB + 2, YP)
            send(here, here, SLAB + 3, ZP)
        send(here, here, FWD + p, SIB)
        cross_piece(piece(core, turn[p]))
        if p > 0:
            there = piece(1 - core, turn[p - 1])
            arrived(slab.at[pl.ds(peer_row, images), pl.ds(there, width)], FWD + p - 1, SIB)
            cross_piece(there)
    there = piece(1 - core, turn[3])
    arrived(slab.at[pl.ds(peer_row, images), pl.ds(there, width)], FWD + 3, SIB)
    cross_piece(there)

    cmsg_s[...] = cacc[pl.ds(peer_first, mine_rows), :].astype(bf16)
    send(cmsg_s, cmsg_r, CROSS, XP)

    arrived(dmsg_r, DIAG, XP)
    target_diag = (my_sq + to_col(dmsg_r[0:1, :], mine_rows)) / pixels + bias_var
    support_diag = (s_row + dmsg_r[8:9, :]) / pixels + bias_var
    arrived(cmsg_r, CROSS, XP)
    cross = (cacc[pl.ds(my_first, mine_rows), :] + cmsg_r[...].astype(f32)) / pixels + bias_var

    def kernel_of(cross_in, diag_in):
        return tangent_tile(cross_in, target_diag, diag_in)

    kernel, pullback = jax.vjp(kernel_of, cross, support_diag)
    load_w.wait()
    arrived(lw.at[pl.ds(peer_row, images), :], WEIGHTS, XP)
    weights = lw[...]
    predicted = jnp.dot(kernel.astype(bf16), weights, preferred_element_type=f32)
    classes = lax.broadcasted_iota(jnp.int32, predicted.shape, 1)
    onehot = (label_col == classes.astype(f32)).astype(f32)
    residual = (predicted - onehot).astype(bf16)
    kernel_grad = scale * lax.dot_general(
        residual, weights, (((1,), (1,)), ((), ())), preferred_element_type=f32
    )
    cross_grad, norm_grad = pullback(kernel_grad)
    mine_low = low.at[pl.ds(my_first, mine_rows), :]
    mine_low[...] = cross_grad.astype(bf16)
    nmsg_s[...] = jnp.broadcast_to(norm_grad, nmsg_s.shape)
    send(mine_low, mine_low, LOW, XP)
    send(nmsg_s, nmsg_r, NORM, XP)
    arrived(low.at[pl.ds(peer_first, mine_rows), :], LOW, XP)
    arrived(nmsg_r, NORM, XP)
    norm_col = to_col(2.0 * (norm_grad + nmsg_r[0:1, :]), lanes)
    grads = low[...]

    order = ((1, 1), (0, 1), (1, 0), (0, 0))
    chunk = 256 if width % 256 == 0 else 128

    def slab_grad(index, other, store):
        dz, dy = order[index]
        number = (z0 + dz - 2 * dz * z0) * 4 + (yy + dy - 2 * dy * yy) * 2 + (1 - core if other else core)

        def body(i, carry):
            columns = pl.ds(aligned(number * width + i * chunk, chunk), chunk)
            value = lax.dot_general(
                grads, t_v[:, columns], (((0,), (0,)), ((), ())), preferred_element_type=f32
            )
            value = value + norm_col * slab[:, columns].astype(f32)
            store(pl.ds(aligned(i * chunk, chunk), chunk), value)
            return carry

        lax.fori_loop(0, width // chunk, body, 0)

    first = slice(0, images)
    second = slice(images, 2 * images)

    def pair_sum(k, part):
        return keep[k, part, :] + r1[k, part, :].astype(f32)

    def give(k):
        def store(columns, value):
            s1[k, :, columns] = value.astype(bf16)

        slab_grad(k, True, store)
        send(s1.at[k], r1.at[k], PAIR + k, SIB)

    def hold(k):
        def store(columns, value):
            keep[k, :, columns] = value

        slab_grad(k, False, store)

    give(0)
    give(1)
    hold(0)
    arrived(r1.at[0], PAIR, SIB)
    s2y[0] = pair_sum(0, first).astype(bf16)
    send(s2y.at[0], r2y.at[0], HALF_Y, YP)
    s2z[0] = pair_sum(0, second).astype(bf16)
    send(s2z.at[0], r2z.at[0], HALF_Z, ZP)
    give(2)
    hold(1)
    arrived(r1.at[1], PAIR + 1, SIB)
    s2y[1] = pair_sum(1, first).astype(bf16)
    send(s2y.at[1], r2y.at[1], HALF_Y + 1, YP)
    hold(2)
    arrived(r1.at[2], PAIR + 2, SIB)
    s2z[1] = pair_sum(2, second).astype(bf16)
    send(s2z.at[1], r2z.at[1], HALF_Z + 1, ZP)
    give(3)
    hold(3)

    arrived(r2y.at[0], HALF_Y, YP)
    s3[0] = (pair_sum(2, first) + r2y[0].astype(f32)).astype(bf16)
    send(s3.at[0], r3.at[0], LATE_Z, ZP)
    arrived(r2z.at[0], HALF_Z, ZP)
    s3[1] = (pair_sum(1, second) + r2z[0].astype(f32)).astype(bf16)
    send(s3.at[1], r3.at[1], LATE_Y, YP)
    arrived(r1.at[3], PAIR + 3, SIB)
    arrived(r2y.at[1], HALF_Y + 1, YP)
    own[0] = pair_sum(3, first) + r2y[1].astype(f32)
    arrived(r2z.at[1], HALF_Z + 1, ZP)
    own[1] = pair_sum(3, second) + r2z[1].astype(f32)
    arrived(r3.at[0], LATE_Z, ZP)
    own[0] = own[0] + r3[0].astype(f32)
    s4[0] = own[0].astype(bf16)
    arrived(r3.at[1], LATE_Y, YP)
    own[1] = own[1] + r3[1].astype(f32)
    s4[1] = own[1].astype(bf16)

    home = z1 == x
    last_x = remote(s4.at[1 - x], r4.at[0], LAST_X, XP)
    last_z = remote(s4.at[x], r4.at[1], LAST_Z, ZF)
    last_a = remote(s4.at[1 - x], r4.at[1], LAST_A, AN)

    @pl.when(home)
    def _():
        last_x.start()
        last_z.wait_recv()
        keep[0, first, :] = own[x] + r4[1].astype(f32)
        last_x.wait_send()

    @pl.when(jnp.logical_not(home))
    def _():
        last_a.start()
        last_z.start()
        last_x.wait_recv()
        last_a.wait_recv()
        keep[0, first, :] = r4[0].astype(f32) + r4[1].astype(f32)
        last_a.wait_send()
        last_z.wait_send()

    def block(ref, index, part=slice(None)):
        return ref.at[part, pl.ds(aligned(index * width, width), width)]

    load_1.wait()
    load_2.wait()
    gradient = keep[0, first, :] / pixels
    new_first = first_decay * m1_ref[...] + (1.0 - first_decay) * gradient
    new_second = second_decay * m2_ref[...] + (1.0 - second_decay) * gradient * gradient
    update = learning_rate * (new_first / first_fix) / (jnp.sqrt(new_second / second_fix) + adam_eps)
    mine = pl.ds(aligned(tgt * width, width), width)
    ns[:, mine] = (sup_v[:, mine].astype(f32) - update).astype(bf16)
    n1_ref[...] = new_first
    n2_ref[...] = new_second

    low_half, high_half = slice(0, images // 2), slice(images // 2, images)
    z1y_t = y_t + z1_t - tgt
    z1z0_t = z0_t + z1_t - tgt
    d_t = y_t + z0_t - tgt
    z1d_t = d_t + z1_t - tgt
    swap = sib_t - tgt

    def pass_on(index, number, device, part=slice(None)):
        send(block(ns, index, part), block(ns, index, part), number, device)

    def came(index, number, device, part=slice(None)):
        arrived(block(ns, index, part), number, device)

    halves = (low_half, high_half)
    pass_on(tgt, GAT, ZF, low_half)
    pass_on(tgt, GAT + 1, ZF, high_half)
    pass_on(tgt, GAT + 2, YP)
    pass_on(tgt, GAT + 3, ZP)
    pass_on(tgt, GAT + 4, SIB)
    came(y_t, GAT + 2, YP)
    pass_on(y_t, GAT + 5, ZP, high_half)
    pass_on(y_t, GAT + 6, SIB)
    came(z0_t, GAT + 3, ZP)
    pass_on(z0_t, GAT + 7, YP, low_half)
    pass_on(z0_t, GAT + 8, SIB)
    for h in (0, 1):
        came(z1_t, GAT + h, ZF, halves[h])
        pass_on(z1_t, GAT + 9 + h, YP, halves[h])
        pass_on(z1_t, GAT + 11 + h, ZP, halves[h])
        pass_on(z1_t, GAT + 13 + h, SIB, halves[h])
    came(d_t, GAT + 5, ZP, high_half)
    pass_on(d_t, GAT + 15, SIB, high_half)
    came(d_t, GAT + 7, YP, low_half)
    pass_on(d_t, GAT + 16, SIB, low_half)
    for h in (0, 1):
        came(z1z0_t, GAT + 11 + h, ZP, halves[h])
        if h == 0:
            pass_on(z1z0_t, GAT + 17, YP, low_half)
        pass_on(z1z0_t, GAT + 18 + h, SIB, halves[h])
        came(z1y_t, GAT + 9 + h, YP, halves[h])
        if h == 1:
            pass_on(z1y_t, GAT + 20, ZP, high_half)
        pass_on(z1y_t, GAT + 21 + h, SIB, halves[h])
    came(z1d_t, GAT + 17, YP, low_half)
    pass_on(z1d_t, GAT + 23, SIB, low_half)
    came(z1d_t, GAT + 20, ZP, high_half)
    pass_on(z1d_t, GAT + 24, SIB, high_half)

    came(tgt + swap, GAT + 4, SIB)
    came(y_t + swap, GAT + 6, SIB)
    came(z0_t + swap, GAT + 8, SIB)
    came(d_t + swap, GAT + 15, SIB, high_half)
    came(d_t + swap, GAT + 16, SIB, low_half)
    for h in (0, 1):
        came(z1_t + swap, GAT + 13 + h, SIB, halves[h])
        came(z1z0_t + swap, GAT + 18 + h, SIB, halves[h])
        came(z1y_t + swap, GAT + 21 + h, SIB, halves[h])
    came(z1d_t + swap, GAT + 23, SIB, low_half)
    came(z1d_t + swap, GAT + 24, SIB, high_half)
    store = pltpu.make_async_copy(ns, out_hbm, out_sem)
    store.start()
    for copy in started:
        copy.wait_send()
    store.wait()


def fused(targets, support, label_weights, labels, first_moment, second_moment):
    rows, half = targets.shape
    images, pixels = support.shape
    width = first_moment.shape[1]
    classes = label_weights.shape[1]
    target_count = rows * lax.axis_size("tgt")
    support_count = images * lax.axis_size("sup")
    scale = 4.0 * pixels * math.sqrt(classes * support_count / target_count)
    everyone, part = 2 * images, rows // 2
    hbm = pl.BlockSpec(memory_space=pltpu.HBM)
    vmem = pl.BlockSpec(memory_space=pltpu.VMEM)
    return pl.pallas_call(
        functools.partial(step_kernel, scale, pixels),
        out_shape=(
            pltpu.VMEM(support.shape, bf16),
            pltpu.VMEM(first_moment.shape, f32),
            pltpu.VMEM(first_moment.shape, f32),
        ),
        in_specs=[hbm] * 6,
        out_specs=(vmem, vmem, vmem),
        scratch_shapes=[
            pltpu.VMEM((rows, half), bf16),
            pltpu.VMEM((everyone, half), bf16),
            pltpu.VMEM((images, pixels), bf16),
            pltpu.VMEM((everyone, classes), bf16),
            pltpu.VMEM((rows, 128), f32),
            pltpu.VMEM((16, everyone), f32),
            pltpu.VMEM((16, everyone), f32),
            pltpu.VMEM((rows, everyone), f32),
            pltpu.VMEM((part, everyone), bf16),
            pltpu.VMEM((part, everyone), bf16),
            pltpu.VMEM((rows, everyone), bf16),
            pltpu.VMEM((8, everyone), f32),
            pltpu.VMEM((8, everyone), f32),
            pltpu.VMEM((4, everyone, width), bf16),
            pltpu.VMEM((4, everyone, width), f32),
            pltpu.VMEM((4, everyone, width), bf16),
            pltpu.VMEM((2, images, width), bf16),
            pltpu.VMEM((2, images, width), bf16),
            pltpu.VMEM((2, images, width), bf16),
            pltpu.VMEM((2, images, width), bf16),
            pltpu.VMEM((2, images, width), bf16),
            pltpu.VMEM((2, images, width), bf16),
            pltpu.VMEM((2, images, width), f32),
            pltpu.VMEM((2, images, width), bf16),
            pltpu.VMEM((2, images, width), bf16),
            pltpu.VMEM((images, pixels), bf16),
            pltpu.VMEM((1, rows), jnp.int32),
            pltpu.VMEM((images, width), f32),
            pltpu.VMEM((images, width), f32),
            pltpu.SemaphoreType.DMA((MESSAGES,)),
            pltpu.SemaphoreType.DMA((MESSAGES,)),
            pltpu.SemaphoreType.DMA((7,)),
            pltpu.SemaphoreType.DMA,
        ],
        compiler_params=pltpu.CompilerParams(
            collective_id=0, has_side_effects=True, vmem_limit_bytes=60000000
        ),
    )(targets, support, label_weights, labels[None, :], first_moment, second_moment)


def hand_over(a_ref, b_ref, c_ref, x_ref, y_ref, z_ref, sem):
    copies = [
        pltpu.make_async_copy(src, dst, sem.at[i])
        for i, (src, dst) in enumerate(((a_ref, x_ref), (b_ref, y_ref), (c_ref, z_ref)))
    ]
    for copy in copies:
        copy.start()
    for copy in copies:
        copy.wait()


def settle(support, first, second, space):
    return pl.pallas_call(
        hand_over,
        out_shape=tuple(jax.ShapeDtypeStruct(a.shape, a.dtype) for a in (support, first, second)),
        in_specs=[pl.BlockSpec(memory_space=space)] * 3,
        out_specs=(pl.BlockSpec(memory_space=pltpu.HBM),) * 3,
        scratch_shapes=[pltpu.SemaphoreType.DMA((3,))],
    )(support, first, second)


def pick(mesh):
    groups, shares = mesh.shape["sup"], mesh.shape["tgt"]

    def run(targets, support, label_weights, labels, first_moment, second_moment):
        width = first_moment.shape[1]
        fits = groups == 2 and shares == 16 and width % 128 == 0
        fits = fits and targets.shape[0] % 32 == 0 and groups * support.shape[0] == 128
        body = fused if fits else shards
        out = body(targets, support, label_weights, labels, first_moment, second_moment)
        return settle(*[pltpu.with_memory_space_constraint(o, pltpu.VMEM) for o in out], pltpu.VMEM) if fits else out

    return run


def solution(mesh):
    return jax.shard_map(
        pick(mesh),
        mesh=mesh,
        in_specs=(
            P("tgt", "sup"),
            P("sup", None),
            P("sup", None),
            P("tgt"),
            P("sup", "tgt"),
            P("sup", "tgt"),
        ),
        out_specs=(P("sup", None), P("sup", "tgt"), P("sup", "tgt")),
        check_vma=False,
    )
```

```python
import functools
import math

import jax
import jax.numpy as jnp
from jax import lax
from jax.experimental import pallas as pl
from jax.experimental.pallas import tpu as pltpu
from jax.sharding import PartitionSpec as P

DEPTH = 3


bias_var = 0.1
learning_rate = 0.05
first_decay = 0.9
second_decay = 0.99
first_fix = 1.0 - 0.9**10
second_fix = 1.0 - 0.99**10
adam_eps = 1e-08


def tangent_kernel(cross, target_diag, support_diag):
    tangent = cross
    current = cross
    left_diag = target_diag
    right_diag = support_diag
    for _ in range(DEPTH):
        product = (1.0 + 2.0 * left_diag)[:, None] * (1.0 + 2.0 * right_diag)[None, :]
        slope = 4.0 / math.pi / jnp.sqrt(product - 4.0 * current * current)
        current = 2.0 / math.pi * jnp.arcsin(2.0 * current / jnp.sqrt(product)) + bias_var
        tangent = current + slope * tangent
        left_diag = 2.0 / math.pi * jnp.arcsin(2.0 * left_diag / (1.0 + 2.0 * left_diag)) + bias_var
        right_diag = (
            2.0 / math.pi * jnp.arcsin(2.0 * right_diag / (1.0 + 2.0 * right_diag)) + bias_var
        )
    return tangent


def row_squares(images):
    return jnp.sum(jnp.square(images.astype(jnp.float32)), axis=1)


def shards(targets, support, label_weights, labels, first_moment, second_moment):
    pixels = support.shape[1]
    target_count = targets.shape[0] * lax.axis_size("tgt")
    support_count = support.shape[0] * lax.axis_size("sup")
    class_count = label_weights.shape[1]
    support_diag = row_squares(support) / pixels + bias_var
    slabs = lax.all_to_all(support, "sup", split_axis=1, concat_axis=0, tiled=True)
    partial_cross = lax.dot_general(
        targets, slabs, (((1,), (1,)), ((), ())), preferred_element_type=jnp.float32
    )
    cross = (
        lax.psum_scatter(
            partial_cross.astype(jnp.bfloat16), "sup", scatter_dimension=1, tiled=True
        ).astype(jnp.float32)
        / pixels
        + bias_var
    )
    target_diag = lax.psum(row_squares(targets), "sup") / pixels + bias_var

    def kernel_of(cross_in, diag_in):
        return tangent_kernel(cross_in, target_diag, diag_in)

    kernel, pullback = jax.vjp(kernel_of, cross, support_diag)
    partial_pred = jnp.dot(
        kernel.astype(jnp.bfloat16), label_weights, preferred_element_type=jnp.float32
    )
    predicted = lax.psum(partial_pred.astype(jnp.bfloat16), "sup").astype(jnp.float32)
    classes = jnp.arange(class_count, dtype=jnp.int32)
    onehot = (labels[:, None] == classes[None, :]).astype(jnp.float32)
    residual = (predicted - onehot).astype(jnp.bfloat16)
    kernel_grad = lax.dot_general(
        residual, label_weights, (((1,), (1,)), ((), ())), preferred_element_type=jnp.float32
    )
    kernel_grad = kernel_grad * (
        4.0 * pixels * math.sqrt(class_count * support_count / target_count)
    )
    cross_grad, norm_grad = pullback(kernel_grad)
    cross_low = cross_grad.astype(jnp.bfloat16)
    all_grads = lax.all_gather(cross_low, "sup", axis=1, tiled=True)
    slab_grad = lax.dot_general(
        all_grads, targets, (((0,), (0,)), ((), ())), preferred_element_type=jnp.float32
    )
    image_grad = lax.all_to_all(
        slab_grad.astype(jnp.bfloat16), "sup", split_axis=0, concat_axis=1, tiled=True
    ).astype(slab_grad.dtype)
    gradient = (image_grad + 2.0 * norm_grad[:, None] * support.astype(jnp.float32)) / pixels
    shares = lax.psum_scatter(gradient, "tgt", scatter_dimension=1, tiled=True)
    slab_width = shares.shape[1]
    own_pixels = lax.dynamic_slice_in_dim(
        support, lax.axis_index("tgt") * slab_width, slab_width, 1
    ).astype(jnp.float32)
    new_first = first_decay * first_moment + (1.0 - first_decay) * shares
    new_second = second_decay * second_moment + (1.0 - second_decay) * shares * shares
    update = (
        learning_rate * (new_first / first_fix) / (jnp.sqrt(new_second / second_fix) + adam_eps)
    )
    new_slab = (own_pixels - update).astype(jnp.bfloat16)
    new_support = lax.all_gather(new_slab, "tgt", axis=1, tiled=True)
    return (new_support, new_first, new_second)


MESH = pl.DeviceIdType.MESH
f32 = jnp.float32
bf16 = jnp.bfloat16


@jax.custom_jvp
def arcsine(x):
    a = jnp.abs(x)
    big = a > 0.5
    z = jnp.where(big, 0.5 * (1.0 - a), a * a)
    s = jnp.where(big, jnp.sqrt(z), a)
    p = 4.2163199048e-2 * z + 2.4181311049e-2
    p = p * z + 4.5470025998e-2
    p = p * z + 7.4953002686e-2
    p = p * z + 1.6666752422e-1
    p = p * z * s + s
    r = jnp.where(big, math.pi / 2.0 - 2.0 * p, p)
    return jnp.where(x < 0.0, -r, r)


@arcsine.defjvp
def arcsine_jvp(primals, tangents):
    (x,) = primals
    (t,) = tangents
    return arcsine(x), t * lax.rsqrt(1.0 - x * x)


def tangent_tile(cross, target_diag, support_diag):
    tangent = cross
    current = cross
    left = target_diag
    right = support_diag
    for _ in range(DEPTH):
        product = (1.0 + 2.0 * left) * (1.0 + 2.0 * right)
        slope = 4.0 / math.pi * lax.rsqrt(product - 4.0 * current * current)
        current = 2.0 / math.pi * arcsine(2.0 * current * lax.rsqrt(product)) + bias_var
        tangent = current + slope * tangent
        left = 2.0 / math.pi * arcsine(2.0 * left / (1.0 + 2.0 * left)) + bias_var
        right = 2.0 / math.pi * arcsine(2.0 * right / (1.0 + 2.0 * right)) + bias_var
    return tangent


def to_row(col, offset, lanes):
    shape = (col.shape[0], lanes)
    hit = lax.broadcasted_iota(jnp.int32, shape, 1) == lax.broadcasted_iota(jnp.int32, shape, 0) + offset
    return jnp.sum(jnp.where(hit, col, 0.0), axis=0, keepdims=True)


def to_col(row, count, offset=0):
    shape = (count, row.shape[1])
    hit = lax.broadcasted_iota(jnp.int32, shape, 1) == lax.broadcasted_iota(jnp.int32, shape, 0) + offset
    return jnp.sum(jnp.where(hit, row, 0.0), axis=1, keepdims=True)


MESSAGES = 128


def support_chain(diag):
    factors, rates = [], []
    right = diag
    for _ in range(DEPTH):
        plus = 1.0 + 2.0 * right
        factors.append(plus)
        rates.append(4.0 / math.pi / (plus * jnp.sqrt(1.0 + 4.0 * right)))
        right = 2.0 / math.pi * arcsine(2.0 * right / plus) + bias_var
    return factors, rates


def target_chain(diag):
    roots = []
    left = diag
    for _ in range(DEPTH):
        plus = 1.0 + 2.0 * left
        roots.append(lax.rsqrt(plus))
        left = 2.0 / math.pi * arcsine(2.0 * left / plus) + bias_var
    return roots


def forward(cross, roots, factors):
    tangent, current = cross, cross
    saved = []
    for root, plus in zip(roots, factors):
        twice = root * (2.0 * lax.rsqrt(plus))
        sine = current * twice
        inverse = lax.rsqrt(1.0 - sine * sine)
        slope = 2.0 / math.pi * twice * inverse
        saved.append((twice, sine, inverse, slope, tangent))
        current = 2.0 / math.pi * arcsine(sine) + bias_var
        tangent = current + slope * tangent
    return tangent, saved


def backward(grad, saved, factors, rates):
    tangent_bar, current_bar = grad, jnp.zeros_like(grad)
    diag_bar = None
    for layer in reversed(range(DEPTH)):
        twice, sine, inverse, slope, tangent = saved[layer]
        total = current_bar + tangent_bar
        next_bar = tangent_bar * slope
        carried = next_bar * tangent * inverse * inverse
        direct = -jnp.sum(carried + 2.0 / math.pi * total * inverse * sine, axis=0, keepdims=True) / factors[layer]
        diag_bar = direct if diag_bar is None else direct + diag_bar * rates[layer]
        current_bar = total * slope + twice * sine * carried
        tangent_bar = next_bar
    return current_bar + tangent_bar, diag_bar


def step_kernel(
    scale, pixels,
    t_hbm, s_hbm, w_hbm, labels_hbm, m1_hbm, m2_hbm,
    out_ref, n1_ref, n2_ref,
    t_v, slab, sup_v, lw, tacc, dmsg_s, dmsg_r, cacc, cmsg_s, cmsg_r, low, nmsg_s, nmsg_r,
    sy, sz, ry, rz, keep, s3, r3, s4, r4, own, labels_ref, m1_ref, m2_ref,
    send_sem, recv_sem, local_sem,
):
    tgt = lax.axis_index("tgt")
    x = lax.axis_index("sup")
    core = lax.rem(tgt, 2)
    yy = lax.rem(tgt // 2, 2)
    z0 = lax.rem(tgt // 4, 2)
    z1 = tgt // 8
    sib_t = tgt + 1 - 2 * core
    y_t = tgt + 2 - 4 * yy
    z0_t = tgt + 4 - 8 * z0
    z1_t = tgt + 8 - 16 * z1
    SIB, YP, ZP, ZF = (sib_t, x), (y_t, x), (z0_t, x), (z1_t, x)
    XP, XS, AN = (tgt, 1 - x), (sib_t, 1 - x), (z1_t, 1 - x)

    images, width = n1_ref.shape
    rows = t_v.shape[0] // 2
    half = 8 * width
    part = rows // 2
    lanes = slab.shape[0]
    piece = width // 2

    numbers = {}

    def remote(src, dst, name, device):
        number = numbers.setdefault(name, len(numbers))
        return pltpu.make_async_remote_copy(
            src_ref=src, dst_ref=dst, send_sem=send_sem.at[number], recv_sem=recv_sem.at[number],
            device_id=device, device_id_type=MESH,
        )

    started = []

    def send(src, dst, name, device):
        copy = remote(src, dst, name, device)
        copy.start()
        started.append(copy)

    def arrived(dst, name, device):
        remote(dst, dst, name, device).wait_recv()

    def aligned(value, by):
        return pl.multiple_of(value, by)

    locals_ = []

    def load(src, dst):
        copy = pltpu.make_async_copy(src, dst, local_sem.at[len(locals_)])
        copy.start()
        locals_.append(copy)
        return copy

    my_row = aligned(x * images, images)
    peer_row = aligned((1 - x) * images, images)

    def columns(block, owner):
        return pl.ds(aligned((2 * block + owner) * width, width), width)

    def far_columns(slab_index, block):
        return pl.ds(aligned(slab_index * half + (2 * block + core) * width, width), width)

    def block_of(j):
        return pl.ds(aligned(j * width, width), width)

    load_s = load(s_hbm, sup_v)
    mine_t = pl.ds(aligned(core * rows, rows), rows)
    load_t = [load(t_hbm.at[:, columns(j, core)], t_v.at[mine_t, block_of(j)]) for j in range(4)]
    load_o = [load(s_hbm.at[:, far_columns(x, j)], slab.at[pl.ds(my_row, images), block_of(j)]) for j in range(4)]
    load_w = load(w_hbm, lw.at[pl.ds(my_row, images), :])
    load_l = load(labels_hbm, labels_ref)
    load_1 = load(m1_hbm, m1_ref)
    load_2 = load(m2_hbm, m2_ref)

    barrier = pltpu.get_barrier_semaphore()
    for device in (SIB, YP, ZP, ZF, XP, XS, AN):
        pl.semaphore_signal(barrier, inc=1, device_id=device, device_id_type=MESH)
    pl.semaphore_wait(barrier, 7)

    seat = 2 * yy + z0
    turn = (seat, 3 - seat, seat + 2 - 4 * yy, seat + 1 - 2 * z0)
    source = (XP, XP, YP, ZP)
    strip = images // 2

    def send_strip(p, r):
        send(
            s_hbm.at[pl.ds(r * strip, strip), far_columns(1 - x, turn[p])],
            slab.at[pl.ds(aligned(my_row + r * strip, strip), strip), block_of(turn[p])],
            ("slab", p, r), XP,
        )

    send_strip(0, 0)
    send_strip(0, 1)
    send_strip(1, 0)
    send_strip(1, 1)
    for j in range(4):
        send(t_hbm.at[:, columns(j, 1 - core)], t_v.at[mine_t, block_of(j)], ("targets", j), SIB)
    weight_rows = pl.ds(aligned(my_row + core * strip, strip), strip)
    send(w_hbm.at[pl.ds(aligned(core * strip, strip), strip), :], lw.at[weight_rows, :], "weights", XP)

    load_s.wait()

    def support_squares(i, acc):
        block = sup_v[:, pl.ds(aligned(i * width, width), width)].astype(f32)
        block = block * block
        for k in range(width // 128):
            acc = acc + block[:, k * 128 : (k + 1) * 128]
        return acc

    sacc = lax.fori_loop(0, pixels // width, support_squares, jnp.zeros((images, 128), f32))
    s_row = to_row(jnp.sum(sacc, axis=1, keepdims=True), x * images, lanes)

    def target_squares(first):
        def body(i, carry):
            where = pl.ds(aligned(first + i * 16, 16), 16)
            sums = []
            for j in range(4):
                block = t_v[where, j * width : (j + 1) * width].astype(f32)
                block = block * block
                acc = block[:, 0:128]
                for k in range(1, width // 128):
                    acc = acc + block[:, k * 128 : (k + 1) * 128]
                sums.append(acc)
            tacc[where, :] = (sums[0] + sums[1]) + (sums[2] + sums[3])
            return carry

        lax.fori_loop(0, rows // 16, body, 0)

    for copy in load_t:
        copy.wait()
    target_squares(core * rows)
    other_t = pl.ds(aligned((1 - core) * rows, rows), rows)
    for j in range(4):
        arrived(t_v.at[other_t, block_of(j)], ("targets", j), SIB)
    target_squares((1 - core) * rows)

    group = (SIB, XP, XS)
    quarter = 2 * core + x
    theirs = (2 * (1 - core) + x, 2 * core + 1 - x, 2 * (1 - core) + 1 - x)

    def rows_of(q):
        return pl.ds(aligned(q * part, part), part)

    def square_col(q):
        return jnp.sum(tacc[rows_of(q), :], axis=1, keepdims=True)

    for i in range(3):
        dmsg_s[i, 0:8, :] = jnp.broadcast_to(to_row(square_col(theirs[i]), 0, lanes), (8, lanes))
        dmsg_s[i, 8:16, :] = jnp.broadcast_to(s_row, (8, lanes))
        send(dmsg_s.at[i], dmsg_r.at[i], ("diag", i), group[i])
    my_sq = square_col(quarter)
    load_l.wait()
    label_col = to_col(labels_ref[...].astype(f32), part, x * part)

    for copy in load_o:
        copy.wait()

    def cross_piece(p, first=False):
        value = lax.dot_general(
            t_v[:, block_of(turn[p])], slab[:, block_of(turn[p])], (((1,), (1,)), ((), ())),
            preferred_element_type=f32,
        )
        cacc[...] = value if first else cacc[...] + value

    def strip_of(p, r):
        return slab.at[pl.ds(aligned(peer_row + r * strip, strip), strip), block_of(turn[p])]

    for r in (0, 1):
        here = strip_of(0, r)
        arrived(here, ("slab", 0, r), XP)
        send(here, here, ("slab", 2, r), YP)
        send(here, here, ("slab", 3, r), ZP)
    cross_piece(0, True)
    for p in range(1, 4):
        for r in (0, 1):
            arrived(strip_of(p, r), ("slab", p, r), source[p])
        if p == 1:
            half_rows = lw.at[pl.ds(aligned(peer_row + core * strip, strip), strip), :]
            arrived(half_rows, "weights", XP)
            send(half_rows, half_rows, "weights on", SIB)
        cross_piece(p)

    for i in (2, 1, 0):
        cmsg_s[i] = cacc[rows_of(theirs[i]), :].astype(bf16)
        send(cmsg_s.at[i], cmsg_r.at[i], ("cross", i), group[i])

    for i in range(3):
        arrived(dmsg_r.at[i], ("diag", i), group[i])
    square_row = dmsg_r[0, 0:1, :] + dmsg_r[1, 0:1, :] + dmsg_r[2, 0:1, :]
    roots = target_chain((my_sq + to_col(square_row, part)) / pixels + bias_var)
    factors, rates = support_chain((s_row + dmsg_r[1, 8:9, :]) / pixels + bias_var)
    load_w.wait()
    arrived(lw.at[pl.ds(aligned(peer_row + (1 - core) * strip, strip), strip), :], "weights on", SIB)

    for i in range(3):
        arrived(cmsg_r.at[i], ("cross", i), group[i])
    total = cacc[rows_of(quarter), :] + cmsg_r[0].astype(f32)
    total = total + (cmsg_r[1].astype(f32) + cmsg_r[2].astype(f32))
    kernel, saved = forward(total / pixels + bias_var, roots, factors)
    weights = lw[...]
    predicted = jnp.dot(kernel.astype(bf16), weights, preferred_element_type=f32)
    classes = lax.broadcasted_iota(jnp.int32, predicted.shape, 1)
    onehot = (label_col == classes.astype(f32)).astype(f32)
    residual = (predicted - onehot).astype(bf16)
    kernel_grad = scale * lax.dot_general(
        residual, weights, (((1,), (1,)), ((), ())), preferred_element_type=f32
    )
    cross_grad, norm_grad = backward(kernel_grad, saved, factors, rates)
    mine_low = low.at[rows_of(quarter), :]
    mine_low[...] = cross_grad.astype(bf16)
    for i in (2, 1, 0):
        send(mine_low, mine_low, ("low", i), group[i])
    nmsg_s[...] = jnp.broadcast_to(norm_grad, nmsg_s.shape)
    for i in (2, 1, 0):
        send(nmsg_s, nmsg_r.at[i], ("norm", i), group[i])
    for i in range(3):
        arrived(low.at[rows_of(theirs[i]), :], ("low", i), group[i])
    for i in range(3):
        arrived(nmsg_r.at[i], ("norm", i), group[i])
    norm_row = norm_grad + nmsg_r[0, 0:1, :] + nmsg_r[1, 0:1, :] + nmsg_r[2, 0:1, :]
    norm_col = to_col(2.0 * norm_row, lanes)
    grads = low[...].astype(f32).T.astype(bf16)

    order = ((1, 1), (0, 1), (1, 0), (0, 0))
    first = slice(0, images)
    second = slice(images, 2 * images)

    def block_grad(k, h):
        dz, dy = order[k]
        number = (z0 + dz - 2 * dz * z0) * 2 + (yy + dy - 2 * dy * yy)
        where = pl.ds(aligned(number * width + h * piece, piece), piece)
        value = jnp.dot(grads, t_v[:, where], preferred_element_type=f32)
        return value + norm_col * slab[:, where].astype(f32)

    for h in (0, 1):
        value = block_grad(0, h)
        sy[0, h] = value[first].astype(bf16)
        send(sy.at[0, h], ry.at[0, h], ("y", 0, h), YP)
        sz[0, h] = value[second].astype(bf16)
        send(sz.at[0, h], rz.at[0, h], ("z", 0, h), ZP)
    for h in (0, 1):
        value = block_grad(1, h)
        sy[1, h] = value[first].astype(bf16)
        send(sy.at[1, h], ry.at[1, h], ("y", 1, h), YP)
        keep[0, h] = value[second]
        value = block_grad(2, h)
        sz[1, h] = value[second].astype(bf16)
        send(sz.at[1, h], rz.at[1, h], ("z", 1, h), ZP)
        keep[1, h] = value[first]
    for h in (0, 1):
        value = block_grad(3, h)
        keep[2, h] = value[first]
        keep[3, h] = value[second]
    for h in (0, 1):
        arrived(ry.at[0, h], ("y", 0, h), YP)
        s3[0, h] = (keep[1, h] + ry[0, h].astype(f32)).astype(bf16)
        send(s3.at[0, h], r3.at[0, h], ("late z", h), ZP)
        arrived(rz.at[0, h], ("z", 0, h), ZP)
        s3[1, h] = (keep[0, h] + rz[0, h].astype(f32)).astype(bf16)
        send(s3.at[1, h], r3.at[1, h], ("late y", h), YP)
    for h in (0, 1):
        arrived(ry.at[1, h], ("y", 1, h), YP)
        keep[2, h] = keep[2, h] + ry[1, h].astype(f32)
        arrived(rz.at[1, h], ("z", 1, h), ZP)
        keep[3, h] = keep[3, h] + rz[1, h].astype(f32)

    home = z1 == x
    last = [
        (
            remote(s4.at[h, 1 - x], r4.at[h, 0], ("last x", h), XP),
            remote(s4.at[h, x], r4.at[h, 1], ("last z", h), ZF),
            remote(s4.at[h, 1 - x], r4.at[h, 1], ("last a", h), AN),
        )
        for h in (0, 1)
    ]
    for h in (0, 1):
        last_x, last_z, last_a = last[h]
        arrived(r3.at[0, h], ("late z", h), ZP)
        keep[2, h] = keep[2, h] + r3[0, h].astype(f32)
        arrived(r3.at[1, h], ("late y", h), YP)
        keep[3, h] = keep[3, h] + r3[1, h].astype(f32)
        s4[h, 0] = keep[2, h].astype(bf16)
        s4[h, 1] = keep[3, h].astype(bf16)

        @pl.when(home)
        def _():
            last_x.start()

        @pl.when(jnp.logical_not(home))
        def _():
            last_a.start()
            last_z.start()

    load_1.wait()
    load_2.wait()

    def cut(index, h):
        return pl.ds(aligned(index * width + h * piece, piece), piece)

    def pass_on(index, name, device, h):
        here = out_ref.at[:, cut(index, h)]
        send(here, here, (name, h), device)

    def came(index, name, device, h):
        arrived(out_ref.at[:, cut(index, h)], (name, h), device)

    for h in (0, 1):
        last_x, last_z, last_a = last[h]

        @pl.when(home)
        def _():
            last_z.wait_recv()
            own[h] = keep[2 + x, h] + r4[h, 1].astype(f32)

        @pl.when(jnp.logical_not(home))
        def _():
            last_x.wait_recv()
            last_a.wait_recv()
            own[h] = r4[h, 0].astype(f32) + r4[h, 1].astype(f32)

        here = slice(h * piece, (h + 1) * piece)
        gradient = own[h] / pixels
        new_first = first_decay * m1_ref[:, here] + (1.0 - first_decay) * gradient
        new_second = second_decay * m2_ref[:, here] + (1.0 - second_decay) * gradient * gradient
        update = learning_rate * (new_first / first_fix) / (jnp.sqrt(new_second / second_fix) + adam_eps)
        out_ref[:, cut(tgt, h)] = (sup_v[:, cut(tgt, h)].astype(f32) - update).astype(bf16)
        pass_on(tgt, "own zf", ZF, h)
        pass_on(tgt, "own y", YP, h)
        pass_on(tgt, "own z", ZP, h)
        pass_on(tgt, "own s", SIB, h)
        n1_ref[:, here] = new_first
        n2_ref[:, here] = new_second

    z1y_t = y_t + z1_t - tgt
    z1z0_t = z0_t + z1_t - tgt
    d_t = y_t + z0_t - tgt
    z1d_t = d_t + z1_t - tgt
    swap = sib_t - tgt

    for h in (0, 1):
        came(z0_t, "own z", ZP, h)
        pass_on(z0_t, "z0 y", YP, h)
        pass_on(z0_t, "z0 s", SIB, h)
        came(z1_t, "own zf", ZF, h)
        pass_on(z1_t, "z1 z", ZP, h)
        pass_on(z1_t, "z1 y", YP, h)
        pass_on(z1_t, "z1 s", SIB, h)
        came(y_t, "own y", YP, h)
        pass_on(y_t, "y s", SIB, h)
    for h in (0, 1):
        came(d_t, "z0 y", YP, h)
        pass_on(d_t, "d s", SIB, h)
        came(z1z0_t, "z1 z", ZP, h)
        if h == 0:
            pass_on(z1z0_t, "zz y", YP, h)
        pass_on(z1z0_t, "zz s", SIB, h)
        came(z1y_t, "z1 y", YP, h)
        if h == 1:
            pass_on(z1y_t, "zy z", ZP, h)
        pass_on(z1y_t, "zy s", SIB, h)
    came(z1d_t, "zz y", YP, 0)
    pass_on(z1d_t, "zd s", SIB, 0)
    came(z1d_t, "zy z", ZP, 1)
    pass_on(z1d_t, "zd s", SIB, 1)

    for h in (0, 1):
        came(tgt + swap, "own s", SIB, h)
        came(y_t + swap, "y s", SIB, h)
        came(z0_t + swap, "z0 s", SIB, h)
        came(d_t + swap, "d s", SIB, h)
        came(z1_t + swap, "z1 s", SIB, h)
        came(z1z0_t + swap, "zz s", SIB, h)
        came(z1y_t + swap, "zy s", SIB, h)
        came(z1d_t + swap, "zd s", SIB, h)

    @pl.when(home)
    def _():
        for h in (0, 1):
            last[h][0].wait_send()

    @pl.when(jnp.logical_not(home))
    def _():
        for h in (0, 1):
            last[h][1].wait_send()
            last[h][2].wait_send()

    for copy in started:
        copy.wait_send()


def fused(targets, support, label_weights, labels, first_moment, second_moment):
    rows, _ = targets.shape
    images, pixels = support.shape
    width = first_moment.shape[1]
    classes = label_weights.shape[1]
    target_count = rows * lax.axis_size("tgt")
    support_count = images * lax.axis_size("sup")
    scale = 4.0 * pixels * math.sqrt(classes * support_count / target_count)
    everyone, part, piece = 2 * images, rows // 2, width // 2
    hbm = pl.BlockSpec(memory_space=pltpu.HBM)
    vmem = pl.BlockSpec(memory_space=pltpu.VMEM)
    slots = pltpu.VMEM((2, 2, images, piece), bf16)
    return pl.pallas_call(
        functools.partial(step_kernel, scale, pixels),
        out_shape=(
            pltpu.VMEM(support.shape, bf16),
            pltpu.VMEM(first_moment.shape, f32),
            pltpu.VMEM(first_moment.shape, f32),
        ),
        in_specs=[hbm] * 6,
        out_specs=(vmem, vmem, vmem),
        scratch_shapes=[
            pltpu.VMEM((2 * rows, 4 * width), bf16),
            pltpu.VMEM((everyone, 4 * width), bf16),
            pltpu.VMEM((images, pixels), bf16),
            pltpu.VMEM((everyone, classes), bf16),
            pltpu.VMEM((2 * rows, 128), f32),
            pltpu.VMEM((3, 16, everyone), f32),
            pltpu.VMEM((3, 16, everyone), f32),
            pltpu.VMEM((2 * rows, everyone), f32),
            pltpu.VMEM((3, part, everyone), bf16),
            pltpu.VMEM((3, part, everyone), bf16),
            pltpu.VMEM((2 * rows, everyone), bf16),
            pltpu.VMEM((8, everyone), f32),
            pltpu.VMEM((3, 8, everyone), f32),
            slots,
            slots,
            slots,
            slots,
            pltpu.VMEM((4, 2, images, piece), f32),
            slots,
            slots,
            slots,
            slots,
            pltpu.VMEM((2, images, piece), f32),
            pltpu.VMEM((1, rows), jnp.int32),
            pltpu.VMEM((images, width), f32),
            pltpu.VMEM((images, width), f32),
            pltpu.SemaphoreType.DMA((MESSAGES,)),
            pltpu.SemaphoreType.DMA((MESSAGES,)),
            pltpu.SemaphoreType.DMA((16,)),
        ],
        compiler_params=pltpu.CompilerParams(
            collective_id=0, has_side_effects=True, vmem_limit_bytes=60000000
        ),
    )(targets, support, label_weights, labels[None, :], first_moment, second_moment)


def hand_over(a_ref, b_ref, c_ref, x_ref, y_ref, z_ref, sem):
    copies = [
        pltpu.make_async_copy(src, dst, sem.at[i])
        for i, (src, dst) in enumerate(((a_ref, x_ref), (b_ref, y_ref), (c_ref, z_ref)))
    ]
    for copy in copies:
        copy.start()
    for copy in copies:
        copy.wait()


def settle(support, first, second, space):
    return pl.pallas_call(
        hand_over,
        out_shape=tuple(jax.ShapeDtypeStruct(a.shape, a.dtype) for a in (support, first, second)),
        in_specs=[pl.BlockSpec(memory_space=space)] * 3,
        out_specs=(pl.BlockSpec(memory_space=pltpu.HBM),) * 3,
        scratch_shapes=[pltpu.SemaphoreType.DMA((3,))],
    )(support, first, second)


def pick(mesh):
    groups, shares = mesh.shape["sup"], mesh.shape["tgt"]

    def run(targets, support, label_weights, labels, first_moment, second_moment):
        width = first_moment.shape[1]
        fits = groups == 2 and shares == 16 and width % 256 == 0
        fits = fits and targets.shape[0] % 32 == 0 and groups * support.shape[0] == 128
        body = fused if fits else shards
        out = body(targets, support, label_weights, labels, first_moment, second_moment)
        return settle(*[pltpu.with_memory_space_constraint(o, pltpu.VMEM) for o in out], pltpu.VMEM) if fits else out

    return run


def solution(mesh):
    return jax.shard_map(
        pick(mesh),
        mesh=mesh,
        in_specs=(
            P("tgt", "sup"),
            P("sup", None),
            P("sup", None),
            P("tgt"),
            P("sup", "tgt"),
            P("sup", "tgt"),
        ),
        out_specs=(P("sup", None), P("sup", "tgt"), P("sup", "tgt")),
        check_vma=False,
    )
```

```python
import functools
import math

import jax
import jax.numpy as jnp
from jax import lax
from jax.experimental import pallas as pl
from jax.experimental.pallas import tpu as pltpu
from jax.sharding import PartitionSpec as P

DEPTH = 3


bias_var = 0.1
learning_rate = 0.05
first_decay = 0.9
second_decay = 0.99
first_fix = 1.0 - 0.9**10
second_fix = 1.0 - 0.99**10
adam_eps = 1e-08


def tangent_kernel(cross, target_diag, support_diag):
    tangent = cross
    current = cross
    left_diag = target_diag
    right_diag = support_diag
    for _ in range(DEPTH):
        product = (1.0 + 2.0 * left_diag)[:, None] * (1.0 + 2.0 * right_diag)[None, :]
        slope = 4.0 / math.pi / jnp.sqrt(product - 4.0 * current * current)
        current = 2.0 / math.pi * jnp.arcsin(2.0 * current / jnp.sqrt(product)) + bias_var
        tangent = current + slope * tangent
        left_diag = 2.0 / math.pi * jnp.arcsin(2.0 * left_diag / (1.0 + 2.0 * left_diag)) + bias_var
        right_diag = (
            2.0 / math.pi * jnp.arcsin(2.0 * right_diag / (1.0 + 2.0 * right_diag)) + bias_var
        )
    return tangent


def row_squares(images):
    return jnp.sum(jnp.square(images.astype(jnp.float32)), axis=1)


def shards(targets, support, label_weights, labels, first_moment, second_moment):
    pixels = support.shape[1]
    target_count = targets.shape[0] * lax.axis_size("tgt")
    support_count = support.shape[0] * lax.axis_size("sup")
    class_count = label_weights.shape[1]
    support_diag = row_squares(support) / pixels + bias_var
    slabs = lax.all_to_all(support, "sup", split_axis=1, concat_axis=0, tiled=True)
    partial_cross = lax.dot_general(
        targets, slabs, (((1,), (1,)), ((), ())), preferred_element_type=jnp.float32
    )
    cross = (
        lax.psum_scatter(
            partial_cross.astype(jnp.bfloat16), "sup", scatter_dimension=1, tiled=True
        ).astype(jnp.float32)
        / pixels
        + bias_var
    )
    target_diag = lax.psum(row_squares(targets), "sup") / pixels + bias_var

    def kernel_of(cross_in, diag_in):
        return tangent_kernel(cross_in, target_diag, diag_in)

    kernel, pullback = jax.vjp(kernel_of, cross, support_diag)
    partial_pred = jnp.dot(
        kernel.astype(jnp.bfloat16), label_weights, preferred_element_type=jnp.float32
    )
    predicted = lax.psum(partial_pred.astype(jnp.bfloat16), "sup").astype(jnp.float32)
    classes = jnp.arange(class_count, dtype=jnp.int32)
    onehot = (labels[:, None] == classes[None, :]).astype(jnp.float32)
    residual = (predicted - onehot).astype(jnp.bfloat16)
    kernel_grad = lax.dot_general(
        residual, label_weights, (((1,), (1,)), ((), ())), preferred_element_type=jnp.float32
    )
    kernel_grad = kernel_grad * (
        4.0 * pixels * math.sqrt(class_count * support_count / target_count)
    )
    cross_grad, norm_grad = pullback(kernel_grad)
    cross_low = cross_grad.astype(jnp.bfloat16)
    all_grads = lax.all_gather(cross_low, "sup", axis=1, tiled=True)
    slab_grad = lax.dot_general(
        all_grads, targets, (((0,), (0,)), ((), ())), preferred_element_type=jnp.float32
    )
    image_grad = lax.all_to_all(
        slab_grad.astype(jnp.bfloat16), "sup", split_axis=0, concat_axis=1, tiled=True
    ).astype(slab_grad.dtype)
    gradient = (image_grad + 2.0 * norm_grad[:, None] * support.astype(jnp.float32)) / pixels
    shares = lax.psum_scatter(gradient, "tgt", scatter_dimension=1, tiled=True)
    slab_width = shares.shape[1]
    own_pixels = lax.dynamic_slice_in_dim(
        support, lax.axis_index("tgt") * slab_width, slab_width, 1
    ).astype(jnp.float32)
    new_first = first_decay * first_moment + (1.0 - first_decay) * shares
    new_second = second_decay * second_moment + (1.0 - second_decay) * shares * shares
    update = (
        learning_rate * (new_first / first_fix) / (jnp.sqrt(new_second / second_fix) + adam_eps)
    )
    new_slab = (own_pixels - update).astype(jnp.bfloat16)
    new_support = lax.all_gather(new_slab, "tgt", axis=1, tiled=True)
    return (new_support, new_first, new_second)


MESH = pl.DeviceIdType.MESH
f32 = jnp.float32
bf16 = jnp.bfloat16


@jax.custom_jvp
def arcsine(x):
    a = jnp.abs(x)
    big = a > 0.5
    z = jnp.where(big, 0.5 * (1.0 - a), a * a)
    s = jnp.where(big, jnp.sqrt(z), a)
    p = 4.2163199048e-2 * z + 2.4181311049e-2
    p = p * z + 4.5470025998e-2
    p = p * z + 7.4953002686e-2
    p = p * z + 1.6666752422e-1
    p = p * z * s + s
    r = jnp.where(big, math.pi / 2.0 - 2.0 * p, p)
    return jnp.where(x < 0.0, -r, r)


@arcsine.defjvp
def arcsine_jvp(primals, tangents):
    (x,) = primals
    (t,) = tangents
    return arcsine(x), t * lax.rsqrt(1.0 - x * x)


def tangent_tile(cross, target_diag, support_diag):
    tangent = cross
    current = cross
    left = target_diag
    right = support_diag
    for _ in range(DEPTH):
        product = (1.0 + 2.0 * left) * (1.0 + 2.0 * right)
        slope = 4.0 / math.pi * lax.rsqrt(product - 4.0 * current * current)
        current = 2.0 / math.pi * arcsine(2.0 * current * lax.rsqrt(product)) + bias_var
        tangent = current + slope * tangent
        left = 2.0 / math.pi * arcsine(2.0 * left / (1.0 + 2.0 * left)) + bias_var
        right = 2.0 / math.pi * arcsine(2.0 * right / (1.0 + 2.0 * right)) + bias_var
    return tangent


def to_row(col, offset, lanes):
    shape = (col.shape[0], lanes)
    hit = lax.broadcasted_iota(jnp.int32, shape, 1) == lax.broadcasted_iota(jnp.int32, shape, 0) + offset
    return jnp.sum(jnp.where(hit, col, 0.0), axis=0, keepdims=True)


def to_col(row, count, offset=0):
    shape = (count, row.shape[1])
    hit = lax.broadcasted_iota(jnp.int32, shape, 1) == lax.broadcasted_iota(jnp.int32, shape, 0) + offset
    return jnp.sum(jnp.where(hit, row, 0.0), axis=1, keepdims=True)


MESSAGES = 200
CHUNKS = 3
STRIPS = 4
DIRECT = (0,)
DIRECT_STEPS = (4, 5)


def support_chain(diag):
    factors, rates = [], []
    right = diag
    for _ in range(DEPTH):
        plus = 1.0 + 2.0 * right
        factors.append(plus)
        rates.append(4.0 / math.pi / (plus * jnp.sqrt(1.0 + 4.0 * right)))
        right = 2.0 / math.pi * arcsine(2.0 * right / plus) + bias_var
    return factors, rates


def target_chain(diag):
    roots = []
    left = diag
    for _ in range(DEPTH):
        plus = 1.0 + 2.0 * left
        roots.append(lax.rsqrt(plus))
        left = 2.0 / math.pi * arcsine(2.0 * left / plus) + bias_var
    return roots


def forward(cross, roots, factors):
    tangent, current = cross, cross
    saved = []
    for root, plus in zip(roots, factors):
        twice = root * (2.0 * lax.rsqrt(plus))
        sine = current * twice
        inverse = lax.rsqrt(1.0 - sine * sine)
        slope = 2.0 / math.pi * twice * inverse
        saved.append((twice, sine, inverse, slope, tangent))
        current = 2.0 / math.pi * arcsine(sine) + bias_var
        tangent = current + slope * tangent
    return tangent, saved


def backward(grad, saved, factors, rates):
    tangent_bar, current_bar = grad, jnp.zeros_like(grad)
    diag_bar = None
    for layer in reversed(range(DEPTH)):
        twice, sine, inverse, slope, tangent = saved[layer]
        total = current_bar + tangent_bar
        next_bar = tangent_bar * slope
        carried = next_bar * tangent * inverse * inverse
        direct = -jnp.sum(carried + 2.0 / math.pi * total * inverse * sine, axis=0, keepdims=True) / factors[layer]
        diag_bar = direct if diag_bar is None else direct + diag_bar * rates[layer]
        current_bar = total * slope + twice * sine * carried
        tangent_bar = next_bar
    return current_bar + tangent_bar, diag_bar


def step_kernel(
    scale, pixels,
    t_hbm, s_hbm, w_hbm, labels_hbm, m1_hbm, m2_hbm,
    out_ref, n1_ref, n2_ref,
    t_v, slab, sup_v, lw, tacc, dmsg_s, dmsg_r, cacc, cmsg_s, cmsg_r, low, nmsg_s, nmsg_r,
    sy, sz, ry, rz, keep, s3, r3, s4, r4, mom, labels_ref, m1_ref, m2_ref,
    send_sem, recv_sem, local_sem,
):
    tgt = lax.axis_index("tgt")
    x = lax.axis_index("sup")
    core = lax.rem(tgt, 2)
    yy = lax.rem(tgt // 2, 2)
    z0 = lax.rem(tgt // 4, 2)
    z1 = tgt // 8
    sib_t = tgt + 1 - 2 * core
    y_t = tgt + 2 - 4 * yy
    z0_t = tgt + 4 - 8 * z0
    z1_t = tgt + 8 - 16 * z1
    SIB, YP, ZP, ZF = (sib_t, x), (y_t, x), (z0_t, x), (z1_t, x)
    XP, XS, AN = (tgt, 1 - x), (sib_t, 1 - x), (z1_t, 1 - x)
    DG = (y_t + z0_t - tgt, x)

    images, width = n1_ref.shape
    rows = t_v.shape[0] // 2
    half = 8 * width
    part = rows // 2
    lanes = slab.shape[0]
    piece = width // CHUNKS
    chunks = range(CHUNKS)

    numbers = {}

    def remote(src, dst, name, device):
        number = numbers.setdefault(name, len(numbers))
        return pltpu.make_async_remote_copy(
            src_ref=src, dst_ref=dst, send_sem=send_sem.at[number], recv_sem=recv_sem.at[number],
            device_id=device, device_id_type=MESH,
        )

    started = []

    def send(src, dst, name, device):
        copy = remote(src, dst, name, device)
        copy.start()
        started.append(copy)

    def arrived(dst, name, device):
        remote(dst, dst, name, device).wait_recv()

    def aligned(value, by):
        return pl.multiple_of(value, by)

    barrier = pltpu.get_barrier_semaphore()
    friends = (XP, XS, SIB, YP, ZP, DG, ZF, AN)
    for device in friends:
        pl.semaphore_signal(barrier, inc=1, device_id=device, device_id_type=MESH)

    locals_ = []

    def load(src, dst):
        copy = pltpu.make_async_copy(src, dst, local_sem.at[len(locals_)])
        copy.start()
        locals_.append(copy)
        return copy

    my_row = aligned(x * images, images)
    peer_row = aligned((1 - x) * images, images)

    def columns(block, owner):
        return pl.ds(aligned((2 * block + owner) * width, width), width)

    def far_columns(slab_index, block):
        return pl.ds(aligned(slab_index * half + (2 * block + core) * width, width), width)

    def block_of(j):
        return pl.ds(aligned(j * width, width), width)

    load_s = load(s_hbm, sup_v)
    mine_t = pl.ds(aligned(core * rows, rows), rows)
    load_t = [load(t_hbm.at[:, columns(j, core)], t_v.at[mine_t, block_of(j)]) for j in range(4)]
    load_o = [load(s_hbm.at[:, far_columns(x, j)], slab.at[pl.ds(my_row, images), block_of(j)]) for j in range(4)]
    load_w = load(w_hbm, lw.at[pl.ds(my_row, images), :])
    load_l = load(labels_hbm, labels_ref)
    load_1 = load(m1_hbm, m1_ref)
    load_2 = load(m2_hbm, m2_ref)

    pl.semaphore_wait(barrier, len(friends))

    seat = 2 * yy + z0
    turn = (seat, 3 - seat, seat + 2 - 4 * yy, seat + 1 - 2 * z0)
    strip = images // STRIPS
    strips = range(STRIPS)
    share = images // 2

    def send_strip(p, r):
        send(
            s_hbm.at[pl.ds(r * strip, strip), far_columns(1 - x, turn[p])],
            slab.at[pl.ds(aligned(my_row + r * strip, strip), strip), block_of(turn[p])],
            ("slab", p, r), XP,
        )

    for r in strips:
        send_strip(0, r)

    def whole(ref, row, columns):
        return ref.at[pl.ds(row, images), columns]

    send(
        s_hbm.at[:, far_columns(1 - x, turn[1])], whole(slab, my_row, block_of(turn[1])), "slab", XP,
    )
    for j in range(4):
        send(t_hbm.at[:, columns(j, 1 - core)], t_v.at[mine_t, block_of(j)], ("targets", j), SIB)
    weight_rows = pl.ds(aligned(my_row + core * share, share), share)
    send(w_hbm.at[pl.ds(aligned(core * share, share), share), :], lw.at[weight_rows, :], "weights", XP)

    load_s.wait()

    def support_squares(i, acc):
        block = sup_v[:, pl.ds(aligned(i * width, width), width)].astype(f32)
        block = block * block
        for k in range(width // 128):
            acc = acc + block[:, k * 128 : (k + 1) * 128]
        return acc

    sacc = lax.fori_loop(0, pixels // width, support_squares, jnp.zeros((images, 128), f32))
    s_row = to_row(jnp.sum(sacc, axis=1, keepdims=True), x * images, lanes)

    def target_squares(first):
        def body(i, carry):
            where = pl.ds(aligned(first + i * 16, 16), 16)
            sums = []
            for j in range(4):
                block = t_v[where, j * width : (j + 1) * width].astype(f32)
                block = block * block
                acc = block[:, 0:128]
                for k in range(1, width // 128):
                    acc = acc + block[:, k * 128 : (k + 1) * 128]
                sums.append(acc)
            tacc[where, :] = (sums[0] + sums[1]) + (sums[2] + sums[3])
            return carry

        lax.fori_loop(0, rows // 16, body, 0)

    for copy in load_t:
        copy.wait()
    target_squares(core * rows)

    def strip_of(p, r):
        return slab.at[pl.ds(aligned(peer_row + r * strip, strip), strip), block_of(turn[p])]

    for r in strips:
        here = strip_of(0, r)
        arrived(here, ("slab", 0, r), XP)
        send(here, here, ("slab", 2, r), YP)
        send(here, here, ("slab", 3, r), ZP)

    other_t = pl.ds(aligned((1 - core) * rows, rows), rows)
    for j in range(4):
        arrived(t_v.at[other_t, block_of(j)], ("targets", j), SIB)
    target_squares((1 - core) * rows)

    group = (SIB, XP, XS)
    quarter = 2 * core + x
    theirs = (2 * (1 - core) + x, 2 * core + 1 - x, 2 * (1 - core) + 1 - x)

    def rows_of(q):
        return pl.ds(aligned(q * part, part), part)

    def square_col(q):
        return jnp.sum(tacc[rows_of(q), :], axis=1, keepdims=True)

    for i in range(3):
        dmsg_s[i, 0:8, :] = jnp.broadcast_to(to_row(square_col(theirs[i]), 0, lanes), (8, lanes))
        dmsg_s[i, 8:16, :] = jnp.broadcast_to(s_row, (8, lanes))
        send(dmsg_s.at[i], dmsg_r.at[i], ("diag", i), group[i])
    my_sq = square_col(quarter)
    load_l.wait()
    label_col = to_col(labels_ref[...].astype(f32), part, x * part)

    for copy in load_o:
        copy.wait()

    def cross_piece(p, first=False):
        value = lax.dot_general(
            t_v[:, block_of(turn[p])], slab[:, block_of(turn[p])], (((1,), (1,)), ((), ())),
            preferred_element_type=f32,
        )
        cacc[...] = value if first else cacc[...] + value

    cross_piece(0, True)
    arrived(whole(slab, peer_row, block_of(turn[1])), "slab", XP)
    half_rows = lw.at[pl.ds(aligned(peer_row + core * share, share), share), :]
    arrived(half_rows, "weights", XP)
    send(half_rows, half_rows, "weights on", SIB)
    cross_piece(1)
    for r in strips:
        arrived(strip_of(2, r), ("slab", 2, r), YP)
    cross_piece(2)
    for r in strips:
        arrived(strip_of(3, r), ("slab", 3, r), ZP)

    def last_piece(q):
        return cacc[rows_of(q), :] + lax.dot_general(
            t_v[rows_of(q), block_of(turn[3])], slab[:, block_of(turn[3])], (((1,), (1,)), ((), ())),
            preferred_element_type=f32,
        )

    for i in (2, 1, 0):
        cmsg_s[i] = last_piece(theirs[i]).astype(bf16)
        send(cmsg_s.at[i], cmsg_r.at[i], ("cross", i), group[i])
    own_cross = last_piece(quarter)
    load_1.wait()
    load_2.wait()
    mom[0, z1] = m1_ref[...].astype(bf16)
    mom[1, z1] = m2_ref[...].astype(bf16)
    for i in (0, 1):
        here = mom.at[i, z1]
        send(here, here, ("moment", i), ZF)

    for i in range(3):
        arrived(dmsg_r.at[i], ("diag", i), group[i])
    square_row = dmsg_r[0, 0:1, :] + dmsg_r[1, 0:1, :] + dmsg_r[2, 0:1, :]
    roots = target_chain((my_sq + to_col(square_row, part)) / pixels + bias_var)
    factors, rates = support_chain((s_row + dmsg_r[1, 8:9, :]) / pixels + bias_var)
    load_w.wait()
    arrived(lw.at[pl.ds(aligned(peer_row + (1 - core) * share, share), share), :], "weights on", SIB)

    for i in range(3):
        arrived(cmsg_r.at[i], ("cross", i), group[i])
    total = own_cross + cmsg_r[0].astype(f32)
    total = total + (cmsg_r[1].astype(f32) + cmsg_r[2].astype(f32))
    kernel, saved = forward(total / pixels + bias_var, roots, factors)
    weights = lw[...]
    predicted = jnp.dot(kernel.astype(bf16), weights, preferred_element_type=f32)
    classes = lax.broadcasted_iota(jnp.int32, predicted.shape, 1)
    onehot = (label_col == classes.astype(f32)).astype(f32)
    residual = (predicted - onehot).astype(bf16)
    kernel_grad = scale * lax.dot_general(
        residual, weights, (((1,), (1,)), ((), ())), preferred_element_type=f32
    )
    cross_grad, norm_grad = backward(kernel_grad, saved, factors, rates)
    mine_low = low.at[rows_of(quarter), :]
    mine_low[...] = cross_grad.astype(bf16)
    for i in (2, 1, 0):
        send(mine_low, mine_low, ("low", i), group[i])
    nmsg_s[...] = jnp.broadcast_to(norm_grad, nmsg_s.shape)
    for i in (2, 1, 0):
        send(nmsg_s, nmsg_r.at[i], ("norm", i), group[i])
    for i in range(3):
        arrived(low.at[rows_of(theirs[i]), :], ("low", i), group[i])
    for i in range(3):
        arrived(nmsg_r.at[i], ("norm", i), group[i])
    norm_row = norm_grad + nmsg_r[0, 0:1, :] + nmsg_r[1, 0:1, :] + nmsg_r[2, 0:1, :]
    norm_col = to_col(2.0 * norm_row, lanes)
    grads = low[...].astype(f32).T.astype(bf16)

    order = ((1, 1), (0, 1), (1, 0), (0, 0))
    first = slice(0, images)
    second = slice(images, 2 * images)

    def block_grad(k, h):
        dz, dy = order[k]
        number = (z0 + dz - 2 * dz * z0) * 2 + (yy + dy - 2 * dy * yy)
        where = pl.ds(aligned(number * width + h * piece, piece), piece)
        value = jnp.dot(grads, t_v[:, where], preferred_element_type=f32)
        return value + norm_col * slab[:, where].astype(f32)

    for h in chunks:
        straight = h in DIRECT
        value = block_grad(0, h)
        sy[0, h] = value[first].astype(bf16)
        send(sy.at[0, h], ry.at[0, h], ("y", 0, h), DG if straight else YP)
        sz[0, h] = value[second].astype(bf16)
        send(sz.at[0, h], rz.at[0, h], ("z", 0, h), DG if straight else ZP)
        value = block_grad(1, h)
        sy[1, h] = value[first].astype(bf16)
        send(sy.at[1, h], ry.at[1, h], ("y", 1, h), YP)
        if straight:
            s3[1, h] = value[second].astype(bf16)
            send(s3.at[1, h], r3.at[1, h], ("late y", h), YP)
        else:
            keep[0, h] = value[second]
        value = block_grad(2, h)
        sz[1, h] = value[second].astype(bf16)
        send(sz.at[1, h], rz.at[1, h], ("z", 1, h), ZP)
        if straight:
            s3[0, h] = value[first].astype(bf16)
            send(s3.at[0, h], r3.at[0, h], ("late z", h), ZP)
        else:
            keep[1, h] = value[first]
    for h in chunks:
        value = block_grad(3, h)
        keep[2, h] = value[first]
        keep[3, h] = value[second]

    def late(h):
        arrived(ry.at[0, h], ("y", 0, h), YP)
        s3[0, h] = (keep[1, h] + ry[0, h].astype(f32)).astype(bf16)
        send(s3.at[0, h], r3.at[0, h], ("late z", h), ZP)
        arrived(rz.at[0, h], ("z", 0, h), ZP)
        s3[1, h] = (keep[0, h] + rz[0, h].astype(f32)).astype(bf16)
        send(s3.at[1, h], r3.at[1, h], ("late y", h), YP)

    def group_sum(h):
        arrived(ry.at[1, h], ("y", 1, h), YP)
        one = keep[2, h] + ry[1, h].astype(f32)
        arrived(rz.at[1, h], ("z", 1, h), ZP)
        two = keep[3, h] + rz[1, h].astype(f32)
        if h in DIRECT:
            arrived(ry.at[0, h], ("y", 0, h), DG)
            one = one + ry[0, h].astype(f32)
            arrived(rz.at[0, h], ("z", 0, h), DG)
            two = two + rz[0, h].astype(f32)
        arrived(r3.at[0, h], ("late z", h), ZP)
        s4[0, h] = (one + r3[0, h].astype(f32)).astype(bf16)
        arrived(r3.at[1, h], ("late y", h), YP)
        s4[1, h] = (two + r3[1, h].astype(f32)).astype(bf16)
        send(s4.at[x, h], r4.at[0, h], ("last z", h), ZF)
        send(s4.at[1 - x, h], r4.at[1, h], ("last a", h), AN)
        send(s4.at[1 - x, h], r4.at[2, h], ("last x", h), XP)

    for h in chunks:
        if h in DIRECT:
            group_sum(h)
    for h in chunks:
        if h not in DIRECT:
            late(h)
    for h in chunks:
        if h not in DIRECT:
            group_sum(h)

    for i in (0, 1):
        arrived(mom.at[i, 1 - z1], ("moment", i), ZF)

    def cut(index, h):
        return pl.ds(aligned(index * width + h * piece, piece), piece)

    def pass_on(index, name, device, h):
        here = out_ref.at[:, cut(index, h)]
        send(here, here, (name, h), device)

    def came(index, name, device, h):
        arrived(out_ref.at[:, cut(index, h)], (name, h), device)

    def moved(first_in, second_in, gradient):
        new_first = first_decay * first_in + (1.0 - first_decay) * gradient
        new_second = second_decay * second_in + (1.0 - second_decay) * gradient * gradient
        return new_first, new_second

    slabs = (x, 1 - x)
    tgt_in = tgt - 8 * z1
    y_in, z_in, d_in = y_t - 8 * z1, z0_t - 8 * z1, y_t + z0_t - tgt - 8 * z1
    swap = sib_t - tgt

    steps = [(h, i) for h in chunks for i in (0, 1)]
    straight_steps = [steps[n] for n in DIRECT_STEPS]

    def adam(h, i):
        here = slice(h * piece, (h + 1) * piece)
        side = slabs[i]
        if i == 0:
            arrived(r4.at[0, h], ("last z", h), ZF)
            gradient = (s4[x, h].astype(f32) + r4[0, h].astype(f32)) / pixels
        else:
            arrived(r4.at[2, h], ("last x", h), XP)
            arrived(r4.at[1, h], ("last a", h), AN)
            gradient = (r4[1, h].astype(f32) + r4[2, h].astype(f32)) / pixels
        new_first, new_second = moved(mom[0, side, :, here].astype(f32), mom[1, side, :, here].astype(f32), gradient)
        update = learning_rate * (new_first / first_fix) / (jnp.sqrt(new_second / second_fix) + adam_eps)
        spot = tgt_in + 8 * side
        out_ref[:, cut(spot, h)] = (sup_v[:, cut(spot, h)].astype(f32) - update).astype(bf16)
        pass_on(spot, ("own z", i), ZP, h)
        pass_on(spot, ("own y", i), YP, h)
        if (h, i) in straight_steps:
            pass_on(spot, ("own d", i), DG, h)
        pass_on(spot, ("own s", i), SIB, h)

        @pl.when(side == z1)
        def _():
            new_first, new_second = moved(m1_ref[:, here], m2_ref[:, here], gradient)
            n1_ref[:, here] = new_first
            n2_ref[:, here] = new_second

    def relay(h, i):
        side = 8 * slabs[i]
        came(side + z_in, ("own z", i), ZP, h)
        if (h, i) not in straight_steps:
            pass_on(side + z_in, ("z y", i), YP, h)
        pass_on(side + z_in, ("z s", i), SIB, h)
        came(side + y_in, ("own y", i), YP, h)
        pass_on(side + y_in, ("y s", i), SIB, h)

    def finish(h, i):
        side = 8 * slabs[i]
        if (h, i) in straight_steps:
            came(side + d_in, ("own d", i), DG, h)
        else:
            came(side + d_in, ("z y", i), YP, h)
        pass_on(side + d_in, ("d s", i), SIB, h)

    for n in range(len(steps)):
        adam(*steps[n])
        if n >= 2:
            relay(*steps[n - 2])
    relay(*steps[-2])
    relay(*steps[-1])
    for step in steps:
        finish(*step)
    for h, i in steps:
        side = 8 * slabs[i] + swap
        came(side + tgt_in, ("own s", i), SIB, h)
        came(side + z_in, ("z s", i), SIB, h)
        came(side + y_in, ("y s", i), SIB, h)
        came(side + d_in, ("d s", i), SIB, h)

    for copy in started:
        copy.wait_send()


def fused(targets, support, label_weights, labels, first_moment, second_moment):
    rows, _ = targets.shape
    images, pixels = support.shape
    width = first_moment.shape[1]
    classes = label_weights.shape[1]
    target_count = rows * lax.axis_size("tgt")
    support_count = images * lax.axis_size("sup")
    scale = 4.0 * pixels * math.sqrt(classes * support_count / target_count)
    everyone, part, piece = 2 * images, rows // 2, width // CHUNKS
    hbm = pl.BlockSpec(memory_space=pltpu.HBM)
    vmem = pl.BlockSpec(memory_space=pltpu.VMEM)
    slots = pltpu.VMEM((2, CHUNKS, images, piece), bf16)
    return pl.pallas_call(
        functools.partial(step_kernel, scale, pixels),
        out_shape=(
            pltpu.VMEM(support.shape, bf16),
            pltpu.VMEM(first_moment.shape, f32),
            pltpu.VMEM(first_moment.shape, f32),
        ),
        in_specs=[hbm] * 6,
        out_specs=(vmem, vmem, vmem),
        scratch_shapes=[
            pltpu.VMEM((2 * rows, 4 * width), bf16),
            pltpu.VMEM((everyone, 4 * width), bf16),
            pltpu.VMEM((images, pixels), bf16),
            pltpu.VMEM((everyone, classes), bf16),
            pltpu.VMEM((2 * rows, 128), f32),
            pltpu.VMEM((3, 16, everyone), f32),
            pltpu.VMEM((3, 16, everyone), f32),
            pltpu.VMEM((2 * rows, everyone), f32),
            pltpu.VMEM((3, part, everyone), bf16),
            pltpu.VMEM((3, part, everyone), bf16),
            pltpu.VMEM((2 * rows, everyone), bf16),
            pltpu.VMEM((8, everyone), f32),
            pltpu.VMEM((3, 8, everyone), f32),
            slots,
            slots,
            slots,
            slots,
            pltpu.VMEM((4, CHUNKS, images, piece), f32),
            slots,
            slots,
            slots,
            pltpu.VMEM((3, CHUNKS, images, piece), bf16),
            pltpu.VMEM((2, 2, images, width), bf16),
            pltpu.VMEM((1, rows), jnp.int32),
            pltpu.VMEM((images, width), f32),
            pltpu.VMEM((images, width), f32),
            pltpu.SemaphoreType.DMA((MESSAGES,)),
            pltpu.SemaphoreType.DMA((MESSAGES,)),
            pltpu.SemaphoreType.DMA((16,)),
        ],
        compiler_params=pltpu.CompilerParams(
            collective_id=0, has_side_effects=True, vmem_limit_bytes=60000000
        ),
    )(targets, support, label_weights, labels[None, :], first_moment, second_moment)


def hand_over(a_ref, b_ref, c_ref, x_ref, y_ref, z_ref, sem):
    copies = [
        pltpu.make_async_copy(src, dst, sem.at[i])
        for i, (src, dst) in enumerate(((a_ref, x_ref), (b_ref, y_ref), (c_ref, z_ref)))
    ]
    for copy in copies:
        copy.start()
    for copy in copies:
        copy.wait()


def settle(support, first, second, space):
    return pl.pallas_call(
        hand_over,
        out_shape=tuple(jax.ShapeDtypeStruct(a.shape, a.dtype) for a in (support, first, second)),
        in_specs=[pl.BlockSpec(memory_space=space)] * 3,
        out_specs=(pl.BlockSpec(memory_space=pltpu.HBM),) * 3,
        scratch_shapes=[pltpu.SemaphoreType.DMA((3,))],
    )(support, first, second)


def pick(mesh):
    groups, shares = mesh.shape["sup"], mesh.shape["tgt"]

    def run(targets, support, label_weights, labels, first_moment, second_moment):
        width = first_moment.shape[1]
        fits = groups == 2 and shares == 16 and width % (128 * CHUNKS) == 0
        fits = fits and targets.shape[0] % 32 == 0 and groups * support.shape[0] == 128
        body = fused if fits else shards
        out = body(targets, support, label_weights, labels, first_moment, second_moment)
        return settle(*[pltpu.with_memory_space_constraint(o, pltpu.VMEM) for o in out], pltpu.VMEM) if fits else out

    return run


def solution(mesh):
    return jax.shard_map(
        pick(mesh),
        mesh=mesh,
        in_specs=(
            P("tgt", "sup"),
            P("sup", None),
            P("sup", None),
            P("tgt"),
            P("sup", "tgt"),
            P("sup", "tgt"),
        ),
        out_specs=(P("sup", None), P("sup", "tgt"), P("sup", "tgt")),
        check_vma=False,
    )
```

```python
import functools
import math

import jax
import jax.numpy as jnp
from jax import lax
from jax.experimental import pallas as pl
from jax.experimental.pallas import tpu as pltpu
from jax.sharding import PartitionSpec as P

DEPTH = 3


bias_var = 0.1
learning_rate = 0.05
first_decay = 0.9
second_decay = 0.99
first_fix = 1.0 - 0.9**10
second_fix = 1.0 - 0.99**10
adam_eps = 1e-08


def tangent_kernel(cross, target_diag, support_diag):
    tangent = cross
    current = cross
    left_diag = target_diag
    right_diag = support_diag
    for _ in range(DEPTH):
        product = (1.0 + 2.0 * left_diag)[:, None] * (1.0 + 2.0 * right_diag)[None, :]
        slope = 4.0 / math.pi / jnp.sqrt(product - 4.0 * current * current)
        current = 2.0 / math.pi * jnp.arcsin(2.0 * current / jnp.sqrt(product)) + bias_var
        tangent = current + slope * tangent
        left_diag = 2.0 / math.pi * jnp.arcsin(2.0 * left_diag / (1.0 + 2.0 * left_diag)) + bias_var
        right_diag = (
            2.0 / math.pi * jnp.arcsin(2.0 * right_diag / (1.0 + 2.0 * right_diag)) + bias_var
        )
    return tangent


def row_squares(images):
    return jnp.sum(jnp.square(images.astype(jnp.float32)), axis=1)


def shards(targets, support, label_weights, labels, first_moment, second_moment):
    pixels = support.shape[1]
    target_count = targets.shape[0] * lax.axis_size("tgt")
    support_count = support.shape[0] * lax.axis_size("sup")
    class_count = label_weights.shape[1]
    support_diag = row_squares(support) / pixels + bias_var
    slabs = lax.all_to_all(support, "sup", split_axis=1, concat_axis=0, tiled=True)
    partial_cross = lax.dot_general(
        targets, slabs, (((1,), (1,)), ((), ())), preferred_element_type=jnp.float32
    )
    cross = (
        lax.psum_scatter(
            partial_cross.astype(jnp.bfloat16), "sup", scatter_dimension=1, tiled=True
        ).astype(jnp.float32)
        / pixels
        + bias_var
    )
    target_diag = lax.psum(row_squares(targets), "sup") / pixels + bias_var

    def kernel_of(cross_in, diag_in):
        return tangent_kernel(cross_in, target_diag, diag_in)

    kernel, pullback = jax.vjp(kernel_of, cross, support_diag)
    partial_pred = jnp.dot(
        kernel.astype(jnp.bfloat16), label_weights, preferred_element_type=jnp.float32
    )
    predicted = lax.psum(partial_pred.astype(jnp.bfloat16), "sup").astype(jnp.float32)
    classes = jnp.arange(class_count, dtype=jnp.int32)
    onehot = (labels[:, None] == classes[None, :]).astype(jnp.float32)
    residual = (predicted - onehot).astype(jnp.bfloat16)
    kernel_grad = lax.dot_general(
        residual, label_weights, (((1,), (1,)), ((), ())), preferred_element_type=jnp.float32
    )
    kernel_grad = kernel_grad * (
        4.0 * pixels * math.sqrt(class_count * support_count / target_count)
    )
    cross_grad, norm_grad = pullback(kernel_grad)
    cross_low = cross_grad.astype(jnp.bfloat16)
    all_grads = lax.all_gather(cross_low, "sup", axis=1, tiled=True)
    slab_grad = lax.dot_general(
        all_grads, targets, (((0,), (0,)), ((), ())), preferred_element_type=jnp.float32
    )
    image_grad = lax.all_to_all(
        slab_grad.astype(jnp.bfloat16), "sup", split_axis=0, concat_axis=1, tiled=True
    ).astype(slab_grad.dtype)
    gradient = (image_grad + 2.0 * norm_grad[:, None] * support.astype(jnp.float32)) / pixels
    shares = lax.psum_scatter(gradient, "tgt", scatter_dimension=1, tiled=True)
    slab_width = shares.shape[1]
    own_pixels = lax.dynamic_slice_in_dim(
        support, lax.axis_index("tgt") * slab_width, slab_width, 1
    ).astype(jnp.float32)
    new_first = first_decay * first_moment + (1.0 - first_decay) * shares
    new_second = second_decay * second_moment + (1.0 - second_decay) * shares * shares
    update = (
        learning_rate * (new_first / first_fix) / (jnp.sqrt(new_second / second_fix) + adam_eps)
    )
    new_slab = (own_pixels - update).astype(jnp.bfloat16)
    new_support = lax.all_gather(new_slab, "tgt", axis=1, tiled=True)
    return (new_support, new_first, new_second)


MESH = pl.DeviceIdType.MESH
f32 = jnp.float32
bf16 = jnp.bfloat16


@jax.custom_jvp
def arcsine(x):
    a = jnp.abs(x)
    big = a > 0.5
    z = jnp.where(big, 0.5 * (1.0 - a), a * a)
    s = jnp.where(big, jnp.sqrt(z), a)
    p = 4.2163199048e-2 * z + 2.4181311049e-2
    p = p * z + 4.5470025998e-2
    p = p * z + 7.4953002686e-2
    p = p * z + 1.6666752422e-1
    p = p * z * s + s
    r = jnp.where(big, math.pi / 2.0 - 2.0 * p, p)
    return jnp.where(x < 0.0, -r, r)


@arcsine.defjvp
def arcsine_jvp(primals, tangents):
    (x,) = primals
    (t,) = tangents
    return arcsine(x), t * lax.rsqrt(1.0 - x * x)


def tangent_tile(cross, target_diag, support_diag):
    tangent = cross
    current = cross
    left = target_diag
    right = support_diag
    for _ in range(DEPTH):
        product = (1.0 + 2.0 * left) * (1.0 + 2.0 * right)
        slope = 4.0 / math.pi * lax.rsqrt(product - 4.0 * current * current)
        current = 2.0 / math.pi * arcsine(2.0 * current * lax.rsqrt(product)) + bias_var
        tangent = current + slope * tangent
        left = 2.0 / math.pi * arcsine(2.0 * left / (1.0 + 2.0 * left)) + bias_var
        right = 2.0 / math.pi * arcsine(2.0 * right / (1.0 + 2.0 * right)) + bias_var
    return tangent


def to_row(col, offset, lanes):
    shape = (col.shape[0], lanes)
    hit = lax.broadcasted_iota(jnp.int32, shape, 1) == lax.broadcasted_iota(jnp.int32, shape, 0) + offset
    return jnp.sum(jnp.where(hit, col, 0.0), axis=0, keepdims=True)


def to_col(row, count, offset=0):
    shape = (count, row.shape[1])
    hit = lax.broadcasted_iota(jnp.int32, shape, 1) == lax.broadcasted_iota(jnp.int32, shape, 0) + offset
    return jnp.sum(jnp.where(hit, row, 0.0), axis=1, keepdims=True)


SENDS, RECEIVES, LOADS = 10, 45, 7
CHUNKS = 3
STRIPS = 4
DIRECT = (0,)
DIRECT_STEPS = (4, 5)


def support_chain(diag):
    factors, rates = [], []
    right = diag
    for _ in range(DEPTH):
        plus = 1.0 + 2.0 * right
        factors.append(plus)
        rates.append(4.0 / math.pi / (plus * jnp.sqrt(1.0 + 4.0 * right)))
        right = 2.0 / math.pi * arcsine(2.0 * right / plus) + bias_var
    return factors, rates


def target_chain(diag):
    roots = []
    left = diag
    for _ in range(DEPTH):
        plus = 1.0 + 2.0 * left
        roots.append(lax.rsqrt(plus))
        left = 2.0 / math.pi * arcsine(2.0 * left / plus) + bias_var
    return roots


def forward(cross, roots, factors):
    tangent, current = cross, cross
    saved = []
    for root, plus in zip(roots, factors):
        twice = root * (2.0 * lax.rsqrt(plus))
        sine = current * twice
        inverse = lax.rsqrt(1.0 - sine * sine)
        slope = 2.0 / math.pi * twice * inverse
        saved.append((twice, sine, inverse, slope, tangent))
        current = 2.0 / math.pi * arcsine(sine) + bias_var
        tangent = current + slope * tangent
    return tangent, saved


def backward(grad, saved, factors, rates):
    tangent_bar, current_bar = grad, jnp.zeros_like(grad)
    diag_bar = None
    for layer in reversed(range(DEPTH)):
        twice, sine, inverse, slope, tangent = saved[layer]
        total = current_bar + tangent_bar
        next_bar = tangent_bar * slope
        carried = next_bar * tangent * inverse * inverse
        direct = -jnp.sum(carried + 2.0 / math.pi * total * inverse * sine, axis=0, keepdims=True) / factors[layer]
        diag_bar = direct if diag_bar is None else direct + diag_bar * rates[layer]
        current_bar = total * slope + twice * sine * carried
        tangent_bar = next_bar
    return current_bar + tangent_bar, diag_bar


def step_kernel(
    scale, pixels,
    t_hbm, s_hbm, w_hbm, labels_hbm, m1_hbm, m2_hbm,
    out_ref, n1_ref, n2_ref,
    t_v, slab, sup_v, lw, tacc, dmsg_s, dmsg_r, cacc, cmsg_s, cmsg_r, low, nmsg_s, nmsg_r,
    sy, sz, ry, rz, keep, s3, r3, s4, r4, mom, labels_ref, m1_ref, m2_ref,
    send_sem, recv_sem, local_sem,
):
    tgt = lax.axis_index("tgt")
    x = lax.axis_index("sup")
    core = lax.rem(tgt, 2)
    yy = lax.rem(tgt // 2, 2)
    z0 = lax.rem(tgt // 4, 2)
    z1 = tgt // 8
    sib_t = tgt + 1 - 2 * core
    y_t = tgt + 2 - 4 * yy
    z0_t = tgt + 4 - 8 * z0
    z1_t = tgt + 8 - 16 * z1
    SIB, YP, ZP, ZF = (sib_t, x), (y_t, x), (z0_t, x), (z1_t, x)
    XP, XS, AN = (tgt, 1 - x), (sib_t, 1 - x), (z1_t, 1 - x)
    DG = (y_t + z0_t - tgt, x)

    images, width = n1_ref.shape
    rows = t_v.shape[0] // 2
    half = 8 * width
    part = rows // 2
    lanes = slab.shape[0]
    piece = width // CHUNKS
    chunks = range(CHUNKS)

    send_ids, receive_ids, counts = {}, {}, {}

    def remote(src, dst, sent, name, device):
        return pltpu.make_async_remote_copy(
            src_ref=src, dst_ref=dst, send_sem=send_sem.at[send_ids.setdefault(sent, len(send_ids))],
            recv_sem=recv_sem.at[receive_ids.setdefault(name, len(receive_ids))],
            device_id=device, device_id_type=MESH,
        )

    def send(src, dst, sent, name, device):
        counts[sent] = counts.get(sent, 0) + 1
        remote(src, dst, sent, name, device).start()

    def arrived(dst, name, device):
        pltpu.make_async_remote_copy(
            src_ref=dst, dst_ref=dst, send_sem=send_sem.at[0],
            recv_sem=recv_sem.at[receive_ids.setdefault(name, len(receive_ids))],
            device_id=device, device_id_type=MESH,
        ).wait_recv()

    def all_sent(src, sent):
        pltpu.make_async_remote_copy(
            src_ref=src, dst_ref=src, send_sem=send_sem.at[send_ids[sent]], recv_sem=recv_sem.at[0],
            device_id=SIB, device_id_type=MESH,
        ).wait_send()

    def aligned(value, by):
        return pl.multiple_of(value, by)

    barrier = pltpu.get_barrier_semaphore()
    friends = (XP, XS, SIB, YP, ZP, DG, ZF, AN)
    for device in friends:
        pl.semaphore_signal(barrier, inc=1, device_id=device, device_id_type=MESH)

    def load(src, dst, number):
        copy = pltpu.make_async_copy(src, dst, local_sem.at[number])
        copy.start()
        return copy

    my_row = aligned(x * images, images)
    peer_row = aligned((1 - x) * images, images)

    def columns(block, owner):
        return pl.ds(aligned((2 * block + owner) * width, width), width)

    def far_columns(slab_index, block):
        return pl.ds(aligned(slab_index * half + (2 * block + core) * width, width), width)

    def block_of(j):
        return pl.ds(aligned(j * width, width), width)

    load_s = load(s_hbm, sup_v, 0)
    mine_t = pl.ds(aligned(core * rows, rows), rows)
    for j in range(4):
        load(t_hbm.at[:, columns(j, core)], t_v.at[mine_t, block_of(j)], 1)
    load_t = pltpu.make_async_copy(t_v.at[mine_t, :], t_v.at[mine_t, :], local_sem.at[1])
    for j in range(4):
        load(s_hbm.at[:, far_columns(x, j)], slab.at[pl.ds(my_row, images), block_of(j)], 2)
    my_slab = slab.at[pl.ds(my_row, images), :]
    load_o = pltpu.make_async_copy(my_slab, my_slab, local_sem.at[2])
    load_w = load(w_hbm, lw.at[pl.ds(my_row, images), :], 3)
    load_l = load(labels_hbm, labels_ref, 4)
    load_1 = load(m1_hbm, m1_ref, 5)
    load_2 = load(m2_hbm, m2_ref, 6)

    pl.semaphore_wait(barrier, len(friends))

    seat = 2 * yy + z0
    turn = (seat, 3 - seat, seat + 2 - 4 * yy, seat + 1 - 2 * z0)
    strip = images // STRIPS
    strips = range(STRIPS)
    share = images // 2

    def send_strip(p, r):
        send(
            s_hbm.at[pl.ds(r * strip, strip), far_columns(1 - x, turn[p])],
            slab.at[pl.ds(aligned(my_row + r * strip, strip), strip), block_of(turn[p])],
            "slab", ("slab", p, r), XP,
        )

    for r in strips:
        send_strip(0, r)

    def whole(ref, row, columns):
        return ref.at[pl.ds(row, images), columns]

    send(
        s_hbm.at[:, far_columns(1 - x, turn[1])], whole(slab, my_row, block_of(turn[1])), "slab", "slab", XP,
    )
    for j in range(4):
        send(t_hbm.at[:, columns(j, 1 - core)], t_v.at[mine_t, block_of(j)], "targets", "targets", SIB)
    weight_rows = pl.ds(aligned(my_row + core * share, share), share)
    send(w_hbm.at[pl.ds(aligned(core * share, share), share), :], lw.at[weight_rows, :], "weights", "weights", XP)

    load_s.wait()

    def support_squares(i, acc):
        block = sup_v[:, pl.ds(aligned(i * width, width), width)].astype(f32)
        block = block * block
        for k in range(width // 128):
            acc = acc + block[:, k * 128 : (k + 1) * 128]
        return acc

    sacc = lax.fori_loop(0, pixels // width, support_squares, jnp.zeros((images, 128), f32))
    s_row = to_row(jnp.sum(sacc, axis=1, keepdims=True), x * images, lanes)

    def target_squares(first):
        def body(i, carry):
            where = pl.ds(aligned(first + i * 16, 16), 16)
            sums = []
            for j in range(4):
                block = t_v[where, j * width : (j + 1) * width].astype(f32)
                block = block * block
                acc = block[:, 0:128]
                for k in range(1, width // 128):
                    acc = acc + block[:, k * 128 : (k + 1) * 128]
                sums.append(acc)
            tacc[where, :] = (sums[0] + sums[1]) + (sums[2] + sums[3])
            return carry

        lax.fori_loop(0, rows // 16, body, 0)

    load_t.wait()
    target_squares(core * rows)

    def strip_of(p, r):
        return slab.at[pl.ds(aligned(peer_row + r * strip, strip), strip), block_of(turn[p])]

    for r in strips:
        here = strip_of(0, r)
        arrived(here, ("slab", 0, r), XP)
        send(here, here, "slab", "slab y", YP)
        send(here, here, "slab", "slab z", ZP)

    other_t = pl.ds(aligned((1 - core) * rows, rows), rows)
    arrived(t_v.at[other_t, :], "targets", SIB)
    target_squares((1 - core) * rows)

    group = (SIB, XP, XS)
    quarter = 2 * core + x
    theirs = (2 * (1 - core) + x, 2 * core + 1 - x, 2 * (1 - core) + 1 - x)

    def rows_of(q):
        return pl.ds(aligned(q * part, part), part)

    def square_col(q):
        return jnp.sum(tacc[rows_of(q), :], axis=1, keepdims=True)

    for i in range(3):
        dmsg_s[i, 0:8, :] = jnp.broadcast_to(to_row(square_col(theirs[i]), 0, lanes), (8, lanes))
        dmsg_s[i, 8:16, :] = jnp.broadcast_to(s_row, (8, lanes))
        send(dmsg_s.at[i], dmsg_r.at[i], "diag", "diag", group[i])
    my_sq = square_col(quarter)
    load_l.wait()
    label_col = to_col(labels_ref[...].astype(f32), part, x * part)

    load_o.wait()

    def cross_piece(p, first=False):
        value = lax.dot_general(
            t_v[:, block_of(turn[p])], slab[:, block_of(turn[p])], (((1,), (1,)), ((), ())),
            preferred_element_type=f32,
        )
        cacc[...] = value if first else cacc[...] + value

    cross_piece(0, True)
    arrived(whole(slab, peer_row, block_of(turn[1])), "slab", XP)
    half_rows = lw.at[pl.ds(aligned(peer_row + core * share, share), share), :]
    arrived(half_rows, "weights", XP)
    send(half_rows, half_rows, "weights", "weights on", SIB)
    cross_piece(1)
    arrived(whole(slab, peer_row, block_of(turn[2])), "slab y", YP)
    cross_piece(2)
    arrived(whole(slab, peer_row, block_of(turn[3])), "slab z", ZP)

    def last_piece(q):
        return cacc[rows_of(q), :] + lax.dot_general(
            t_v[rows_of(q), block_of(turn[3])], slab[:, block_of(turn[3])], (((1,), (1,)), ((), ())),
            preferred_element_type=f32,
        )

    for i in (2, 1, 0):
        cmsg_s[i] = last_piece(theirs[i]).astype(bf16)
        send(cmsg_s.at[i], cmsg_r.at[i], "cross", "cross", group[i])
    own_cross = last_piece(quarter)
    load_1.wait()
    load_2.wait()
    mom[0, z1] = m1_ref[...].astype(bf16)
    mom[1, z1] = m2_ref[...].astype(bf16)
    for i in (0, 1):
        here = mom.at[i, z1]
        send(here, here, "moment", "moment", ZF)

    arrived(dmsg_r, "diag", SIB)
    square_row = dmsg_r[0, 0:1, :] + dmsg_r[1, 0:1, :] + dmsg_r[2, 0:1, :]
    roots = target_chain((my_sq + to_col(square_row, part)) / pixels + bias_var)
    factors, rates = support_chain((s_row + dmsg_r[1, 8:9, :]) / pixels + bias_var)
    load_w.wait()
    arrived(lw.at[pl.ds(aligned(peer_row + (1 - core) * share, share), share), :], "weights on", SIB)

    arrived(cmsg_r, "cross", SIB)
    total = own_cross + cmsg_r[0].astype(f32)
    total = total + (cmsg_r[1].astype(f32) + cmsg_r[2].astype(f32))
    kernel, saved = forward(total / pixels + bias_var, roots, factors)
    weights = lw[...]
    predicted = jnp.dot(kernel.astype(bf16), weights, preferred_element_type=f32)
    classes = lax.broadcasted_iota(jnp.int32, predicted.shape, 1)
    onehot = (label_col == classes.astype(f32)).astype(f32)
    residual = (predicted - onehot).astype(bf16)
    kernel_grad = scale * lax.dot_general(
        residual, weights, (((1,), (1,)), ((), ())), preferred_element_type=f32
    )
    cross_grad, norm_grad = backward(kernel_grad, saved, factors, rates)
    mine_low = low.at[rows_of(quarter), :]
    mine_low[...] = cross_grad.astype(bf16)
    for i in (2, 1, 0):
        send(mine_low, mine_low, "low", "low", group[i])
    nmsg_s[...] = jnp.broadcast_to(norm_grad, nmsg_s.shape)
    for i in (2, 1, 0):
        send(nmsg_s, nmsg_r.at[i], "norm", "norm", group[i])
    arrived(low.at[0 : 3 * part, :], "low", SIB)
    arrived(nmsg_r, "norm", SIB)
    norm_row = norm_grad + nmsg_r[0, 0:1, :] + nmsg_r[1, 0:1, :] + nmsg_r[2, 0:1, :]
    norm_col = to_col(2.0 * norm_row, lanes)
    grads = low[...].astype(f32).T.astype(bf16)

    order = ((1, 1), (0, 1), (1, 0), (0, 0))
    first = slice(0, images)
    second = slice(images, 2 * images)

    def block_grad(k, h):
        dz, dy = order[k]
        number = (z0 + dz - 2 * dz * z0) * 2 + (yy + dy - 2 * dy * yy)
        where = pl.ds(aligned(number * width + h * piece, piece), piece)
        value = jnp.dot(grads, t_v[:, where], preferred_element_type=f32)
        return value + norm_col * slab[:, where].astype(f32)

    for h in chunks:
        straight = h in DIRECT
        value = block_grad(0, h)
        sy[0, h] = value[first].astype(bf16)
        send(sy.at[0, h], ry.at[0, h], "sum", ("sum", h) if straight else ("pair", h), DG if straight else YP)
        sz[0, h] = value[second].astype(bf16)
        send(sz.at[0, h], rz.at[0, h], "sum", ("sum", h) if straight else ("pair", h), DG if straight else ZP)
        value = block_grad(1, h)
        sy[1, h] = value[first].astype(bf16)
        send(sy.at[1, h], ry.at[1, h], "sum", ("sum", h), YP)
        if straight:
            s3[1, h] = value[second].astype(bf16)
            send(s3.at[1, h], r3.at[1, h], "sum", ("sum", h), YP)
        else:
            keep[0, h] = value[second]
        value = block_grad(2, h)
        sz[1, h] = value[second].astype(bf16)
        send(sz.at[1, h], rz.at[1, h], "sum", ("sum", h), ZP)
        if straight:
            s3[0, h] = value[first].astype(bf16)
            send(s3.at[0, h], r3.at[0, h], "sum", ("sum", h), ZP)
        else:
            keep[1, h] = value[first]
    for h in chunks:
        value = block_grad(3, h)
        keep[2, h] = value[first]
        keep[3, h] = value[second]

    def pieces(count):
        return sup_v.at[:, 0 : count * piece]

    def late(h):
        arrived(pieces(2), ("pair", h), YP)
        s3[0, h] = (keep[1, h] + ry[0, h].astype(f32)).astype(bf16)
        send(s3.at[0, h], r3.at[0, h], "sum", ("sum", h), ZP)
        s3[1, h] = (keep[0, h] + rz[0, h].astype(f32)).astype(bf16)
        send(s3.at[1, h], r3.at[1, h], "sum", ("sum", h), YP)

    def group_sum(h):
        arrived(pieces(6 if h in DIRECT else 4), ("sum", h), YP)
        one = (keep[2, h] + ry[1, h].astype(f32)) + r3[0, h].astype(f32)
        two = (keep[3, h] + rz[1, h].astype(f32)) + r3[1, h].astype(f32)
        if h in DIRECT:
            one = one + ry[0, h].astype(f32)
            two = two + rz[0, h].astype(f32)
        s4[0, h] = one.astype(bf16)
        s4[1, h] = two.astype(bf16)
        send(s4.at[x, h], r4.at[0, h], "sum", ("last z", h), ZF)
        send(s4.at[1 - x, h], r4.at[1, h], "sum", ("last", h), AN)
        send(s4.at[1 - x, h], r4.at[2, h], "sum", ("last", h), XP)

    for h in chunks:
        if h in DIRECT:
            group_sum(h)
    for h in chunks:
        if h not in DIRECT:
            late(h)
    for h in chunks:
        if h not in DIRECT:
            group_sum(h)

    arrived(mom.at[:, 1 - z1], "moment", ZF)

    def cut(index, h):
        return pl.ds(aligned(index * width + h * piece, piece), piece)

    def pass_on(index, name, device, h):
        here = out_ref.at[:, cut(index, h)]
        send(here, here, "gather", (name, h) if device is not SIB else "sibling", device)

    def came(index, name, device, h):
        arrived(out_ref.at[:, cut(index, h)], (name, h), device)

    def moved(first_in, second_in, gradient):
        new_first = first_decay * first_in + (1.0 - first_decay) * gradient
        new_second = second_decay * second_in + (1.0 - second_decay) * gradient * gradient
        return new_first, new_second

    slabs = (x, 1 - x)
    tgt_in = tgt - 8 * z1
    y_in, z_in, d_in = y_t - 8 * z1, z0_t - 8 * z1, y_t + z0_t - tgt - 8 * z1

    steps = [(h, i) for h in chunks for i in (0, 1)]
    straight_steps = [steps[n] for n in DIRECT_STEPS]

    def adam(h, i):
        here = slice(h * piece, (h + 1) * piece)
        side = slabs[i]
        if i == 0:
            arrived(r4.at[0, h], ("last z", h), ZF)
            gradient = (s4[x, h].astype(f32) + r4[0, h].astype(f32)) / pixels
        else:
            arrived(pieces(2), ("last", h), XP)
            gradient = (r4[1, h].astype(f32) + r4[2, h].astype(f32)) / pixels
        new_first, new_second = moved(mom[0, side, :, here].astype(f32), mom[1, side, :, here].astype(f32), gradient)
        update = learning_rate * (new_first / first_fix) / (jnp.sqrt(new_second / second_fix) + adam_eps)
        spot = tgt_in + 8 * side
        out_ref[:, cut(spot, h)] = (sup_v[:, cut(spot, h)].astype(f32) - update).astype(bf16)
        pass_on(spot, ("own z", i), ZP, h)
        pass_on(spot, ("own y", i), YP, h)
        if (h, i) in straight_steps:
            pass_on(spot, ("own d", i), DG, h)
        pass_on(spot, ("own s", i), SIB, h)

        @pl.when(side == z1)
        def _():
            new_first, new_second = moved(m1_ref[:, here], m2_ref[:, here], gradient)
            n1_ref[:, here] = new_first
            n2_ref[:, here] = new_second

    def relay(h, i):
        side = 8 * slabs[i]
        came(side + z_in, ("own z", i), ZP, h)
        if (h, i) not in straight_steps:
            pass_on(side + z_in, ("z y", i), YP, h)
        pass_on(side + z_in, ("z s", i), SIB, h)
        came(side + y_in, ("own y", i), YP, h)
        pass_on(side + y_in, ("y s", i), SIB, h)

    def finish(h, i):
        side = 8 * slabs[i]
        if (h, i) in straight_steps:
            came(side + d_in, ("own d", i), DG, h)
        else:
            came(side + d_in, ("z y", i), YP, h)
        pass_on(side + d_in, ("d s", i), SIB, h)

    for n in range(len(steps)):
        adam(*steps[n])
        if n >= 2:
            relay(*steps[n - 2])
    relay(*steps[-2])
    relay(*steps[-1])
    for step in steps:
        finish(*step)
    arrived(out_ref.at[:, 0 : 4 * len(steps) * piece], "sibling", SIB)
    all_sent(sup_v.at[:, 0 : 4 * width], "slab")
    all_sent(t_v.at[other_t, :], "targets")
    all_sent(lw.at[0:images, :], "weights")
    all_sent(dmsg_s, "diag")
    all_sent(cmsg_s, "cross")
    all_sent(low.at[0 : 3 * part, :], "low")
    all_sent(nmsg_r, "norm")
    all_sent(mom.at[:, 0], "moment")
    all_sent(pieces(counts["sum"]), "sum")
    all_sent(pieces(counts["gather"]), "gather")
    assert len(send_ids) <= SENDS and len(receive_ids) <= RECEIVES


def fused(targets, support, label_weights, labels, first_moment, second_moment):
    rows, _ = targets.shape
    images, pixels = support.shape
    width = first_moment.shape[1]
    classes = label_weights.shape[1]
    target_count = rows * lax.axis_size("tgt")
    support_count = images * lax.axis_size("sup")
    scale = 4.0 * pixels * math.sqrt(classes * support_count / target_count)
    everyone, part, piece = 2 * images, rows // 2, width // CHUNKS
    hbm = pl.BlockSpec(memory_space=pltpu.HBM)
    vmem = pl.BlockSpec(memory_space=pltpu.VMEM)
    slots = pltpu.VMEM((2, CHUNKS, images, piece), bf16)
    return pl.pallas_call(
        functools.partial(step_kernel, scale, pixels),
        out_shape=(
            pltpu.VMEM(support.shape, bf16),
            pltpu.VMEM(first_moment.shape, f32),
            pltpu.VMEM(first_moment.shape, f32),
        ),
        in_specs=[hbm] * 6,
        out_specs=(vmem, vmem, vmem),
        scratch_shapes=[
            pltpu.VMEM((2 * rows, 4 * width), bf16),
            pltpu.VMEM((everyone, 4 * width), bf16),
            pltpu.VMEM((images, pixels), bf16),
            pltpu.VMEM((everyone, classes), bf16),
            pltpu.VMEM((2 * rows, 128), f32),
            pltpu.VMEM((3, 16, everyone), f32),
            pltpu.VMEM((3, 16, everyone), f32),
            pltpu.VMEM((2 * rows, everyone), f32),
            pltpu.VMEM((3, part, everyone), bf16),
            pltpu.VMEM((3, part, everyone), bf16),
            pltpu.VMEM((2 * rows, everyone), bf16),
            pltpu.VMEM((8, everyone), f32),
            pltpu.VMEM((3, 8, everyone), f32),
            slots,
            slots,
            slots,
            slots,
            pltpu.VMEM((4, CHUNKS, images, piece), f32),
            slots,
            slots,
            slots,
            pltpu.VMEM((3, CHUNKS, images, piece), bf16),
            pltpu.VMEM((2, 2, images, width), bf16),
            pltpu.VMEM((1, rows), jnp.int32),
            pltpu.VMEM((images, width), f32),
            pltpu.VMEM((images, width), f32),
            pltpu.SemaphoreType.DMA((SENDS,)),
            pltpu.SemaphoreType.DMA((RECEIVES,)),
            pltpu.SemaphoreType.DMA((LOADS,)),
        ],
        compiler_params=pltpu.CompilerParams(
            collective_id=0, has_side_effects=True, vmem_limit_bytes=60000000
        ),
    )(targets, support, label_weights, labels[None, :], first_moment, second_moment)


def hand_over(a_ref, b_ref, c_ref, x_ref, y_ref, z_ref, sem):
    copies = [
        pltpu.make_async_copy(src, dst, sem.at[i])
        for i, (src, dst) in enumerate(((a_ref, x_ref), (b_ref, y_ref), (c_ref, z_ref)))
    ]
    for copy in copies:
        copy.start()
    for copy in copies:
        copy.wait()


def settle(support, first, second, space):
    return pl.pallas_call(
        hand_over,
        out_shape=tuple(jax.ShapeDtypeStruct(a.shape, a.dtype) for a in (support, first, second)),
        in_specs=[pl.BlockSpec(memory_space=space)] * 3,
        out_specs=(pl.BlockSpec(memory_space=pltpu.HBM),) * 3,
        scratch_shapes=[pltpu.SemaphoreType.DMA((3,))],
    )(support, first, second)


def pick(mesh):
    groups, shares = mesh.shape["sup"], mesh.shape["tgt"]

    def run(targets, support, label_weights, labels, first_moment, second_moment):
        width = first_moment.shape[1]
        fits = groups == 2 and shares == 16 and width % (128 * CHUNKS) == 0
        fits = fits and targets.shape[0] % 32 == 0 and groups * support.shape[0] == 128
        body = fused if fits else shards
        out = body(targets, support, label_weights, labels, first_moment, second_moment)
        return settle(*[pltpu.with_memory_space_constraint(o, pltpu.VMEM) for o in out], pltpu.VMEM) if fits else out

    return run


def solution(mesh):
    return jax.shard_map(
        pick(mesh),
        mesh=mesh,
        in_specs=(
            P("tgt", "sup"),
            P("sup", None),
            P("sup", None),
            P("tgt"),
            P("sup", "tgt"),
            P("sup", "tgt"),
        ),
        out_specs=(P("sup", None), P("sup", "tgt"), P("sup", "tgt")),
        check_vma=False,
    )
```

```python
import functools
import math

import jax
import jax.numpy as jnp
from jax import lax
from jax.experimental import pallas as pl
from jax.experimental.pallas import tpu as pltpu
from jax.sharding import PartitionSpec as P

DEPTH = 3


bias_var = 0.1
learning_rate = 0.05
first_decay = 0.9
second_decay = 0.99
first_fix = 1.0 - 0.9**10
second_fix = 1.0 - 0.99**10
adam_eps = 1e-08


def tangent_kernel(cross, target_diag, support_diag):
    tangent = cross
    current = cross
    left_diag = target_diag
    right_diag = support_diag
    for _ in range(DEPTH):
        product = (1.0 + 2.0 * left_diag)[:, None] * (1.0 + 2.0 * right_diag)[None, :]
        slope = 4.0 / math.pi / jnp.sqrt(product - 4.0 * current * current)
        current = 2.0 / math.pi * jnp.arcsin(2.0 * current / jnp.sqrt(product)) + bias_var
        tangent = current + slope * tangent
        left_diag = 2.0 / math.pi * jnp.arcsin(2.0 * left_diag / (1.0 + 2.0 * left_diag)) + bias_var
        right_diag = (
            2.0 / math.pi * jnp.arcsin(2.0 * right_diag / (1.0 + 2.0 * right_diag)) + bias_var
        )
    return tangent


def row_squares(images):
    return jnp.sum(jnp.square(images.astype(jnp.float32)), axis=1)


def shards(targets, support, label_weights, labels, first_moment, second_moment):
    pixels = support.shape[1]
    target_count = targets.shape[0] * lax.axis_size("tgt")
    support_count = support.shape[0] * lax.axis_size("sup")
    class_count = label_weights.shape[1]
    support_diag = row_squares(support) / pixels + bias_var
    slabs = lax.all_to_all(support, "sup", split_axis=1, concat_axis=0, tiled=True)
    partial_cross = lax.dot_general(
        targets, slabs, (((1,), (1,)), ((), ())), preferred_element_type=jnp.float32
    )
    cross = (
        lax.psum_scatter(
            partial_cross.astype(jnp.bfloat16), "sup", scatter_dimension=1, tiled=True
        ).astype(jnp.float32)
        / pixels
        + bias_var
    )
    target_diag = lax.psum(row_squares(targets), "sup") / pixels + bias_var

    def kernel_of(cross_in, diag_in):
        return tangent_kernel(cross_in, target_diag, diag_in)

    kernel, pullback = jax.vjp(kernel_of, cross, support_diag)
    partial_pred = jnp.dot(
        kernel.astype(jnp.bfloat16), label_weights, preferred_element_type=jnp.float32
    )
    predicted = lax.psum(partial_pred.astype(jnp.bfloat16), "sup").astype(jnp.float32)
    classes = jnp.arange(class_count, dtype=jnp.int32)
    onehot = (labels[:, None] == classes[None, :]).astype(jnp.float32)
    residual = (predicted - onehot).astype(jnp.bfloat16)
    kernel_grad = lax.dot_general(
        residual, label_weights, (((1,), (1,)), ((), ())), preferred_element_type=jnp.float32
    )
    kernel_grad = kernel_grad * (
        4.0 * pixels * math.sqrt(class_count * support_count / target_count)
    )
    cross_grad, norm_grad = pullback(kernel_grad)
    cross_low = cross_grad.astype(jnp.bfloat16)
    all_grads = lax.all_gather(cross_low, "sup", axis=1, tiled=True)
    slab_grad = lax.dot_general(
        all_grads, targets, (((0,), (0,)), ((), ())), preferred_element_type=jnp.float32
    )
    image_grad = lax.all_to_all(
        slab_grad.astype(jnp.bfloat16), "sup", split_axis=0, concat_axis=1, tiled=True
    ).astype(slab_grad.dtype)
    gradient = (image_grad + 2.0 * norm_grad[:, None] * support.astype(jnp.float32)) / pixels
    shares = lax.psum_scatter(gradient, "tgt", scatter_dimension=1, tiled=True)
    slab_width = shares.shape[1]
    own_pixels = lax.dynamic_slice_in_dim(
        support, lax.axis_index("tgt") * slab_width, slab_width, 1
    ).astype(jnp.float32)
    new_first = first_decay * first_moment + (1.0 - first_decay) * shares
    new_second = second_decay * second_moment + (1.0 - second_decay) * shares * shares
    update = (
        learning_rate * (new_first / first_fix) / (jnp.sqrt(new_second / second_fix) + adam_eps)
    )
    new_slab = (own_pixels - update).astype(jnp.bfloat16)
    new_support = lax.all_gather(new_slab, "tgt", axis=1, tiled=True)
    return (new_support, new_first, new_second)


MESH = pl.DeviceIdType.MESH
f32 = jnp.float32
bf16 = jnp.bfloat16


@jax.custom_jvp
def arcsine(x):
    a = jnp.abs(x)
    big = a > 0.5
    z = jnp.where(big, 0.5 * (1.0 - a), a * a)
    s = jnp.where(big, jnp.sqrt(z), a)
    p = 4.2163199048e-2 * z + 2.4181311049e-2
    p = p * z + 4.5470025998e-2
    p = p * z + 7.4953002686e-2
    p = p * z + 1.6666752422e-1
    p = p * z * s + s
    r = jnp.where(big, math.pi / 2.0 - 2.0 * p, p)
    return jnp.where(x < 0.0, -r, r)


@arcsine.defjvp
def arcsine_jvp(primals, tangents):
    (x,) = primals
    (t,) = tangents
    return arcsine(x), t * lax.rsqrt(1.0 - x * x)


def tangent_tile(cross, target_diag, support_diag):
    tangent = cross
    current = cross
    left = target_diag
    right = support_diag
    for _ in range(DEPTH):
        product = (1.0 + 2.0 * left) * (1.0 + 2.0 * right)
        slope = 4.0 / math.pi * lax.rsqrt(product - 4.0 * current * current)
        current = 2.0 / math.pi * arcsine(2.0 * current * lax.rsqrt(product)) + bias_var
        tangent = current + slope * tangent
        left = 2.0 / math.pi * arcsine(2.0 * left / (1.0 + 2.0 * left)) + bias_var
        right = 2.0 / math.pi * arcsine(2.0 * right / (1.0 + 2.0 * right)) + bias_var
    return tangent


def to_row(col, offset, lanes):
    shape = (col.shape[0], lanes)
    hit = lax.broadcasted_iota(jnp.int32, shape, 1) == lax.broadcasted_iota(jnp.int32, shape, 0) + offset
    return jnp.sum(jnp.where(hit, col, 0.0), axis=0, keepdims=True)


def to_col(row, count, offset=0):
    shape = (count, row.shape[1])
    hit = lax.broadcasted_iota(jnp.int32, shape, 1) == lax.broadcasted_iota(jnp.int32, shape, 0) + offset
    return jnp.sum(jnp.where(hit, row, 0.0), axis=1, keepdims=True)


SENDS, RECEIVES, LOADS = 10, 45, 7
CUTS = (2, 2, 2)
STRIPS = 2
DIRECT = (0,)
DIRECT_STEPS = (4, 5)


def support_chain(diag):
    factors, rates = [], []
    right = diag
    for _ in range(DEPTH):
        plus = 1.0 + 2.0 * right
        factors.append(plus)
        rates.append(4.0 / math.pi / (plus * jnp.sqrt(1.0 + 4.0 * right)))
        right = 2.0 / math.pi * arcsine(2.0 * right / plus) + bias_var
    return factors, rates


def target_chain(diag):
    roots = []
    left = diag
    for _ in range(DEPTH):
        plus = 1.0 + 2.0 * left
        roots.append(lax.rsqrt(plus))
        left = 2.0 / math.pi * arcsine(2.0 * left / plus) + bias_var
    return roots


def forward(cross, roots, factors):
    tangent, current = cross, cross
    saved = []
    for root, plus in zip(roots, factors):
        twice = root * (2.0 * lax.rsqrt(plus))
        sine = current * twice
        inverse = lax.rsqrt(1.0 - sine * sine)
        slope = 2.0 / math.pi * twice * inverse
        saved.append((twice, sine, inverse, slope, tangent))
        current = 2.0 / math.pi * arcsine(sine) + bias_var
        tangent = current + slope * tangent
    return tangent, saved


def backward(grad, saved, factors, rates):
    tangent_bar, current_bar = grad, jnp.zeros_like(grad)
    diag_bar = None
    for layer in reversed(range(DEPTH)):
        twice, sine, inverse, slope, tangent = saved[layer]
        total = current_bar + tangent_bar
        next_bar = tangent_bar * slope
        carried = next_bar * tangent * inverse * inverse
        direct = -jnp.sum(carried + 2.0 / math.pi * total * inverse * sine, axis=0, keepdims=True) / factors[layer]
        diag_bar = direct if diag_bar is None else direct + diag_bar * rates[layer]
        current_bar = total * slope + twice * sine * carried
        tangent_bar = next_bar
    return current_bar + tangent_bar, diag_bar


def step_kernel(
    scale, pixels,
    t_hbm, s_hbm, w_hbm, labels_hbm, m1_hbm, m2_hbm,
    out_ref, n1_ref, n2_ref,
    t_v, slab, sup_v, lw, tacc, dmsg_s, dmsg_r, cacc, cmsg_s, cmsg_r, low, nmsg_s, nmsg_r,
    sy, sz, ry, rz, keep, s3, r3, s4, r4, ds, dr, mom, labels_ref, m1_ref, m2_ref,
    send_sem, recv_sem, local_sem,
):
    tgt = lax.axis_index("tgt")
    x = lax.axis_index("sup")
    core = lax.rem(tgt, 2)
    yy = lax.rem(tgt // 2, 2)
    z0 = lax.rem(tgt // 4, 2)
    z1 = tgt // 8
    sib_t = tgt + 1 - 2 * core
    y_t = tgt + 2 - 4 * yy
    z0_t = tgt + 4 - 8 * z0
    z1_t = tgt + 8 - 16 * z1
    SIB, YP, ZP, ZF = (sib_t, x), (y_t, x), (z0_t, x), (z1_t, x)
    XP, XS, AN = (tgt, 1 - x), (sib_t, 1 - x), (z1_t, 1 - x)
    DG = (y_t + z0_t - tgt, x)

    images, width = n1_ref.shape
    rows = t_v.shape[0] // 2
    half = 8 * width
    part = rows // 2
    lanes = slab.shape[0]
    sizes = [128 * n for n in CUTS]
    starts = [sum(sizes[:h]) for h in range(len(sizes))]
    chunks = range(len(sizes))

    send_ids, receive_ids, counts = {}, {}, {}

    def remote(src, dst, sent, name, device):
        return pltpu.make_async_remote_copy(
            src_ref=src, dst_ref=dst, send_sem=send_sem.at[send_ids.setdefault(sent, len(send_ids))],
            recv_sem=recv_sem.at[receive_ids.setdefault(name, len(receive_ids))],
            device_id=device, device_id_type=MESH,
        )

    def send(src, dst, sent, name, device):
        counts[sent] = counts.get(sent, 0) + src.shape[0] * src.shape[-1] // images
        remote(src, dst, sent, name, device).start()

    def arrived(dst, name, device):
        pltpu.make_async_remote_copy(
            src_ref=dst, dst_ref=dst, send_sem=send_sem.at[0],
            recv_sem=recv_sem.at[receive_ids.setdefault(name, len(receive_ids))],
            device_id=device, device_id_type=MESH,
        ).wait_recv()

    def all_sent(src, sent):
        pltpu.make_async_remote_copy(
            src_ref=src, dst_ref=src, send_sem=send_sem.at[send_ids[sent]], recv_sem=recv_sem.at[0],
            device_id=SIB, device_id_type=MESH,
        ).wait_send()

    def aligned(value, by):
        return pl.multiple_of(value, by)

    barrier = pltpu.get_barrier_semaphore()
    friends = (XP, XS, SIB, YP, ZP, DG, ZF, AN)
    for device in friends:
        pl.semaphore_signal(barrier, inc=1, device_id=device, device_id_type=MESH)

    def load(src, dst, number):
        copy = pltpu.make_async_copy(src, dst, local_sem.at[number])
        copy.start()
        return copy

    my_row = aligned(x * images, images)
    peer_row = aligned((1 - x) * images, images)

    def columns(block, owner):
        return pl.ds(aligned((2 * block + owner) * width, width), width)

    def far_columns(slab_index, block):
        return pl.ds(aligned(slab_index * half + (2 * block + core) * width, width), width)

    def block_of(j):
        return pl.ds(aligned(j * width, width), width)

    load_s = load(s_hbm, sup_v, 0)
    mine_t = pl.ds(aligned(core * rows, rows), rows)
    for j in range(4):
        load(t_hbm.at[:, columns(j, core)], t_v.at[mine_t, block_of(j)], 1)
    load_t = pltpu.make_async_copy(t_v.at[mine_t, :], t_v.at[mine_t, :], local_sem.at[1])
    for j in range(4):
        load(s_hbm.at[:, far_columns(x, j)], slab.at[pl.ds(my_row, images), block_of(j)], 2)
    my_slab = slab.at[pl.ds(my_row, images), :]
    load_o = pltpu.make_async_copy(my_slab, my_slab, local_sem.at[2])
    load_w = load(w_hbm, lw.at[pl.ds(my_row, images), :], 3)
    load_l = load(labels_hbm, labels_ref, 4)
    load_1 = load(m1_hbm, m1_ref, 5)
    load_2 = load(m2_hbm, m2_ref, 6)

    pl.semaphore_wait(barrier, len(friends))

    seat = 2 * yy + z0
    turn = (seat, 3 - seat, seat + 2 - 4 * yy, seat + 1 - 2 * z0)
    strip = images // STRIPS
    strips = range(STRIPS)
    share = images // 2

    def send_strip(p, r):
        send(
            s_hbm.at[pl.ds(r * strip, strip), far_columns(1 - x, turn[p])],
            slab.at[pl.ds(aligned(my_row + r * strip, strip), strip), block_of(turn[p])],
            "slab", ("slab", p, r), XP,
        )

    for r in strips:
        send_strip(0, r)

    def whole(ref, row, columns):
        return ref.at[pl.ds(row, images), columns]

    send(
        s_hbm.at[:, far_columns(1 - x, turn[1])], whole(slab, my_row, block_of(turn[1])), "slab", "slab", XP,
    )
    for j in range(4):
        send(t_hbm.at[:, columns(j, 1 - core)], t_v.at[mine_t, block_of(j)], "targets", "targets", SIB)
    load_1.wait()
    mom[0, z1] = m1_ref[...].astype(bf16)
    here = mom.at[0, z1]
    send(here, here, "moment", "moment", ZF)

    load_s.wait()

    def support_squares(i, acc):
        block = sup_v[:, pl.ds(aligned(i * width, width), width)].astype(f32)
        block = block * block
        for k in range(width // 128):
            acc = acc + block[:, k * 128 : (k + 1) * 128]
        return acc

    sacc = lax.fori_loop(0, pixels // width, support_squares, jnp.zeros((images, 128), f32))
    s_row = to_row(jnp.sum(sacc, axis=1, keepdims=True), x * images, lanes)

    def target_squares(first):
        def body(i, carry):
            where = pl.ds(aligned(first + i * 16, 16), 16)
            sums = []
            for j in range(4):
                block = t_v[where, j * width : (j + 1) * width].astype(f32)
                block = block * block
                acc = block[:, 0:128]
                for k in range(1, width // 128):
                    acc = acc + block[:, k * 128 : (k + 1) * 128]
                sums.append(acc)
            tacc[where, :] = (sums[0] + sums[1]) + (sums[2] + sums[3])
            return carry

        lax.fori_loop(0, rows // 16, body, 0)

    load_t.wait()
    target_squares(core * rows)

    def strip_of(p, r):
        return slab.at[pl.ds(aligned(peer_row + r * strip, strip), strip), block_of(turn[p])]

    for r in strips:
        here = strip_of(0, r)
        arrived(here, ("slab", 0, r), XP)
        send(here, here, "slab", "slab y", YP)
        send(here, here, "slab", "slab z", ZP)

    weight_rows = pl.ds(aligned(my_row + core * share, share), share)
    send(w_hbm.at[pl.ds(aligned(core * share, share), share), :], lw.at[weight_rows, :], "weights", "weights", XP)

    other_t = pl.ds(aligned((1 - core) * rows, rows), rows)
    arrived(t_v.at[other_t, :], "targets", SIB)
    target_squares((1 - core) * rows)

    group = (SIB, XP, XS)
    quarter = 2 * core + x
    theirs = (2 * (1 - core) + x, 2 * core + 1 - x, 2 * (1 - core) + 1 - x)

    def rows_of(q):
        return pl.ds(aligned(q * part, part), part)

    def square_col(q):
        return jnp.sum(tacc[rows_of(q), :], axis=1, keepdims=True)

    for i in range(3):
        dmsg_s[i, 0:8, :] = jnp.broadcast_to(to_row(square_col(theirs[i]), 0, lanes), (8, lanes))
        dmsg_s[i, 8:16, :] = jnp.broadcast_to(s_row, (8, lanes))
        send(dmsg_s.at[i], dmsg_r.at[i], "diag", "diag", group[i])
    my_sq = square_col(quarter)
    load_l.wait()
    label_col = to_col(labels_ref[...].astype(f32), part, x * part)

    load_o.wait()

    def cross_piece(p, first=False):
        value = lax.dot_general(
            t_v[:, block_of(turn[p])], slab[:, block_of(turn[p])], (((1,), (1,)), ((), ())),
            preferred_element_type=f32,
        )
        cacc[...] = value if first else cacc[...] + value

    cross_piece(0, True)
    arrived(whole(slab, peer_row, block_of(turn[1])), "slab", XP)
    cross_piece(1)
    arrived(whole(slab, peer_row, block_of(turn[2])), "slab y", YP)
    cross_piece(2)
    arrived(whole(slab, peer_row, block_of(turn[3])), "slab z", ZP)

    def last_piece(q):
        return cacc[rows_of(q), :] + lax.dot_general(
            t_v[rows_of(q), block_of(turn[3])], slab[:, block_of(turn[3])], (((1,), (1,)), ((), ())),
            preferred_element_type=f32,
        )

    for i in (2, 1, 0):
        cmsg_s[i] = last_piece(theirs[i]).astype(bf16)
        send(cmsg_s.at[i], cmsg_r.at[i], "cross", "cross", group[i])
    own_cross = last_piece(quarter)
    half_rows = lw.at[pl.ds(aligned(peer_row + core * share, share), share), :]
    arrived(half_rows, "weights", XP)
    send(half_rows, half_rows, "weights", "weights on", SIB)
    load_2.wait()
    mom[1, z1] = m2_ref[...].astype(bf16)
    here = mom.at[1, z1]
    send(here, here, "moment", "moment", ZF)

    arrived(dmsg_r, "diag", SIB)
    square_row = dmsg_r[0, 0:1, :] + dmsg_r[1, 0:1, :] + dmsg_r[2, 0:1, :]
    roots = target_chain((my_sq + to_col(square_row, part)) / pixels + bias_var)
    factors, rates = support_chain((s_row + dmsg_r[1, 8:9, :]) / pixels + bias_var)
    load_w.wait()
    arrived(lw.at[pl.ds(aligned(peer_row + (1 - core) * share, share), share), :], "weights on", SIB)

    arrived(cmsg_r, "cross", SIB)
    total = own_cross + cmsg_r[0].astype(f32)
    total = total + (cmsg_r[1].astype(f32) + cmsg_r[2].astype(f32))
    kernel, saved = forward(total / pixels + bias_var, roots, factors)
    weights = lw[...]
    predicted = jnp.dot(kernel.astype(bf16), weights, preferred_element_type=f32)
    classes = lax.broadcasted_iota(jnp.int32, predicted.shape, 1)
    onehot = (label_col == classes.astype(f32)).astype(f32)
    residual = (predicted - onehot).astype(bf16)
    kernel_grad = scale * lax.dot_general(
        residual, weights, (((1,), (1,)), ((), ())), preferred_element_type=f32
    )
    cross_grad, norm_grad = backward(kernel_grad, saved, factors, rates)
    mine_low = low.at[rows_of(quarter), :]
    mine_low[...] = cross_grad.astype(bf16)
    for i in (2, 1, 0):
        send(mine_low, mine_low, "low", "low", group[i])
    nmsg_s[...] = jnp.broadcast_to(norm_grad, nmsg_s.shape)
    for i in (2, 1, 0):
        send(nmsg_s, nmsg_r.at[i], "norm", "norm", group[i])
    arrived(low.at[0 : 3 * part, :], "low", SIB)
    arrived(nmsg_r, "norm", SIB)
    norm_row = norm_grad + nmsg_r[0, 0:1, :] + nmsg_r[1, 0:1, :] + nmsg_r[2, 0:1, :]
    norm_col = to_col(2.0 * norm_row, lanes)
    grads = low[...].astype(f32).T.astype(bf16)

    order = ((1, 1), (0, 1), (1, 0), (0, 0))
    first = slice(0, images)
    second = slice(images, 2 * images)

    def at(k, h):
        return (k, slice(None), slice(starts[h], starts[h] + sizes[h]))

    def block_grad(k, h):
        dz, dy = order[k]
        number = (z0 + dz - 2 * dz * z0) * 2 + (yy + dy - 2 * dy * yy)
        where = pl.ds(aligned(number * width + starts[h], 128), sizes[h])
        value = jnp.dot(grads, t_v[:, where], preferred_element_type=f32)
        return value + norm_col * slab[:, where].astype(f32)

    for h in chunks:
        if h in DIRECT:
            for k, device in enumerate((DG, YP, ZP)):
                here = at(k, h)
                ds[here] = block_grad(k, h).astype(bf16)
                send(ds.at[here], dr.at[here], "sum", ("sum", h), device)
            continue
        value = block_grad(0, h)
        sy[at(0, h)] = value[first].astype(bf16)
        send(sy.at[at(0, h)], ry.at[at(0, h)], "sum", ("pair", h), YP)
        sz[at(0, h)] = value[second].astype(bf16)
        send(sz.at[at(0, h)], rz.at[at(0, h)], "sum", ("pair", h), ZP)
        value = block_grad(1, h)
        sy[at(1, h)] = value[first].astype(bf16)
        send(sy.at[at(1, h)], ry.at[at(1, h)], "sum", ("sum", h), YP)
        keep[at(0, h)] = value[second]
        value = block_grad(2, h)
        sz[at(1, h)] = value[second].astype(bf16)
        send(sz.at[at(1, h)], rz.at[at(1, h)], "sum", ("sum", h), ZP)
        keep[at(1, h)] = value[first]
    for h in chunks:
        value = block_grad(3, h)
        keep[at(2, h)] = value[first]
        keep[at(3, h)] = value[second]

    def pieces(count):
        return sup_v.at[:, 0:count]

    def late(h):
        arrived(pieces(2 * sizes[h]), ("pair", h), YP)
        s3[at(0, h)] = (keep[at(1, h)] + ry[at(0, h)].astype(f32)).astype(bf16)
        send(s3.at[at(0, h)], r3.at[at(0, h)], "sum", ("sum", h), ZP)
        s3[at(1, h)] = (keep[at(0, h)] + rz[at(0, h)].astype(f32)).astype(bf16)
        send(s3.at[at(1, h)], r3.at[at(1, h)], "sum", ("sum", h), YP)

    def group_sum(h):
        arrived(pieces((6 if h in DIRECT else 4) * sizes[h]), ("sum", h), YP)
        if h in DIRECT:
            extra = dr[at(0, h)].astype(f32) + dr[at(1, h)].astype(f32) + dr[at(2, h)].astype(f32)
            one = keep[at(2, h)] + extra[first]
            two = keep[at(3, h)] + extra[second]
        else:
            one = (keep[at(2, h)] + ry[at(1, h)].astype(f32)) + r3[at(0, h)].astype(f32)
            two = (keep[at(3, h)] + rz[at(1, h)].astype(f32)) + r3[at(1, h)].astype(f32)
        s4[at(0, h)] = one.astype(bf16)
        s4[at(1, h)] = two.astype(bf16)
        send(s4.at[at(x, h)], r4.at[at(0, h)], "sum", ("last z", h), ZF)
        send(s4.at[at(1 - x, h)], r4.at[at(2, h)], "sum", ("last", h), XP)
        send(s4.at[at(1 - x, h)], r4.at[at(1, h)], "sum", ("last", h), AN)

    for h in chunks:
        if h in DIRECT:
            group_sum(h)
    for h in chunks:
        if h not in DIRECT:
            late(h)
    for h in chunks:
        if h not in DIRECT:
            group_sum(h)

    arrived(mom.at[:, 1 - z1], "moment", ZF)

    def cut(index, h):
        return pl.ds(aligned(index * width + starts[h], 128), sizes[h])

    def pass_on(index, name, device, h):
        here = out_ref.at[:, cut(index, h)]
        send(here, here, "gather", (name, h) if device is not SIB else "sibling", device)

    def came(index, name, device, h):
        arrived(out_ref.at[:, cut(index, h)], (name, h), device)

    def moved(first_in, second_in, gradient):
        new_first = first_decay * first_in + (1.0 - first_decay) * gradient
        new_second = second_decay * second_in + (1.0 - second_decay) * gradient * gradient
        return new_first, new_second

    slabs = (x, 1 - x)
    tgt_in = tgt - 8 * z1
    y_in, z_in, d_in = y_t - 8 * z1, z0_t - 8 * z1, y_t + z0_t - tgt - 8 * z1

    steps = [(h, i) for h in chunks for i in (0, 1)]
    straight_steps = [steps[n] for n in DIRECT_STEPS]

    def adam(h, i):
        here = slice(starts[h], starts[h] + sizes[h])
        side = slabs[i]
        if i == 0:
            arrived(r4.at[at(0, h)], ("last z", h), ZF)
            gradient = (s4[at(x, h)].astype(f32) + r4[at(0, h)].astype(f32)) / pixels
        else:
            arrived(pieces(2 * sizes[h]), ("last", h), XP)
            gradient = (r4[at(1, h)].astype(f32) + r4[at(2, h)].astype(f32)) / pixels
        new_first, new_second = moved(mom[0, side, :, here].astype(f32), mom[1, side, :, here].astype(f32), gradient)
        update = learning_rate * (new_first / first_fix) / (jnp.sqrt(new_second / second_fix) + adam_eps)
        spot = tgt_in + 8 * side
        out_ref[:, cut(spot, h)] = (sup_v[:, cut(spot, h)].astype(f32) - update).astype(bf16)
        if (h, i) in straight_steps:
            pass_on(spot, ("own d", i), DG, h)
        pass_on(spot, ("own z", i), ZP, h)
        pass_on(spot, ("own y", i), YP, h)
        pass_on(spot, ("own s", i), SIB, h)

        @pl.when(side == z1)
        def _():
            new_first, new_second = moved(m1_ref[:, here], m2_ref[:, here], gradient)
            n1_ref[:, here] = new_first
            n2_ref[:, here] = new_second

    def relay(h, i):
        side = 8 * slabs[i]
        came(side + z_in, ("own z", i), ZP, h)
        if (h, i) not in straight_steps:
            pass_on(side + z_in, ("z y", i), YP, h)
        pass_on(side + z_in, ("z s", i), SIB, h)
        came(side + y_in, ("own y", i), YP, h)
        pass_on(side + y_in, ("y s", i), SIB, h)

    def finish(h, i):
        side = 8 * slabs[i]
        if (h, i) in straight_steps:
            came(side + d_in, ("own d", i), DG, h)
        else:
            came(side + d_in, ("z y", i), YP, h)
        pass_on(side + d_in, ("d s", i), SIB, h)

    for n in range(len(steps)):
        adam(*steps[n])
        if n >= 3:
            relay(*steps[n - 3])
    relay(*steps[-3])
    relay(*steps[-2])
    relay(*steps[-1])
    for step in steps:
        finish(*step)
    arrived(out_ref.at[:, 0 : 8 * width], "sibling", SIB)
    all_sent(sup_v.at[:, 0 : 4 * width], "slab")
    all_sent(t_v.at[other_t, :], "targets")
    all_sent(lw.at[0:images, :], "weights")
    all_sent(dmsg_s, "diag")
    all_sent(cmsg_s, "cross")
    all_sent(low.at[0 : 3 * part, :], "low")
    all_sent(nmsg_r, "norm")
    all_sent(mom.at[:, 0], "moment")
    all_sent(pieces(counts["sum"]), "sum")
    all_sent(pieces(counts["gather"]), "gather")
    assert len(send_ids) <= SENDS and len(receive_ids) <= RECEIVES


def fused(targets, support, label_weights, labels, first_moment, second_moment):
    rows, _ = targets.shape
    images, pixels = support.shape
    width = first_moment.shape[1]
    classes = label_weights.shape[1]
    target_count = rows * lax.axis_size("tgt")
    support_count = images * lax.axis_size("sup")
    scale = 4.0 * pixels * math.sqrt(classes * support_count / target_count)
    everyone, part = 2 * images, rows // 2
    hbm = pl.BlockSpec(memory_space=pltpu.HBM)
    vmem = pl.BlockSpec(memory_space=pltpu.VMEM)
    slots = pltpu.VMEM((2, images, width), bf16)
    return pl.pallas_call(
        functools.partial(step_kernel, scale, pixels),
        out_shape=(
            pltpu.VMEM(support.shape, bf16),
            pltpu.VMEM(first_moment.shape, f32),
            pltpu.VMEM(first_moment.shape, f32),
        ),
        in_specs=[hbm] * 6,
        out_specs=(vmem, vmem, vmem),
        scratch_shapes=[
            pltpu.VMEM((2 * rows, 4 * width), bf16),
            pltpu.VMEM((everyone, 4 * width), bf16),
            pltpu.VMEM((images, pixels), bf16),
            pltpu.VMEM((everyone, classes), bf16),
            pltpu.VMEM((2 * rows, 128), f32),
            pltpu.VMEM((3, 16, everyone), f32),
            pltpu.VMEM((3, 16, everyone), f32),
            pltpu.VMEM((2 * rows, everyone), f32),
            pltpu.VMEM((3, part, everyone), bf16),
            pltpu.VMEM((3, part, everyone), bf16),
            pltpu.VMEM((2 * rows, everyone), bf16),
            pltpu.VMEM((8, everyone), f32),
            pltpu.VMEM((3, 8, everyone), f32),
            slots,
            slots,
            slots,
            slots,
            pltpu.VMEM((4, images, width), f32),
            slots,
            slots,
            slots,
            pltpu.VMEM((3, images, width), bf16),
            pltpu.VMEM((3, everyone, width), bf16),
            pltpu.VMEM((3, everyone, width), bf16),
            pltpu.VMEM((2, 2, images, width), bf16),
            pltpu.VMEM((1, rows), jnp.int32),
            pltpu.VMEM((images, width), f32),
            pltpu.VMEM((images, width), f32),
            pltpu.SemaphoreType.DMA((SENDS,)),
            pltpu.SemaphoreType.DMA((RECEIVES,)),
            pltpu.SemaphoreType.DMA((LOADS,)),
        ],
        compiler_params=pltpu.CompilerParams(
            collective_id=0, has_side_effects=True, vmem_limit_bytes=60000000
        ),
    )(targets, support, label_weights, labels[None, :], first_moment, second_moment)


def hand_over(a_ref, b_ref, c_ref, x_ref, y_ref, z_ref, sem):
    copies = [
        pltpu.make_async_copy(src, dst, sem.at[i])
        for i, (src, dst) in enumerate(((a_ref, x_ref), (b_ref, y_ref), (c_ref, z_ref)))
    ]
    for copy in copies:
        copy.start()
    for copy in copies:
        copy.wait()


def settle(support, first, second, space):
    return pl.pallas_call(
        hand_over,
        out_shape=tuple(jax.ShapeDtypeStruct(a.shape, a.dtype) for a in (support, first, second)),
        in_specs=[pl.BlockSpec(memory_space=space)] * 3,
        out_specs=(pl.BlockSpec(memory_space=pltpu.HBM),) * 3,
        scratch_shapes=[pltpu.SemaphoreType.DMA((3,))],
    )(support, first, second)


def pick(mesh):
    groups, shares = mesh.shape["sup"], mesh.shape["tgt"]

    def run(targets, support, label_weights, labels, first_moment, second_moment):
        width = first_moment.shape[1]
        fits = groups == 2 and shares == 16 and width == 128 * sum(CUTS)
        fits = fits and targets.shape[0] % 32 == 0 and groups * support.shape[0] == 128
        body = fused if fits else shards
        out = body(targets, support, label_weights, labels, first_moment, second_moment)
        return settle(*[pltpu.with_memory_space_constraint(o, pltpu.VMEM) for o in out], pltpu.VMEM) if fits else out

    return run


def solution(mesh):
    return jax.shard_map(
        pick(mesh),
        mesh=mesh,
        in_specs=(
            P("tgt", "sup"),
            P("sup", None),
            P("sup", None),
            P("tgt"),
            P("sup", "tgt"),
            P("sup", "tgt"),
        ),
        out_specs=(P("sup", None), P("sup", "tgt"), P("sup", "tgt")),
        check_vma=False,
    )
```

```python
import functools
import math

import jax
import jax.numpy as jnp
from jax import lax
from jax.experimental import pallas as pl
from jax.experimental.pallas import tpu as pltpu
from jax.sharding import PartitionSpec as P

DEPTH = 3


bias_var = 0.1
learning_rate = 0.05
first_decay = 0.9
second_decay = 0.99
first_fix = 1.0 - 0.9**10
second_fix = 1.0 - 0.99**10
adam_eps = 1e-08


def tangent_kernel(cross, target_diag, support_diag):
    tangent = cross
    current = cross
    left_diag = target_diag
    right_diag = support_diag
    for _ in range(DEPTH):
        product = (1.0 + 2.0 * left_diag)[:, None] * (1.0 + 2.0 * right_diag)[None, :]
        slope = 4.0 / math.pi / jnp.sqrt(product - 4.0 * current * current)
        current = 2.0 / math.pi * jnp.arcsin(2.0 * current / jnp.sqrt(product)) + bias_var
        tangent = current + slope * tangent
        left_diag = 2.0 / math.pi * jnp.arcsin(2.0 * left_diag / (1.0 + 2.0 * left_diag)) + bias_var
        right_diag = (
            2.0 / math.pi * jnp.arcsin(2.0 * right_diag / (1.0 + 2.0 * right_diag)) + bias_var
        )
    return tangent


def row_squares(images):
    return jnp.sum(jnp.square(images.astype(jnp.float32)), axis=1)


def shards(targets, support, label_weights, labels, first_moment, second_moment):
    pixels = support.shape[1]
    target_count = targets.shape[0] * lax.axis_size("tgt")
    support_count = support.shape[0] * lax.axis_size("sup")
    class_count = label_weights.shape[1]
    support_diag = row_squares(support) / pixels + bias_var
    slabs = lax.all_to_all(support, "sup", split_axis=1, concat_axis=0, tiled=True)
    partial_cross = lax.dot_general(
        targets, slabs, (((1,), (1,)), ((), ())), preferred_element_type=jnp.float32
    )
    cross = (
        lax.psum_scatter(
            partial_cross.astype(jnp.bfloat16), "sup", scatter_dimension=1, tiled=True
        ).astype(jnp.float32)
        / pixels
        + bias_var
    )
    target_diag = lax.psum(row_squares(targets), "sup") / pixels + bias_var

    def kernel_of(cross_in, diag_in):
        return tangent_kernel(cross_in, target_diag, diag_in)

    kernel, pullback = jax.vjp(kernel_of, cross, support_diag)
    partial_pred = jnp.dot(
        kernel.astype(jnp.bfloat16), label_weights, preferred_element_type=jnp.float32
    )
    predicted = lax.psum(partial_pred.astype(jnp.bfloat16), "sup").astype(jnp.float32)
    classes = jnp.arange(class_count, dtype=jnp.int32)
    onehot = (labels[:, None] == classes[None, :]).astype(jnp.float32)
    residual = (predicted - onehot).astype(jnp.bfloat16)
    kernel_grad = lax.dot_general(
        residual, label_weights, (((1,), (1,)), ((), ())), preferred_element_type=jnp.float32
    )
    kernel_grad = kernel_grad * (
        4.0 * pixels * math.sqrt(class_count * support_count / target_count)
    )
    cross_grad, norm_grad = pullback(kernel_grad)
    cross_low = cross_grad.astype(jnp.bfloat16)
    all_grads = lax.all_gather(cross_low, "sup", axis=1, tiled=True)
    slab_grad = lax.dot_general(
        all_grads, targets, (((0,), (0,)), ((), ())), preferred_element_type=jnp.float32
    )
    image_grad = lax.all_to_all(
        slab_grad.astype(jnp.bfloat16), "sup", split_axis=0, concat_axis=1, tiled=True
    ).astype(slab_grad.dtype)
    gradient = (image_grad + 2.0 * norm_grad[:, None] * support.astype(jnp.float32)) / pixels
    shares = lax.psum_scatter(gradient, "tgt", scatter_dimension=1, tiled=True)
    slab_width = shares.shape[1]
    own_pixels = lax.dynamic_slice_in_dim(
        support, lax.axis_index("tgt") * slab_width, slab_width, 1
    ).astype(jnp.float32)
    new_first = first_decay * first_moment + (1.0 - first_decay) * shares
    new_second = second_decay * second_moment + (1.0 - second_decay) * shares * shares
    update = (
        learning_rate * (new_first / first_fix) / (jnp.sqrt(new_second / second_fix) + adam_eps)
    )
    new_slab = (own_pixels - update).astype(jnp.bfloat16)
    new_support = lax.all_gather(new_slab, "tgt", axis=1, tiled=True)
    return (new_support, new_first, new_second)


MESH = pl.DeviceIdType.MESH
f32 = jnp.float32
bf16 = jnp.bfloat16


@jax.custom_jvp
def arcsine(x):
    a = jnp.abs(x)
    big = a > 0.5
    z = jnp.where(big, 0.5 * (1.0 - a), a * a)
    s = jnp.where(big, jnp.sqrt(z), a)
    p = 4.2163199048e-2 * z + 2.4181311049e-2
    p = p * z + 4.5470025998e-2
    p = p * z + 7.4953002686e-2
    p = p * z + 1.6666752422e-1
    p = p * z * s + s
    r = jnp.where(big, math.pi / 2.0 - 2.0 * p, p)
    return jnp.where(x < 0.0, -r, r)


@arcsine.defjvp
def arcsine_jvp(primals, tangents):
    (x,) = primals
    (t,) = tangents
    return arcsine(x), t * lax.rsqrt(1.0 - x * x)


def tangent_tile(cross, target_diag, support_diag):
    tangent = cross
    current = cross
    left = target_diag
    right = support_diag
    for _ in range(DEPTH):
        product = (1.0 + 2.0 * left) * (1.0 + 2.0 * right)
        slope = 4.0 / math.pi * lax.rsqrt(product - 4.0 * current * current)
        current = 2.0 / math.pi * arcsine(2.0 * current * lax.rsqrt(product)) + bias_var
        tangent = current + slope * tangent
        left = 2.0 / math.pi * arcsine(2.0 * left / (1.0 + 2.0 * left)) + bias_var
        right = 2.0 / math.pi * arcsine(2.0 * right / (1.0 + 2.0 * right)) + bias_var
    return tangent


def to_row(col, offset, lanes):
    shape = (col.shape[0], lanes)
    hit = lax.broadcasted_iota(jnp.int32, shape, 1) == lax.broadcasted_iota(jnp.int32, shape, 0) + offset
    return jnp.sum(jnp.where(hit, col, 0.0), axis=0, keepdims=True)


def to_col(row, count, offset=0):
    shape = (count, row.shape[1])
    hit = lax.broadcasted_iota(jnp.int32, shape, 1) == lax.broadcasted_iota(jnp.int32, shape, 0) + offset
    return jnp.sum(jnp.where(hit, row, 0.0), axis=1, keepdims=True)


SENDS, RECEIVES, LOADS = 10, 43, 7
CUTS = (2, 2, 2)
STRIPS = 2
DIRECT = (0,)
DIRECT_STEPS = (3, 4, 5)
LAG = 4
TURNED = ()


def support_chain(diag):
    factors, rates = [], []
    right = diag
    for _ in range(DEPTH):
        plus = 1.0 + 2.0 * right
        factors.append(plus)
        rates.append(4.0 / math.pi / (plus * jnp.sqrt(1.0 + 4.0 * right)))
        right = 2.0 / math.pi * arcsine(2.0 * right / plus) + bias_var
    return factors, rates


def target_chain(diag):
    roots = []
    left = diag
    for _ in range(DEPTH):
        plus = 1.0 + 2.0 * left
        roots.append(lax.rsqrt(plus))
        left = 2.0 / math.pi * arcsine(2.0 * left / plus) + bias_var
    return roots


def forward(cross, roots, factors):
    tangent, current = cross, cross
    saved = []
    for root, plus in zip(roots, factors):
        twice = root * (2.0 * lax.rsqrt(plus))
        sine = current * twice
        inverse = lax.rsqrt(1.0 - sine * sine)
        slope = 2.0 / math.pi * twice * inverse
        saved.append((twice, sine, inverse, slope, tangent))
        current = 2.0 / math.pi * arcsine(sine) + bias_var
        tangent = current + slope * tangent
    return tangent, saved


def backward(grad, saved, factors, rates):
    tangent_bar, current_bar = grad, jnp.zeros_like(grad)
    diag_bar = None
    for layer in reversed(range(DEPTH)):
        twice, sine, inverse, slope, tangent = saved[layer]
        total = current_bar + tangent_bar
        next_bar = tangent_bar * slope
        carried = next_bar * tangent * inverse * inverse
        direct = -jnp.sum(carried + 2.0 / math.pi * total * inverse * sine, axis=0, keepdims=True) / factors[layer]
        diag_bar = direct if diag_bar is None else direct + diag_bar * rates[layer]
        current_bar = total * slope + twice * sine * carried
        tangent_bar = next_bar
    return current_bar + tangent_bar, diag_bar


def step_kernel(
    scale, pixels,
    t_hbm, s_hbm, w_hbm, labels_hbm, m1_hbm, m2_hbm,
    out_ref, n1_ref, n2_ref,
    t_v, slab, sup_v, lw, tacc, dmsg_s, dmsg_r, cacc, cmsg_s, cmsg_r, low, nmsg_s, nmsg_r,
    sy, sz, ry, rz, keep, s3, r3, s4, r4, ds, dr, mom, labels_ref, m1_ref, m2_ref,
    send_sem, recv_sem, local_sem,
):
    tgt = lax.axis_index("tgt")
    x = lax.axis_index("sup")
    core = lax.rem(tgt, 2)
    yy = lax.rem(tgt // 2, 2)
    z0 = lax.rem(tgt // 4, 2)
    z1 = tgt // 8
    sib_t = tgt + 1 - 2 * core
    y_t = tgt + 2 - 4 * yy
    z0_t = tgt + 4 - 8 * z0
    z1_t = tgt + 8 - 16 * z1
    SIB, YP, ZP, ZF = (sib_t, x), (y_t, x), (z0_t, x), (z1_t, x)
    XP, XS, AN = (tgt, 1 - x), (sib_t, 1 - x), (z1_t, 1 - x)
    DG = (y_t + z0_t - tgt, x)

    images, width = n1_ref.shape
    rows = t_v.shape[0] // 2
    half = 8 * width
    part = rows // 2
    lanes = slab.shape[0]
    sizes = [128 * n for n in CUTS]
    starts = [sum(sizes[:h]) for h in range(len(sizes))]
    chunks = range(len(sizes))

    send_ids, receive_ids, counts = {}, {}, {}

    def remote(src, dst, sent, name, device):
        return pltpu.make_async_remote_copy(
            src_ref=src, dst_ref=dst, send_sem=send_sem.at[send_ids.setdefault(sent, len(send_ids))],
            recv_sem=recv_sem.at[receive_ids.setdefault(name, len(receive_ids))],
            device_id=device, device_id_type=MESH,
        )

    def send(src, dst, sent, name, device):
        counts[sent] = counts.get(sent, 0) + src.shape[0] * src.shape[-1] // images
        remote(src, dst, sent, name, device).start()

    def arrived(dst, name, device):
        pltpu.make_async_remote_copy(
            src_ref=dst, dst_ref=dst, send_sem=send_sem.at[0],
            recv_sem=recv_sem.at[receive_ids.setdefault(name, len(receive_ids))],
            device_id=device, device_id_type=MESH,
        ).wait_recv()

    def all_sent(src, sent):
        pltpu.make_async_remote_copy(
            src_ref=src, dst_ref=src, send_sem=send_sem.at[send_ids[sent]], recv_sem=recv_sem.at[0],
            device_id=SIB, device_id_type=MESH,
        ).wait_send()

    def aligned(value, by):
        return pl.multiple_of(value, by)

    barrier = pltpu.get_barrier_semaphore()
    friends = (XP, XS, SIB, YP, ZP, DG, ZF, AN)
    for device in friends:
        pl.semaphore_signal(barrier, inc=1, device_id=device, device_id_type=MESH)

    def load(src, dst, number):
        copy = pltpu.make_async_copy(src, dst, local_sem.at[number])
        copy.start()
        return copy

    my_row = aligned(x * images, images)
    peer_row = aligned((1 - x) * images, images)

    def columns(block, owner):
        return pl.ds(aligned((2 * block + owner) * width, width), width)

    def far_columns(slab_index, block):
        return pl.ds(aligned(slab_index * half + (2 * block + core) * width, width), width)

    def block_of(j):
        return pl.ds(aligned(j * width, width), width)

    load_s = load(s_hbm, sup_v, 0)
    mine_t = pl.ds(aligned(core * rows, rows), rows)
    for j in range(4):
        load(t_hbm.at[:, columns(j, core)], t_v.at[mine_t, block_of(j)], 1)
    load_t = pltpu.make_async_copy(t_v.at[mine_t, :], t_v.at[mine_t, :], local_sem.at[1])
    for j in range(4):
        load(s_hbm.at[:, far_columns(x, j)], slab.at[pl.ds(my_row, images), block_of(j)], 2)
    my_slab = slab.at[pl.ds(my_row, images), :]
    load_o = pltpu.make_async_copy(my_slab, my_slab, local_sem.at[2])
    load_w = load(w_hbm, lw.at[pl.ds(my_row, images), :], 3)
    load_l = load(labels_hbm, labels_ref, 4)
    load_1 = load(m1_hbm, m1_ref, 5)
    load_2 = load(m2_hbm, m2_ref, 6)

    pl.semaphore_wait(barrier, len(friends))

    seat = 2 * yy + z0
    turn = (seat, 3 - seat, seat + 2 - 4 * yy, seat + 1 - 2 * z0)
    strip = images // STRIPS
    strips = range(STRIPS)
    share = images // 2

    def send_strip(p, r):
        send(
            s_hbm.at[pl.ds(r * strip, strip), far_columns(1 - x, turn[p])],
            slab.at[pl.ds(aligned(my_row + r * strip, strip), strip), block_of(turn[p])],
            "slab", ("slab", p, r), XP,
        )

    for r in strips:
        send_strip(0, r)

    def whole(ref, row, columns):
        return ref.at[pl.ds(row, images), columns]

    send(
        s_hbm.at[:, far_columns(1 - x, turn[1])], whole(slab, my_row, block_of(turn[1])), "slab", "slab", XP,
    )
    for j in range(4):
        send(t_hbm.at[:, columns(j, 1 - core)], t_v.at[mine_t, block_of(j)], "targets", "targets", SIB)
    load_1.wait()
    mom[0, z1] = m1_ref[...].astype(bf16)
    here = mom.at[0, z1]
    send(here, here, "moment", "moment", ZF)

    load_s.wait()

    def support_squares(i, acc):
        block = sup_v[:, pl.ds(aligned(i * width, width), width)].astype(f32)
        block = block * block
        for k in range(width // 128):
            acc = acc + block[:, k * 128 : (k + 1) * 128]
        return acc

    sacc = lax.fori_loop(0, pixels // width, support_squares, jnp.zeros((images, 128), f32))
    s_row = to_row(jnp.sum(sacc, axis=1, keepdims=True), x * images, lanes)

    def target_squares(first):
        def body(i, carry):
            where = pl.ds(aligned(first + i * 16, 16), 16)
            sums = []
            for j in range(4):
                block = t_v[where, j * width : (j + 1) * width].astype(f32)
                block = block * block
                acc = block[:, 0:128]
                for k in range(1, width // 128):
                    acc = acc + block[:, k * 128 : (k + 1) * 128]
                sums.append(acc)
            tacc[where, :] = (sums[0] + sums[1]) + (sums[2] + sums[3])
            return carry

        lax.fori_loop(0, rows // 16, body, 0)

    load_t.wait()
    target_squares(core * rows)

    def strip_of(p, r):
        return slab.at[pl.ds(aligned(peer_row + r * strip, strip), strip), block_of(turn[p])]

    for r in strips:
        here = strip_of(0, r)
        arrived(here, ("slab", 0, r), XP)
        send(here, here, "slab", "slab y", YP)
        send(here, here, "slab", "slab z", ZP)

    weight_rows = pl.ds(aligned(my_row + core * share, share), share)
    send(w_hbm.at[pl.ds(aligned(core * share, share), share), :], lw.at[weight_rows, :], "weights", "weights", XP)

    other_t = pl.ds(aligned((1 - core) * rows, rows), rows)
    arrived(t_v.at[other_t, :], "targets", SIB)
    target_squares((1 - core) * rows)

    group = (SIB, XP, XS)
    quarter = 2 * core + x
    theirs = (2 * (1 - core) + x, 2 * core + 1 - x, 2 * (1 - core) + 1 - x)

    def rows_of(q):
        return pl.ds(aligned(q * part, part), part)

    def square_col(q):
        return jnp.sum(tacc[rows_of(q), :], axis=1, keepdims=True)

    for i in range(3):
        dmsg_s[i, 0:8, :] = jnp.broadcast_to(to_row(square_col(theirs[i]), 0, lanes), (8, lanes))
        dmsg_s[i, 8:16, :] = jnp.broadcast_to(s_row, (8, lanes))
        send(dmsg_s.at[i], dmsg_r.at[i], "diag", "diag", group[i])
    my_sq = square_col(quarter)
    load_l.wait()
    label_col = to_col(labels_ref[...].astype(f32), part, x * part)

    load_o.wait()

    def cross_piece(p, first=False):
        value = lax.dot_general(
            t_v[:, block_of(turn[p])], slab[:, block_of(turn[p])], (((1,), (1,)), ((), ())),
            preferred_element_type=f32,
        )
        cacc[...] = value if first else cacc[...] + value

    cross_piece(0, True)
    arrived(whole(slab, peer_row, block_of(turn[1])), "slab", XP)
    cross_piece(1)
    arrived(whole(slab, peer_row, block_of(turn[2])), "slab y", YP)
    cross_piece(2)
    arrived(whole(slab, peer_row, block_of(turn[3])), "slab z", ZP)

    def last_piece(q):
        return cacc[rows_of(q), :] + lax.dot_general(
            t_v[rows_of(q), block_of(turn[3])], slab[:, block_of(turn[3])], (((1,), (1,)), ((), ())),
            preferred_element_type=f32,
        )

    for i in (2, 1, 0):
        cmsg_s[i] = last_piece(theirs[i]).astype(bf16)
        send(cmsg_s.at[i], cmsg_r.at[i], "cross", "cross", group[i])
    own_cross = last_piece(quarter)
    half_rows = lw.at[pl.ds(aligned(peer_row + core * share, share), share), :]
    arrived(half_rows, "weights", XP)
    send(half_rows, half_rows, "weights", "weights on", SIB)
    load_2.wait()
    mom[1, z1] = m2_ref[...].astype(bf16)
    here = mom.at[1, z1]
    send(here, here, "moment", "moment", ZF)

    arrived(dmsg_r, "diag", SIB)
    square_row = dmsg_r[0, 0:1, :] + dmsg_r[1, 0:1, :] + dmsg_r[2, 0:1, :]
    roots = target_chain((my_sq + to_col(square_row, part)) / pixels + bias_var)
    factors, rates = support_chain((s_row + dmsg_r[1, 8:9, :]) / pixels + bias_var)
    load_w.wait()
    arrived(lw.at[pl.ds(aligned(peer_row + (1 - core) * share, share), share), :], "weights on", SIB)

    arrived(cmsg_r, "cross", SIB)
    total = own_cross + cmsg_r[0].astype(f32)
    total = total + (cmsg_r[1].astype(f32) + cmsg_r[2].astype(f32))
    kernel, saved = forward(total / pixels + bias_var, roots, factors)
    weights = lw[...]
    predicted = jnp.dot(kernel.astype(bf16), weights, preferred_element_type=f32)
    classes = lax.broadcasted_iota(jnp.int32, predicted.shape, 1)
    onehot = (label_col == classes.astype(f32)).astype(f32)
    residual = (predicted - onehot).astype(bf16)
    kernel_grad = scale * lax.dot_general(
        residual, weights, (((1,), (1,)), ((), ())), preferred_element_type=f32
    )
    cross_grad, norm_grad = backward(kernel_grad, saved, factors, rates)
    mine_low = low.at[rows_of(quarter), :]
    mine_low[...] = cross_grad.astype(bf16)
    for i in (2, 1, 0):
        send(mine_low, mine_low, "low", "low", group[i])
    nmsg_s[...] = jnp.broadcast_to(norm_grad, nmsg_s.shape)
    for i in (2, 1, 0):
        send(nmsg_s, nmsg_r.at[i], "norm", "norm", group[i])
    arrived(low.at[0 : 3 * part, :], "low", SIB)
    arrived(nmsg_r, "norm", SIB)
    norm_row = norm_grad + nmsg_r[0, 0:1, :] + nmsg_r[1, 0:1, :] + nmsg_r[2, 0:1, :]
    norm_col = to_col(2.0 * norm_row, lanes)
    grads = low[...].astype(f32).T.astype(bf16)

    order = ((1, 1), (0, 1), (1, 0), (0, 0))
    first = slice(0, images)
    second = slice(images, 2 * images)

    def at(k, h):
        return (k, slice(None), slice(starts[h], starts[h] + sizes[h]))

    def block_grad(k, h):
        dz, dy = order[k]
        number = (z0 + dz - 2 * dz * z0) * 2 + (yy + dy - 2 * dy * yy)
        where = pl.ds(aligned(number * width + starts[h], 128), sizes[h])
        value = jnp.dot(grads, t_v[:, where], preferred_element_type=f32)
        return value + norm_col * slab[:, where].astype(f32)

    for h in chunks:
        if h in DIRECT:
            for k, device in enumerate((DG, YP, ZP)):
                here = at(k, h)
                ds[here] = block_grad(k, h).astype(bf16)
                send(ds.at[here], dr.at[here], "sum", ("sum", h), device)
            continue
        value = block_grad(0, h)
        sy[at(0, h)] = value[first].astype(bf16)
        send(sy.at[at(0, h)], ry.at[at(0, h)], "sum", ("pair", h), YP)
        sz[at(0, h)] = value[second].astype(bf16)
        send(sz.at[at(0, h)], rz.at[at(0, h)], "sum", ("pair", h), ZP)
        value = block_grad(1, h)
        sy[at(1, h)] = value[first].astype(bf16)
        send(sy.at[at(1, h)], ry.at[at(1, h)], "sum", ("sum", h), YP)
        keep[at(0, h)] = value[second]
        value = block_grad(2, h)
        sz[at(1, h)] = value[second].astype(bf16)
        send(sz.at[at(1, h)], rz.at[at(1, h)], "sum", ("sum", h), ZP)
        keep[at(1, h)] = value[first]
    for h in chunks:
        value = block_grad(3, h)
        keep[at(2, h)] = value[first]
        keep[at(3, h)] = value[second]

    def pieces(count):
        return sup_v.at[:, 0:count]

    def late(h):
        arrived(pieces(2 * sizes[h]), ("pair", h), YP)
        s3[at(0, h)] = (keep[at(1, h)] + ry[at(0, h)].astype(f32)).astype(bf16)
        send(s3.at[at(0, h)], r3.at[at(0, h)], "sum", ("sum", h), ZP)
        s3[at(1, h)] = (keep[at(0, h)] + rz[at(0, h)].astype(f32)).astype(bf16)
        send(s3.at[at(1, h)], r3.at[at(1, h)], "sum", ("sum", h), YP)

    def group_sum(h):
        arrived(pieces((6 if h in DIRECT else 4) * sizes[h]), ("sum", h), YP)
        if h in DIRECT:
            extra = dr[at(0, h)].astype(f32) + dr[at(1, h)].astype(f32) + dr[at(2, h)].astype(f32)
            one = keep[at(2, h)] + extra[first]
            two = keep[at(3, h)] + extra[second]
        else:
            one = (keep[at(2, h)] + ry[at(1, h)].astype(f32)) + r3[at(0, h)].astype(f32)
            two = (keep[at(3, h)] + rz[at(1, h)].astype(f32)) + r3[at(1, h)].astype(f32)
        s4[at(0, h)] = one.astype(bf16)
        s4[at(1, h)] = two.astype(bf16)
        send(s4.at[at(x, h)], r4.at[at(0, h)], "sum", ("last z", h), ZF)
        send(s4.at[at(1 - x, h)], r4.at[at(2, h)], "sum", ("last", h), XP)
        send(s4.at[at(1 - x, h)], r4.at[at(1, h)], "sum", ("last", h), AN)

    for h in chunks:
        if h in DIRECT:
            group_sum(h)
    for h in chunks:
        if h not in DIRECT:
            late(h)
    for h in chunks:
        if h not in DIRECT:
            group_sum(h)

    arrived(mom.at[:, 1 - z1], "moment", ZF)

    def cut(index, h):
        return pl.ds(aligned(index * width + starts[h], 128), sizes[h])

    def pass_on(index, name, device, h):
        here = out_ref.at[:, cut(index, h)]
        send(here, here, "gather", (name, h) if device is not SIB else "sibling", device)

    def came(index, name, device, h):
        arrived(out_ref.at[:, cut(index, h)], (name, h), device)

    def moved(first_in, second_in, gradient):
        new_first = first_decay * first_in + (1.0 - first_decay) * gradient
        new_second = second_decay * second_in + (1.0 - second_decay) * gradient * gradient
        return new_first, new_second

    slabs = (x, 1 - x)
    tgt_in = tgt - 8 * z1
    y_in, z_in, d_in = y_t - 8 * z1, z0_t - 8 * z1, y_t + z0_t - tgt - 8 * z1

    steps = [(h, i) for h in chunks for i in (0, 1)]
    straight_steps = [steps[n] for n in DIRECT_STEPS]

    def adam(h, i):
        here = slice(starts[h], starts[h] + sizes[h])
        side = slabs[i]
        if i == 0:
            arrived(r4.at[at(0, h)], ("last z", h), ZF)
            gradient = (s4[at(x, h)].astype(f32) + r4[at(0, h)].astype(f32)) / pixels
        else:
            arrived(pieces(2 * sizes[h]), ("last", h), XP)
            gradient = (r4[at(1, h)].astype(f32) + r4[at(2, h)].astype(f32)) / pixels
        new_first, new_second = moved(mom[0, side, :, here].astype(f32), mom[1, side, :, here].astype(f32), gradient)
        update = learning_rate * (new_first / first_fix) / (jnp.sqrt(new_second / second_fix) + adam_eps)
        spot = tgt_in + 8 * side
        out_ref[:, cut(spot, h)] = (sup_v[:, cut(spot, h)].astype(f32) - update).astype(bf16)
        if (h, i) in straight_steps:
            pass_on(spot, ("own d", i), DG, h)
        pass_on(spot, ("own z", i), ZP, h)
        pass_on(spot, ("own y", i), YP, h)
        pass_on(spot, ("own s", i), SIB, h)

        @pl.when(side == z1)
        def _():
            new_first, new_second = moved(m1_ref[:, here], m2_ref[:, here], gradient)
            n1_ref[:, here] = new_first
            n2_ref[:, here] = new_second

    def relay(h, i):
        side = 8 * slabs[i]
        turned = steps.index((h, i)) in TURNED
        came(side + z_in, ("own z", i), ZP, h)
        if (h, i) not in straight_steps and not turned:
            pass_on(side + z_in, ("z y", i), YP, h)
        pass_on(side + z_in, ("z s", i), SIB, h)
        came(side + y_in, ("own y", i), YP, h)
        if (h, i) not in straight_steps and turned:
            pass_on(side + y_in, ("z y", i), ZP, h)
        pass_on(side + y_in, ("y s", i), SIB, h)

    def finish(h, i):
        side = 8 * slabs[i]
        if (h, i) in straight_steps:
            came(side + d_in, ("own d", i), DG, h)
        else:
            came(side + d_in, ("z y", i), YP, h)
        pass_on(side + d_in, ("d s", i), SIB, h)

    for n in range(len(steps) + LAG):
        if n < len(steps):
            adam(*steps[n])
        if n >= LAG:
            relay(*steps[n - LAG])
    for step in steps:
        finish(*step)
    arrived(out_ref.at[:, 0 : 8 * width], "sibling", SIB)
    all_sent(sup_v.at[:, 0 : 4 * width], "slab")
    all_sent(t_v.at[other_t, :], "targets")
    all_sent(lw.at[0:images, :], "weights")
    all_sent(dmsg_s, "diag")
    all_sent(cmsg_s, "cross")
    all_sent(low.at[0 : 3 * part, :], "low")
    all_sent(nmsg_r, "norm")
    all_sent(mom.at[:, 0], "moment")
    all_sent(pieces(counts["sum"]), "sum")
    all_sent(pieces(counts["gather"]), "gather")
    assert len(send_ids) <= SENDS and len(receive_ids) <= RECEIVES


def fused(targets, support, label_weights, labels, first_moment, second_moment):
    rows, _ = targets.shape
    images, pixels = support.shape
    width = first_moment.shape[1]
    classes = label_weights.shape[1]
    target_count = rows * lax.axis_size("tgt")
    support_count = images * lax.axis_size("sup")
    scale = 4.0 * pixels * math.sqrt(classes * support_count / target_count)
    everyone, part = 2 * images, rows // 2
    hbm = pl.BlockSpec(memory_space=pltpu.HBM)
    vmem = pl.BlockSpec(memory_space=pltpu.VMEM)
    slots = pltpu.VMEM((2, images, width), bf16)
    return pl.pallas_call(
        functools.partial(step_kernel, scale, pixels),
        out_shape=(
            pltpu.VMEM(support.shape, bf16),
            pltpu.VMEM(first_moment.shape, f32),
            pltpu.VMEM(first_moment.shape, f32),
        ),
        in_specs=[hbm] * 6,
        out_specs=(vmem, vmem, vmem),
        scratch_shapes=[
            pltpu.VMEM((2 * rows, 4 * width), bf16),
            pltpu.VMEM((everyone, 4 * width), bf16),
            pltpu.VMEM((images, pixels), bf16),
            pltpu.VMEM((everyone, classes), bf16),
            pltpu.VMEM((2 * rows, 128), f32),
            pltpu.VMEM((3, 16, everyone), f32),
            pltpu.VMEM((3, 16, everyone), f32),
            pltpu.VMEM((2 * rows, everyone), f32),
            pltpu.VMEM((3, part, everyone), bf16),
            pltpu.VMEM((3, part, everyone), bf16),
            pltpu.VMEM((2 * rows, everyone), bf16),
            pltpu.VMEM((8, everyone), f32),
            pltpu.VMEM((3, 8, everyone), f32),
            slots,
            slots,
            slots,
            slots,
            pltpu.VMEM((4, images, width), f32),
            slots,
            slots,
            slots,
            pltpu.VMEM((3, images, width), bf16),
            pltpu.VMEM((3, everyone, width), bf16),
            pltpu.VMEM((3, everyone, width), bf16),
            pltpu.VMEM((2, 2, images, width), bf16),
            pltpu.VMEM((1, rows), jnp.int32),
            pltpu.VMEM((images, width), f32),
            pltpu.VMEM((images, width), f32),
            pltpu.SemaphoreType.DMA((SENDS,)),
            pltpu.SemaphoreType.DMA((RECEIVES,)),
            pltpu.SemaphoreType.DMA((LOADS,)),
        ],
        compiler_params=pltpu.CompilerParams(
            collective_id=0, has_side_effects=True, vmem_limit_bytes=60000000
        ),
    )(targets, support, label_weights, labels[None, :], first_moment, second_moment)


def hand_over(a_ref, b_ref, c_ref, x_ref, y_ref, z_ref, sem):
    copies = [
        pltpu.make_async_copy(src, dst, sem.at[i])
        for i, (src, dst) in enumerate(((a_ref, x_ref), (b_ref, y_ref), (c_ref, z_ref)))
    ]
    for copy in copies:
        copy.start()
    for copy in copies:
        copy.wait()


def settle(support, first, second, space):
    return pl.pallas_call(
        hand_over,
        out_shape=tuple(jax.ShapeDtypeStruct(a.shape, a.dtype) for a in (support, first, second)),
        in_specs=[pl.BlockSpec(memory_space=space)] * 3,
        out_specs=(pl.BlockSpec(memory_space=pltpu.HBM),) * 3,
        scratch_shapes=[pltpu.SemaphoreType.DMA((3,))],
    )(support, first, second)


def pick(mesh):
    groups, shares = mesh.shape["sup"], mesh.shape["tgt"]

    def run(targets, support, label_weights, labels, first_moment, second_moment):
        width = first_moment.shape[1]
        fits = groups == 2 and shares == 16 and width == 128 * sum(CUTS)
        fits = fits and targets.shape[0] % 32 == 0 and groups * support.shape[0] == 128
        body = fused if fits else shards
        out = body(targets, support, label_weights, labels, first_moment, second_moment)
        return settle(*[pltpu.with_memory_space_constraint(o, pltpu.VMEM) for o in out], pltpu.VMEM) if fits else out

    return run


def solution(mesh):
    return jax.shard_map(
        pick(mesh),
        mesh=mesh,
        in_specs=(
            P("tgt", "sup"),
            P("sup", None),
            P("sup", None),
            P("tgt"),
            P("sup", "tgt"),
            P("sup", "tgt"),
        ),
        out_specs=(P("sup", None), P("sup", "tgt"), P("sup", "tgt")),
        check_vma=False,
    )
```

```python
import functools
import math

import jax
import jax.numpy as jnp
from jax import lax
from jax.experimental import pallas as pl
from jax.experimental.pallas import tpu as pltpu
from jax.sharding import PartitionSpec as P

DEPTH = 3


bias_var = 0.1
learning_rate = 0.05
first_decay = 0.9
second_decay = 0.99
first_fix = 1.0 - 0.9**10
second_fix = 1.0 - 0.99**10
adam_eps = 1e-08


def tangent_kernel(cross, target_diag, support_diag):
    tangent = cross
    current = cross
    left_diag = target_diag
    right_diag = support_diag
    for _ in range(DEPTH):
        product = (1.0 + 2.0 * left_diag)[:, None] * (1.0 + 2.0 * right_diag)[None, :]
        slope = 4.0 / math.pi / jnp.sqrt(product - 4.0 * current * current)
        current = 2.0 / math.pi * jnp.arcsin(2.0 * current / jnp.sqrt(product)) + bias_var
        tangent = current + slope * tangent
        left_diag = 2.0 / math.pi * jnp.arcsin(2.0 * left_diag / (1.0 + 2.0 * left_diag)) + bias_var
        right_diag = (
            2.0 / math.pi * jnp.arcsin(2.0 * right_diag / (1.0 + 2.0 * right_diag)) + bias_var
        )
    return tangent


def row_squares(images):
    return jnp.sum(jnp.square(images.astype(jnp.float32)), axis=1)


def shards(targets, support, label_weights, labels, first_moment, second_moment):
    pixels = support.shape[1]
    target_count = targets.shape[0] * lax.axis_size("tgt")
    support_count = support.shape[0] * lax.axis_size("sup")
    class_count = label_weights.shape[1]
    support_diag = row_squares(support) / pixels + bias_var
    slabs = lax.all_to_all(support, "sup", split_axis=1, concat_axis=0, tiled=True)
    partial_cross = lax.dot_general(
        targets, slabs, (((1,), (1,)), ((), ())), preferred_element_type=jnp.float32
    )
    cross = (
        lax.psum_scatter(
            partial_cross.astype(jnp.bfloat16), "sup", scatter_dimension=1, tiled=True
        ).astype(jnp.float32)
        / pixels
        + bias_var
    )
    target_diag = lax.psum(row_squares(targets), "sup") / pixels + bias_var

    def kernel_of(cross_in, diag_in):
        return tangent_kernel(cross_in, target_diag, diag_in)

    kernel, pullback = jax.vjp(kernel_of, cross, support_diag)
    partial_pred = jnp.dot(
        kernel.astype(jnp.bfloat16), label_weights, preferred_element_type=jnp.float32
    )
    predicted = lax.psum(partial_pred.astype(jnp.bfloat16), "sup").astype(jnp.float32)
    classes = jnp.arange(class_count, dtype=jnp.int32)
    onehot = (labels[:, None] == classes[None, :]).astype(jnp.float32)
    residual = (predicted - onehot).astype(jnp.bfloat16)
    kernel_grad = lax.dot_general(
        residual, label_weights, (((1,), (1,)), ((), ())), preferred_element_type=jnp.float32
    )
    kernel_grad = kernel_grad * (
        4.0 * pixels * math.sqrt(class_count * support_count / target_count)
    )
    cross_grad, norm_grad = pullback(kernel_grad)
    cross_low = cross_grad.astype(jnp.bfloat16)
    all_grads = lax.all_gather(cross_low, "sup", axis=1, tiled=True)
    slab_grad = lax.dot_general(
        all_grads, targets, (((0,), (0,)), ((), ())), preferred_element_type=jnp.float32
    )
    image_grad = lax.all_to_all(
        slab_grad.astype(jnp.bfloat16), "sup", split_axis=0, concat_axis=1, tiled=True
    ).astype(slab_grad.dtype)
    gradient = (image_grad + 2.0 * norm_grad[:, None] * support.astype(jnp.float32)) / pixels
    shares = lax.psum_scatter(gradient, "tgt", scatter_dimension=1, tiled=True)
    slab_width = shares.shape[1]
    own_pixels = lax.dynamic_slice_in_dim(
        support, lax.axis_index("tgt") * slab_width, slab_width, 1
    ).astype(jnp.float32)
    new_first = first_decay * first_moment + (1.0 - first_decay) * shares
    new_second = second_decay * second_moment + (1.0 - second_decay) * shares * shares
    update = (
        learning_rate * (new_first / first_fix) / (jnp.sqrt(new_second / second_fix) + adam_eps)
    )
    new_slab = (own_pixels - update).astype(jnp.bfloat16)
    new_support = lax.all_gather(new_slab, "tgt", axis=1, tiled=True)
    return (new_support, new_first, new_second)


MESH = pl.DeviceIdType.MESH
f32 = jnp.float32
bf16 = jnp.bfloat16


@jax.custom_jvp
def arcsine(x):
    a = jnp.abs(x)
    big = a > 0.5
    z = jnp.where(big, 0.5 * (1.0 - a), a * a)
    s = jnp.where(big, jnp.sqrt(z), a)
    p = 4.2163199048e-2 * z + 2.4181311049e-2
    p = p * z + 4.5470025998e-2
    p = p * z + 7.4953002686e-2
    p = p * z + 1.6666752422e-1
    p = p * z * s + s
    r = jnp.where(big, math.pi / 2.0 - 2.0 * p, p)
    return jnp.where(x < 0.0, -r, r)


@arcsine.defjvp
def arcsine_jvp(primals, tangents):
    (x,) = primals
    (t,) = tangents
    return arcsine(x), t * lax.rsqrt(1.0 - x * x)


def tangent_tile(cross, target_diag, support_diag):
    tangent = cross
    current = cross
    left = target_diag
    right = support_diag
    for _ in range(DEPTH):
        product = (1.0 + 2.0 * left) * (1.0 + 2.0 * right)
        slope = 4.0 / math.pi * lax.rsqrt(product - 4.0 * current * current)
        current = 2.0 / math.pi * arcsine(2.0 * current * lax.rsqrt(product)) + bias_var
        tangent = current + slope * tangent
        left = 2.0 / math.pi * arcsine(2.0 * left / (1.0 + 2.0 * left)) + bias_var
        right = 2.0 / math.pi * arcsine(2.0 * right / (1.0 + 2.0 * right)) + bias_var
    return tangent


def to_row(col, offset, lanes):
    shape = (col.shape[0], lanes)
    hit = lax.broadcasted_iota(jnp.int32, shape, 1) == lax.broadcasted_iota(jnp.int32, shape, 0) + offset
    return jnp.sum(jnp.where(hit, col, 0.0), axis=0, keepdims=True)


def to_col(row, count, offset=0):
    shape = (count, row.shape[1])
    hit = lax.broadcasted_iota(jnp.int32, shape, 1) == lax.broadcasted_iota(jnp.int32, shape, 0) + offset
    return jnp.sum(jnp.where(hit, row, 0.0), axis=1, keepdims=True)


SENDS, RECEIVES, LOADS = 10, 43, 7
CUTS = (2, 2, 2)
STRIPS = 2
DIRECT = (0,)
DIRECT_STEPS = (3, 4, 5)
LAG = 4
TURNED = ()


def support_chain(diag):
    factors, rates = [], []
    right = diag
    for _ in range(DEPTH):
        plus = 1.0 + 2.0 * right
        factors.append(plus)
        rates.append(4.0 / math.pi / (plus * jnp.sqrt(1.0 + 4.0 * right)))
        right = 2.0 / math.pi * arcsine(2.0 * right / plus) + bias_var
    return factors, rates


def target_chain(diag):
    roots = []
    left = diag
    for _ in range(DEPTH):
        plus = 1.0 + 2.0 * left
        roots.append(lax.rsqrt(plus))
        left = 2.0 / math.pi * arcsine(2.0 * left / plus) + bias_var
    return roots


def forward(cross, roots, factors):
    tangent, current = cross, cross
    saved = []
    for root, plus in zip(roots, factors):
        twice = root * (2.0 * lax.rsqrt(plus))
        sine = current * twice
        inverse = lax.rsqrt(1.0 - sine * sine)
        slope = 2.0 / math.pi * twice * inverse
        saved.append((twice, sine, inverse, slope, tangent))
        current = 2.0 / math.pi * arcsine(sine) + bias_var
        tangent = current + slope * tangent
    return tangent, saved


def backward(grad, saved, factors, rates):
    tangent_bar, current_bar = grad, jnp.zeros_like(grad)
    diag_bar = None
    for layer in reversed(range(DEPTH)):
        twice, sine, inverse, slope, tangent = saved[layer]
        total = current_bar + tangent_bar
        next_bar = tangent_bar * slope
        carried = next_bar * tangent * inverse * inverse
        direct = -jnp.sum(carried + 2.0 / math.pi * total * inverse * sine, axis=0, keepdims=True) / factors[layer]
        diag_bar = direct if diag_bar is None else direct + diag_bar * rates[layer]
        current_bar = total * slope + twice * sine * carried
        tangent_bar = next_bar
    return current_bar + tangent_bar, diag_bar


def step_kernel(
    scale, pixels,
    t_hbm, s_hbm, w_hbm, labels_hbm, m1_hbm, m2_hbm,
    out_ref, n1_ref, n2_ref,
    t_v, slab, sup_v, lw, tacc, dmsg_s, dmsg_r, cacc, cmsg_s, cmsg_r, low, nmsg_s, nmsg_r,
    sy, sz, ry, rz, keep, s3, r3, s4, r4, ds, dr, mom, labels_ref, m1_ref, m2_ref,
    send_sem, recv_sem, local_sem,
):
    tgt = lax.axis_index("tgt")
    x = lax.axis_index("sup")
    core = lax.rem(tgt, 2)
    yy = lax.rem(tgt // 2, 2)
    z0 = lax.rem(tgt // 4, 2)
    z1 = tgt // 8
    sib_t = tgt + 1 - 2 * core
    y_t = tgt + 2 - 4 * yy
    z0_t = tgt + 4 - 8 * z0
    z1_t = tgt + 8 - 16 * z1
    SIB, YP, ZP, ZF = (sib_t, x), (y_t, x), (z0_t, x), (z1_t, x)
    XP, XS, AN = (tgt, 1 - x), (sib_t, 1 - x), (z1_t, 1 - x)
    DG = (y_t + z0_t - tgt, x)

    images, width = n1_ref.shape
    rows = t_v.shape[0] // 2
    half = 8 * width
    part = rows // 2
    lanes = slab.shape[0]
    sizes = [128 * n for n in CUTS]
    starts = [sum(sizes[:h]) for h in range(len(sizes))]
    chunks = range(len(sizes))

    send_ids, receive_ids, counts = {}, {}, {}

    def remote(src, dst, sent, name, device):
        return pltpu.make_async_remote_copy(
            src_ref=src, dst_ref=dst, send_sem=send_sem.at[send_ids.setdefault(sent, len(send_ids))],
            recv_sem=recv_sem.at[receive_ids.setdefault(name, len(receive_ids))],
            device_id=device, device_id_type=MESH,
        )

    def send(src, dst, sent, name, device):
        counts[sent] = counts.get(sent, 0) + src.shape[0] * src.shape[-1] // images
        remote(src, dst, sent, name, device).start()

    def arrived(dst, name, device):
        pltpu.make_async_remote_copy(
            src_ref=dst, dst_ref=dst, send_sem=send_sem.at[0],
            recv_sem=recv_sem.at[receive_ids.setdefault(name, len(receive_ids))],
            device_id=device, device_id_type=MESH,
        ).wait_recv()

    def all_sent(src, sent):
        pltpu.make_async_remote_copy(
            src_ref=src, dst_ref=src, send_sem=send_sem.at[send_ids[sent]], recv_sem=recv_sem.at[0],
            device_id=SIB, device_id_type=MESH,
        ).wait_send()

    def aligned(value, by):
        return pl.multiple_of(value, by)

    barrier = pltpu.get_barrier_semaphore()
    friends = (XP, XS, SIB, YP, ZP, DG, ZF, AN)
    for device in friends:
        pl.semaphore_signal(barrier, inc=1, device_id=device, device_id_type=MESH)

    def load(src, dst, number):
        copy = pltpu.make_async_copy(src, dst, local_sem.at[number])
        copy.start()
        return copy

    my_row = aligned(x * images, images)
    peer_row = aligned((1 - x) * images, images)

    def columns(block, owner):
        return pl.ds(aligned((2 * block + owner) * width, width), width)

    def far_columns(slab_index, block):
        return pl.ds(aligned(slab_index * half + (2 * block + core) * width, width), width)

    def block_of(j):
        return pl.ds(aligned(j * width, width), width)

    load_1 = load(m1_hbm, m1_ref, 5)
    load_s = load(s_hbm, sup_v, 0)
    mine_t = pl.ds(aligned(core * rows, rows), rows)
    for j in range(4):
        load(t_hbm.at[:, columns(j, core)], t_v.at[mine_t, block_of(j)], 1)
    load_t = pltpu.make_async_copy(t_v.at[mine_t, :], t_v.at[mine_t, :], local_sem.at[1])
    for j in range(4):
        load(s_hbm.at[:, far_columns(x, j)], slab.at[pl.ds(my_row, images), block_of(j)], 2)
    my_slab = slab.at[pl.ds(my_row, images), :]
    load_o = pltpu.make_async_copy(my_slab, my_slab, local_sem.at[2])
    load_w = load(w_hbm, lw.at[pl.ds(my_row, images), :], 3)
    load_l = load(labels_hbm, labels_ref, 4)
    load_2 = load(m2_hbm, m2_ref, 6)

    pl.semaphore_wait(barrier, len(friends))

    seat = 2 * yy + z0
    turn = (seat, 3 - seat, seat + 2 - 4 * yy, seat + 1 - 2 * z0)
    strip = images // STRIPS
    strips = range(STRIPS)
    share = images // 2

    def send_strip(p, r):
        send(
            s_hbm.at[pl.ds(r * strip, strip), far_columns(1 - x, turn[p])],
            slab.at[pl.ds(aligned(my_row + r * strip, strip), strip), block_of(turn[p])],
            "slab", ("slab", p, r), XP,
        )

    for r in strips:
        send_strip(0, r)

    def whole(ref, row, columns):
        return ref.at[pl.ds(row, images), columns]

    send(
        s_hbm.at[:, far_columns(1 - x, turn[1])], whole(slab, my_row, block_of(turn[1])), "slab", "slab", XP,
    )
    load_1.wait()
    mom[0, z1] = m1_ref[...].astype(bf16)
    here = mom.at[0, z1]
    send(here, here, "moment", "moment", ZF)

    for j in range(4):
        send(t_hbm.at[:, columns(j, 1 - core)], t_v.at[mine_t, block_of(j)], "targets", "targets", SIB)
    load_s.wait()

    def support_squares(i, acc):
        block = sup_v[:, pl.ds(aligned(i * width, width), width)].astype(f32)
        block = block * block
        for k in range(width // 128):
            acc = acc + block[:, k * 128 : (k + 1) * 128]
        return acc

    sacc = lax.fori_loop(0, pixels // width, support_squares, jnp.zeros((images, 128), f32))
    s_row = to_row(jnp.sum(sacc, axis=1, keepdims=True), x * images, lanes)

    def target_squares(first):
        def body(i, carry):
            where = pl.ds(aligned(first + i * 16, 16), 16)
            sums = []
            for j in range(4):
                block = t_v[where, j * width : (j + 1) * width].astype(f32)
                block = block * block
                acc = block[:, 0:128]
                for k in range(1, width // 128):
                    acc = acc + block[:, k * 128 : (k + 1) * 128]
                sums.append(acc)
            tacc[where, :] = (sums[0] + sums[1]) + (sums[2] + sums[3])
            return carry

        lax.fori_loop(0, rows // 16, body, 0)

    load_t.wait()
    target_squares(core * rows)

    def strip_of(p, r):
        return slab.at[pl.ds(aligned(peer_row + r * strip, strip), strip), block_of(turn[p])]

    for r in strips:
        here = strip_of(0, r)
        arrived(here, ("slab", 0, r), XP)
        send(here, here, "slab", "slab y", YP)
        send(here, here, "slab", "slab z", ZP)

    weight_rows = pl.ds(aligned(my_row + core * share, share), share)
    send(w_hbm.at[pl.ds(aligned(core * share, share), share), :], lw.at[weight_rows, :], "weights", "weights", XP)

    other_t = pl.ds(aligned((1 - core) * rows, rows), rows)
    arrived(t_v.at[other_t, :], "targets", SIB)
    target_squares((1 - core) * rows)

    group = (SIB, XP, XS)
    quarter = 2 * core + x
    theirs = (2 * (1 - core) + x, 2 * core + 1 - x, 2 * (1 - core) + 1 - x)

    def rows_of(q):
        return pl.ds(aligned(q * part, part), part)

    def square_col(q):
        return jnp.sum(tacc[rows_of(q), :], axis=1, keepdims=True)

    for i in range(3):
        dmsg_s[i, 0:8, :] = jnp.broadcast_to(to_row(square_col(theirs[i]), 0, lanes), (8, lanes))
        dmsg_s[i, 8:16, :] = jnp.broadcast_to(s_row, (8, lanes))
        send(dmsg_s.at[i], dmsg_r.at[i], "diag", "diag", group[i])
    my_sq = square_col(quarter)
    load_l.wait()
    label_col = to_col(labels_ref[...].astype(f32), part, x * part)

    load_o.wait()

    def cross_piece(p, first=False):
        value = lax.dot_general(
            t_v[:, block_of(turn[p])], slab[:, block_of(turn[p])], (((1,), (1,)), ((), ())),
            preferred_element_type=f32,
        )
        cacc[...] = value if first else cacc[...] + value

    cross_piece(0, True)
    arrived(whole(slab, peer_row, block_of(turn[1])), "slab", XP)
    cross_piece(1)
    arrived(whole(slab, peer_row, block_of(turn[2])), "slab y", YP)
    cross_piece(2)
    arrived(whole(slab, peer_row, block_of(turn[3])), "slab z", ZP)

    def last_piece(q):
        return cacc[rows_of(q), :] + lax.dot_general(
            t_v[rows_of(q), block_of(turn[3])], slab[:, block_of(turn[3])], (((1,), (1,)), ((), ())),
            preferred_element_type=f32,
        )

    for i in (2, 1, 0):
        cmsg_s[i] = last_piece(theirs[i]).astype(bf16)
        send(cmsg_s.at[i], cmsg_r.at[i], "cross", "cross", group[i])
    own_cross = last_piece(quarter)
    half_rows = lw.at[pl.ds(aligned(peer_row + core * share, share), share), :]
    arrived(half_rows, "weights", XP)
    send(half_rows, half_rows, "weights", "weights on", SIB)
    load_2.wait()
    mom[1, z1] = m2_ref[...].astype(bf16)
    here = mom.at[1, z1]
    send(here, here, "moment", "moment", ZF)

    arrived(dmsg_r, "diag", SIB)
    square_row = dmsg_r[0, 0:1, :] + dmsg_r[1, 0:1, :] + dmsg_r[2, 0:1, :]
    roots = target_chain((my_sq + to_col(square_row, part)) / pixels + bias_var)
    factors, rates = support_chain((s_row + dmsg_r[1, 8:9, :]) / pixels + bias_var)
    load_w.wait()
    arrived(lw.at[pl.ds(aligned(peer_row + (1 - core) * share, share), share), :], "weights on", SIB)

    arrived(cmsg_r, "cross", SIB)
    total = own_cross + cmsg_r[0].astype(f32)
    total = total + (cmsg_r[1].astype(f32) + cmsg_r[2].astype(f32))
    kernel, saved = forward(total / pixels + bias_var, roots, factors)
    weights = lw[...]
    predicted = jnp.dot(kernel.astype(bf16), weights, preferred_element_type=f32)
    classes = lax.broadcasted_iota(jnp.int32, predicted.shape, 1)
    onehot = (label_col == classes.astype(f32)).astype(f32)
    residual = (predicted - onehot).astype(bf16)
    kernel_grad = scale * lax.dot_general(
        residual, weights, (((1,), (1,)), ((), ())), preferred_element_type=f32
    )
    cross_grad, norm_grad = backward(kernel_grad, saved, factors, rates)
    mine_low = low.at[rows_of(quarter), :]
    mine_low[...] = cross_grad.astype(bf16)
    for i in (2, 1, 0):
        send(mine_low, mine_low, "low", "low", group[i])
    nmsg_s[...] = jnp.broadcast_to(norm_grad, nmsg_s.shape)
    for i in (2, 1, 0):
        send(nmsg_s, nmsg_r.at[i], "norm", "norm", group[i])
    arrived(low.at[0 : 3 * part, :], "low", SIB)
    arrived(nmsg_r, "norm", SIB)
    norm_row = norm_grad + nmsg_r[0, 0:1, :] + nmsg_r[1, 0:1, :] + nmsg_r[2, 0:1, :]
    norm_col = to_col(2.0 * norm_row, lanes)
    grads = low[...].astype(f32).T.astype(bf16)

    order = ((1, 1), (0, 1), (1, 0), (0, 0))
    first = slice(0, images)
    second = slice(images, 2 * images)

    def at(k, h):
        return (k, slice(None), slice(starts[h], starts[h] + sizes[h]))

    def block_grad(k, h):
        dz, dy = order[k]
        number = (z0 + dz - 2 * dz * z0) * 2 + (yy + dy - 2 * dy * yy)
        where = pl.ds(aligned(number * width + starts[h], 128), sizes[h])
        value = jnp.dot(grads, t_v[:, where], preferred_element_type=f32)
        return value + norm_col * slab[:, where].astype(f32)

    for h in chunks:
        if h in DIRECT:
            for k, device in enumerate((DG, YP, ZP)):
                here = at(k, h)
                ds[here] = block_grad(k, h).astype(bf16)
                send(ds.at[here], dr.at[here], "sum", ("sum", h), device)
            continue
        value = block_grad(0, h)
        sy[at(0, h)] = value[first].astype(bf16)
        send(sy.at[at(0, h)], ry.at[at(0, h)], "sum", ("pair", h), YP)
        sz[at(0, h)] = value[second].astype(bf16)
        send(sz.at[at(0, h)], rz.at[at(0, h)], "sum", ("pair", h), ZP)
        value = block_grad(1, h)
        sy[at(1, h)] = value[first].astype(bf16)
        send(sy.at[at(1, h)], ry.at[at(1, h)], "sum", ("sum", h), YP)
        keep[at(0, h)] = value[second]
        value = block_grad(2, h)
        sz[at(1, h)] = value[second].astype(bf16)
        send(sz.at[at(1, h)], rz.at[at(1, h)], "sum", ("sum", h), ZP)
        keep[at(1, h)] = value[first]
    for h in chunks:
        value = block_grad(3, h)
        keep[at(2, h)] = value[first]
        keep[at(3, h)] = value[second]

    def pieces(count):
        return sup_v.at[:, 0:count]

    def late(h):
        arrived(pieces(2 * sizes[h]), ("pair", h), YP)
        s3[at(0, h)] = (keep[at(1, h)] + ry[at(0, h)].astype(f32)).astype(bf16)
        send(s3.at[at(0, h)], r3.at[at(0, h)], "sum", ("sum", h), ZP)
        s3[at(1, h)] = (keep[at(0, h)] + rz[at(0, h)].astype(f32)).astype(bf16)
        send(s3.at[at(1, h)], r3.at[at(1, h)], "sum", ("sum", h), YP)

    def group_sum(h):
        arrived(pieces((6 if h in DIRECT else 4) * sizes[h]), ("sum", h), YP)
        if h in DIRECT:
            extra = dr[at(0, h)].astype(f32) + dr[at(1, h)].astype(f32) + dr[at(2, h)].astype(f32)
            one = keep[at(2, h)] + extra[first]
            two = keep[at(3, h)] + extra[second]
        else:
            one = (keep[at(2, h)] + ry[at(1, h)].astype(f32)) + r3[at(0, h)].astype(f32)
            two = (keep[at(3, h)] + rz[at(1, h)].astype(f32)) + r3[at(1, h)].astype(f32)
        s4[at(0, h)] = one.astype(bf16)
        s4[at(1, h)] = two.astype(bf16)
        send(s4.at[at(x, h)], r4.at[at(0, h)], "sum", ("last z", h), ZF)
        send(s4.at[at(1 - x, h)], r4.at[at(2, h)], "sum", ("last", h), XP)
        send(s4.at[at(1 - x, h)], r4.at[at(1, h)], "sum", ("last", h), AN)

    for h in chunks:
        if h in DIRECT:
            group_sum(h)
    for h in chunks:
        if h not in DIRECT:
            late(h)
    for h in chunks:
        if h not in DIRECT:
            group_sum(h)

    arrived(mom.at[:, 1 - z1], "moment", ZF)

    def cut(index, h):
        return pl.ds(aligned(index * width + starts[h], 128), sizes[h])

    def pass_on(index, name, device, h):
        here = out_ref.at[:, cut(index, h)]
        send(here, here, "gather", (name, h) if device is not SIB else "sibling", device)

    def came(index, name, device, h):
        arrived(out_ref.at[:, cut(index, h)], (name, h), device)

    def moved(first_in, second_in, gradient):
        new_first = first_decay * first_in + (1.0 - first_decay) * gradient
        new_second = second_decay * second_in + (1.0 - second_decay) * gradient * gradient
        return new_first, new_second

    slabs = (x, 1 - x)
    tgt_in = tgt - 8 * z1
    y_in, z_in, d_in = y_t - 8 * z1, z0_t - 8 * z1, y_t + z0_t - tgt - 8 * z1

    steps = [(h, i) for h in chunks for i in (0, 1)]
    straight_steps = [steps[n] for n in DIRECT_STEPS]

    def adam(h, i):
        here = slice(starts[h], starts[h] + sizes[h])
        side = slabs[i]
        if i == 0:
            arrived(r4.at[at(0, h)], ("last z", h), ZF)
            gradient = (s4[at(x, h)].astype(f32) + r4[at(0, h)].astype(f32)) / pixels
        else:
            arrived(pieces(2 * sizes[h]), ("last", h), XP)
            gradient = (r4[at(1, h)].astype(f32) + r4[at(2, h)].astype(f32)) / pixels
        new_first, new_second = moved(mom[0, side, :, here].astype(f32), mom[1, side, :, here].astype(f32), gradient)
        update = learning_rate * (new_first / first_fix) / (jnp.sqrt(new_second / second_fix) + adam_eps)
        spot = tgt_in + 8 * side
        out_ref[:, cut(spot, h)] = (sup_v[:, cut(spot, h)].astype(f32) - update).astype(bf16)
        if (h, i) in straight_steps:
            pass_on(spot, ("own d", i), DG, h)
        pass_on(spot, ("own z", i), ZP, h)
        pass_on(spot, ("own y", i), YP, h)
        pass_on(spot, ("own s", i), SIB, h)

        @pl.when(side == z1)
        def _():
            new_first, new_second = moved(m1_ref[:, here], m2_ref[:, here], gradient)
            n1_ref[:, here] = new_first
            n2_ref[:, here] = new_second

    def relay(h, i):
        side = 8 * slabs[i]
        turned = steps.index((h, i)) in TURNED
        came(side + z_in, ("own z", i), ZP, h)
        if (h, i) not in straight_steps and not turned:
            pass_on(side + z_in, ("z y", i), YP, h)
        pass_on(side + z_in, ("z s", i), SIB, h)
        came(side + y_in, ("own y", i), YP, h)
        if (h, i) not in straight_steps and turned:
            pass_on(side + y_in, ("z y", i), ZP, h)
        pass_on(side + y_in, ("y s", i), SIB, h)

    def finish(h, i):
        side = 8 * slabs[i]
        if (h, i) in straight_steps:
            came(side + d_in, ("own d", i), DG, h)
        else:
            came(side + d_in, ("z y", i), YP, h)
        pass_on(side + d_in, ("d s", i), SIB, h)

    for n in range(len(steps) + LAG):
        if n < len(steps):
            adam(*steps[n])
        if n >= LAG:
            relay(*steps[n - LAG])
    for step in steps:
        finish(*step)
    arrived(out_ref.at[:, 0 : 8 * width], "sibling", SIB)
    all_sent(sup_v.at[:, 0 : 4 * width], "slab")
    all_sent(t_v.at[other_t, :], "targets")
    all_sent(lw.at[0:images, :], "weights")
    all_sent(dmsg_s, "diag")
    all_sent(cmsg_s, "cross")
    all_sent(low.at[0 : 3 * part, :], "low")
    all_sent(nmsg_r, "norm")
    all_sent(mom.at[:, 0], "moment")
    all_sent(pieces(counts["sum"]), "sum")
    all_sent(pieces(counts["gather"]), "gather")
    assert len(send_ids) <= SENDS and len(receive_ids) <= RECEIVES


def fused(targets, support, label_weights, labels, first_moment, second_moment):
    rows, _ = targets.shape
    images, pixels = support.shape
    width = first_moment.shape[1]
    classes = label_weights.shape[1]
    target_count = rows * lax.axis_size("tgt")
    support_count = images * lax.axis_size("sup")
    scale = 4.0 * pixels * math.sqrt(classes * support_count / target_count)
    everyone, part = 2 * images, rows // 2
    hbm = pl.BlockSpec(memory_space=pltpu.HBM)
    vmem = pl.BlockSpec(memory_space=pltpu.VMEM)
    slots = pltpu.VMEM((2, images, width), bf16)
    return pl.pallas_call(
        functools.partial(step_kernel, scale, pixels),
        out_shape=(
            pltpu.VMEM(support.shape, bf16),
            pltpu.VMEM(first_moment.shape, f32),
            pltpu.VMEM(first_moment.shape, f32),
        ),
        in_specs=[hbm] * 6,
        out_specs=(vmem, vmem, vmem),
        scratch_shapes=[
            pltpu.VMEM((2 * rows, 4 * width), bf16),
            pltpu.VMEM((everyone, 4 * width), bf16),
            pltpu.VMEM((images, pixels), bf16),
            pltpu.VMEM((everyone, classes), bf16),
            pltpu.VMEM((2 * rows, 128), f32),
            pltpu.VMEM((3, 16, everyone), f32),
            pltpu.VMEM((3, 16, everyone), f32),
            pltpu.VMEM((2 * rows, everyone), f32),
            pltpu.VMEM((3, part, everyone), bf16),
            pltpu.VMEM((3, part, everyone), bf16),
            pltpu.VMEM((2 * rows, everyone), bf16),
            pltpu.VMEM((8, everyone), f32),
            pltpu.VMEM((3, 8, everyone), f32),
            slots,
            slots,
            slots,
            slots,
            pltpu.VMEM((4, images, width), f32),
            slots,
            slots,
            slots,
            pltpu.VMEM((3, images, width), bf16),
            pltpu.VMEM((3, everyone, width), bf16),
            pltpu.VMEM((3, everyone, width), bf16),
            pltpu.VMEM((2, 2, images, width), bf16),
            pltpu.VMEM((1, rows), jnp.int32),
            pltpu.VMEM((images, width), f32),
            pltpu.VMEM((images, width), f32),
            pltpu.SemaphoreType.DMA((SENDS,)),
            pltpu.SemaphoreType.DMA((RECEIVES,)),
            pltpu.SemaphoreType.DMA((LOADS,)),
        ],
        compiler_params=pltpu.CompilerParams(
            collective_id=0, has_side_effects=True, vmem_limit_bytes=60000000
        ),
    )(targets, support, label_weights, labels[None, :], first_moment, second_moment)


def hand_over(a_ref, b_ref, c_ref, x_ref, y_ref, z_ref, sem):
    copies = [
        pltpu.make_async_copy(src, dst, sem.at[i])
        for i, (src, dst) in enumerate(((a_ref, x_ref), (b_ref, y_ref), (c_ref, z_ref)))
    ]
    for copy in copies:
        copy.start()
    for copy in copies:
        copy.wait()


def settle(support, first, second, space):
    return pl.pallas_call(
        hand_over,
        out_shape=tuple(jax.ShapeDtypeStruct(a.shape, a.dtype) for a in (support, first, second)),
        in_specs=[pl.BlockSpec(memory_space=space)] * 3,
        out_specs=(pl.BlockSpec(memory_space=pltpu.HBM),) * 3,
        scratch_shapes=[pltpu.SemaphoreType.DMA((3,))],
    )(support, first, second)


def pick(mesh):
    groups, shares = mesh.shape["sup"], mesh.shape["tgt"]

    def run(targets, support, label_weights, labels, first_moment, second_moment):
        width = first_moment.shape[1]
        fits = groups == 2 and shares == 16 and width == 128 * sum(CUTS)
        fits = fits and targets.shape[0] % 32 == 0 and groups * support.shape[0] == 128
        body = fused if fits else shards
        out = body(targets, support, label_weights, labels, first_moment, second_moment)
        return settle(*[pltpu.with_memory_space_constraint(o, pltpu.VMEM) for o in out], pltpu.VMEM) if fits else out

    return run


def solution(mesh):
    return jax.shard_map(
        pick(mesh),
        mesh=mesh,
        in_specs=(
            P("tgt", "sup"),
            P("sup", None),
            P("sup", None),
            P("tgt"),
            P("sup", "tgt"),
            P("sup", "tgt"),
        ),
        out_specs=(P("sup", None), P("sup", "tgt"), P("sup", "tgt")),
        check_vma=False,
    )
```

```python
import functools
import math

import jax
import jax.numpy as jnp
from jax import lax
from jax.experimental import pallas as pl
from jax.experimental.pallas import tpu as pltpu
from jax.sharding import PartitionSpec as P

DEPTH = 3


bias_var = 0.1
learning_rate = 0.05
first_decay = 0.9
second_decay = 0.99
first_fix = 1.0 - 0.9**10
second_fix = 1.0 - 0.99**10
adam_eps = 1e-08


def tangent_kernel(cross, target_diag, support_diag):
    tangent = cross
    current = cross
    left_diag = target_diag
    right_diag = support_diag
    for _ in range(DEPTH):
        product = (1.0 + 2.0 * left_diag)[:, None] * (1.0 + 2.0 * right_diag)[None, :]
        slope = 4.0 / math.pi / jnp.sqrt(product - 4.0 * current * current)
        current = 2.0 / math.pi * jnp.arcsin(2.0 * current / jnp.sqrt(product)) + bias_var
        tangent = current + slope * tangent
        left_diag = 2.0 / math.pi * jnp.arcsin(2.0 * left_diag / (1.0 + 2.0 * left_diag)) + bias_var
        right_diag = (
            2.0 / math.pi * jnp.arcsin(2.0 * right_diag / (1.0 + 2.0 * right_diag)) + bias_var
        )
    return tangent


def row_squares(images):
    return jnp.sum(jnp.square(images.astype(jnp.float32)), axis=1)


def shards(targets, support, label_weights, labels, first_moment, second_moment):
    pixels = support.shape[1]
    target_count = targets.shape[0] * lax.axis_size("tgt")
    support_count = support.shape[0] * lax.axis_size("sup")
    class_count = label_weights.shape[1]
    support_diag = row_squares(support) / pixels + bias_var
    slabs = lax.all_to_all(support, "sup", split_axis=1, concat_axis=0, tiled=True)
    partial_cross = lax.dot_general(
        targets, slabs, (((1,), (1,)), ((), ())), preferred_element_type=jnp.float32
    )
    cross = (
        lax.psum_scatter(
            partial_cross.astype(jnp.bfloat16), "sup", scatter_dimension=1, tiled=True
        ).astype(jnp.float32)
        / pixels
        + bias_var
    )
    target_diag = lax.psum(row_squares(targets), "sup") / pixels + bias_var

    def kernel_of(cross_in, diag_in):
        return tangent_kernel(cross_in, target_diag, diag_in)

    kernel, pullback = jax.vjp(kernel_of, cross, support_diag)
    partial_pred = jnp.dot(
        kernel.astype(jnp.bfloat16), label_weights, preferred_element_type=jnp.float32
    )
    predicted = lax.psum(partial_pred.astype(jnp.bfloat16), "sup").astype(jnp.float32)
    classes = jnp.arange(class_count, dtype=jnp.int32)
    onehot = (labels[:, None] == classes[None, :]).astype(jnp.float32)
    residual = (predicted - onehot).astype(jnp.bfloat16)
    kernel_grad = lax.dot_general(
        residual, label_weights, (((1,), (1,)), ((), ())), preferred_element_type=jnp.float32
    )
    kernel_grad = kernel_grad * (
        4.0 * pixels * math.sqrt(class_count * support_count / target_count)
    )
    cross_grad, norm_grad = pullback(kernel_grad)
    cross_low = cross_grad.astype(jnp.bfloat16)
    all_grads = lax.all_gather(cross_low, "sup", axis=1, tiled=True)
    slab_grad = lax.dot_general(
        all_grads, targets, (((0,), (0,)), ((), ())), preferred_element_type=jnp.float32
    )
    image_grad = lax.all_to_all(
        slab_grad.astype(jnp.bfloat16), "sup", split_axis=0, concat_axis=1, tiled=True
    ).astype(slab_grad.dtype)
    gradient = (image_grad + 2.0 * norm_grad[:, None] * support.astype(jnp.float32)) / pixels
    shares = lax.psum_scatter(gradient, "tgt", scatter_dimension=1, tiled=True)
    slab_width = shares.shape[1]
    own_pixels = lax.dynamic_slice_in_dim(
        support, lax.axis_index("tgt") * slab_width, slab_width, 1
    ).astype(jnp.float32)
    new_first = first_decay * first_moment + (1.0 - first_decay) * shares
    new_second = second_decay * second_moment + (1.0 - second_decay) * shares * shares
    update = (
        learning_rate * (new_first / first_fix) / (jnp.sqrt(new_second / second_fix) + adam_eps)
    )
    new_slab = (own_pixels - update).astype(jnp.bfloat16)
    new_support = lax.all_gather(new_slab, "tgt", axis=1, tiled=True)
    return (new_support, new_first, new_second)


MESH = pl.DeviceIdType.MESH
f32 = jnp.float32
bf16 = jnp.bfloat16


@jax.custom_jvp
def arcsine(x):
    a = jnp.abs(x)
    big = a > 0.5
    z = jnp.where(big, 0.5 * (1.0 - a), a * a)
    s = jnp.where(big, jnp.sqrt(z), a)
    p = 4.2163199048e-2 * z + 2.4181311049e-2
    p = p * z + 4.5470025998e-2
    p = p * z + 7.4953002686e-2
    p = p * z + 1.6666752422e-1
    p = p * z * s + s
    r = jnp.where(big, math.pi / 2.0 - 2.0 * p, p)
    return jnp.where(x < 0.0, -r, r)


@arcsine.defjvp
def arcsine_jvp(primals, tangents):
    (x,) = primals
    (t,) = tangents
    return arcsine(x), t * lax.rsqrt(1.0 - x * x)


def tangent_tile(cross, target_diag, support_diag):
    tangent = cross
    current = cross
    left = target_diag
    right = support_diag
    for _ in range(DEPTH):
        product = (1.0 + 2.0 * left) * (1.0 + 2.0 * right)
        slope = 4.0 / math.pi * lax.rsqrt(product - 4.0 * current * current)
        current = 2.0 / math.pi * arcsine(2.0 * current * lax.rsqrt(product)) + bias_var
        tangent = current + slope * tangent
        left = 2.0 / math.pi * arcsine(2.0 * left / (1.0 + 2.0 * left)) + bias_var
        right = 2.0 / math.pi * arcsine(2.0 * right / (1.0 + 2.0 * right)) + bias_var
    return tangent


def to_row(col, offset, lanes):
    shape = (col.shape[0], lanes)
    hit = lax.broadcasted_iota(jnp.int32, shape, 1) == lax.broadcasted_iota(jnp.int32, shape, 0) + offset
    return jnp.sum(jnp.where(hit, col, 0.0), axis=0, keepdims=True)


def to_col(row, count, offset=0):
    shape = (count, row.shape[1])
    hit = lax.broadcasted_iota(jnp.int32, shape, 1) == lax.broadcasted_iota(jnp.int32, shape, 0) + offset
    return jnp.sum(jnp.where(hit, row, 0.0), axis=1, keepdims=True)


SENDS, RECEIVES, LOADS = 8, 43, 7
CUTS = (2, 2, 2)
STRIPS = 2
DIRECT = (0,)
DIRECT_STEPS = (3, 4, 5)
LAG = 4
TURNED = ()


def support_chain(diag):
    factors, rates = [], []
    right = diag
    for _ in range(DEPTH):
        plus = 1.0 + 2.0 * right
        factors.append(plus)
        rates.append(4.0 / math.pi / (plus * jnp.sqrt(1.0 + 4.0 * right)))
        right = 2.0 / math.pi * arcsine(2.0 * right / plus) + bias_var
    return factors, rates


def target_chain(diag):
    roots = []
    left = diag
    for _ in range(DEPTH):
        plus = 1.0 + 2.0 * left
        roots.append(lax.rsqrt(plus))
        left = 2.0 / math.pi * arcsine(2.0 * left / plus) + bias_var
    return roots


def forward(cross, roots, factors):
    tangent, current = cross, cross
    saved = []
    for root, plus in zip(roots, factors):
        twice = root * (2.0 * lax.rsqrt(plus))
        sine = current * twice
        inverse = lax.rsqrt(1.0 - sine * sine)
        slope = 2.0 / math.pi * twice * inverse
        saved.append((twice, sine, inverse, slope, tangent))
        current = 2.0 / math.pi * arcsine(sine) + bias_var
        tangent = current + slope * tangent
    return tangent, saved


def backward(grad, saved, factors, rates):
    tangent_bar, current_bar = grad, jnp.zeros_like(grad)
    diag_bar = None
    for layer in reversed(range(DEPTH)):
        twice, sine, inverse, slope, tangent = saved[layer]
        total = current_bar + tangent_bar
        next_bar = tangent_bar * slope
        carried = next_bar * tangent * inverse * inverse
        direct = -jnp.sum(carried + 2.0 / math.pi * total * inverse * sine, axis=0, keepdims=True) / factors[layer]
        diag_bar = direct if diag_bar is None else direct + diag_bar * rates[layer]
        current_bar = total * slope + twice * sine * carried
        tangent_bar = next_bar
    return current_bar + tangent_bar, diag_bar


def step_kernel(
    scale, pixels,
    t_hbm, s_hbm, w_hbm, labels_hbm, m1_hbm, m2_hbm,
    out_ref, n1_ref, n2_ref,
    t_v, slab, sup_v, lw, tacc, dmsg_s, dmsg_r, cacc, cmsg_s, cmsg_r, low, nmsg_s, nmsg_r,
    sy, sz, ry, rz, keep, s3, r3, s4, r4, ds, dr, mom, labels_ref, m1_ref, m2_ref,
    send_sem, recv_sem, local_sem,
):
    tgt = lax.axis_index("tgt")
    x = lax.axis_index("sup")
    core = lax.rem(tgt, 2)
    yy = lax.rem(tgt // 2, 2)
    z0 = lax.rem(tgt // 4, 2)
    z1 = tgt // 8
    sib_t = tgt + 1 - 2 * core
    y_t = tgt + 2 - 4 * yy
    z0_t = tgt + 4 - 8 * z0
    z1_t = tgt + 8 - 16 * z1
    SIB, YP, ZP, ZF = (sib_t, x), (y_t, x), (z0_t, x), (z1_t, x)
    XP, XS, AN = (tgt, 1 - x), (sib_t, 1 - x), (z1_t, 1 - x)
    DG = (y_t + z0_t - tgt, x)

    images, width = n1_ref.shape
    rows = t_v.shape[0] // 2
    half = 8 * width
    part = rows // 2
    lanes = slab.shape[0]
    sizes = [128 * n for n in CUTS]
    starts = [sum(sizes[:h]) for h in range(len(sizes))]
    chunks = range(len(sizes))

    send_ids, receive_ids, counts = {}, {}, {}

    def remote(src, dst, sent, name, device):
        return pltpu.make_async_remote_copy(
            src_ref=src, dst_ref=dst, send_sem=send_sem.at[send_ids.setdefault(sent, len(send_ids))],
            recv_sem=recv_sem.at[receive_ids.setdefault(name, len(receive_ids))],
            device_id=device, device_id_type=MESH,
        )

    def send(src, dst, sent, name, device):
        counts[sent] = counts.get(sent, 0) + src.shape[0] * src.shape[-1] // images
        remote(src, dst, sent, name, device).start()

    def arrived(dst, name, device):
        pltpu.make_async_remote_copy(
            src_ref=dst, dst_ref=dst, send_sem=send_sem.at[0],
            recv_sem=recv_sem.at[receive_ids.setdefault(name, len(receive_ids))],
            device_id=device, device_id_type=MESH,
        ).wait_recv()

    def all_sent(src, sent):
        pltpu.make_async_remote_copy(
            src_ref=src, dst_ref=src, send_sem=send_sem.at[send_ids[sent]], recv_sem=recv_sem.at[0],
            device_id=SIB, device_id_type=MESH,
        ).wait_send()

    def aligned(value, by):
        return pl.multiple_of(value, by)

    barrier = pltpu.get_barrier_semaphore()
    friends = (XP, XS, SIB, YP, ZP, DG, ZF, AN)
    for device in friends:
        pl.semaphore_signal(barrier, inc=1, device_id=device, device_id_type=MESH)

    def load(src, dst, number):
        copy = pltpu.make_async_copy(src, dst, local_sem.at[number])
        copy.start()
        return copy

    my_row = aligned(x * images, images)
    peer_row = aligned((1 - x) * images, images)

    def columns(block, owner):
        return pl.ds(aligned((2 * block + owner) * width, width), width)

    def far_columns(slab_index, block):
        return pl.ds(aligned(slab_index * half + (2 * block + core) * width, width), width)

    def block_of(j):
        return pl.ds(aligned(j * width, width), width)

    load_s = load(s_hbm, sup_v, 0)
    mine_t = pl.ds(aligned(core * rows, rows), rows)
    for j in range(4):
        load(t_hbm.at[:, columns(j, core)], t_v.at[mine_t, block_of(j)], 1)
    load_t = pltpu.make_async_copy(t_v.at[mine_t, :], t_v.at[mine_t, :], local_sem.at[1])
    for j in range(4):
        load(s_hbm.at[:, far_columns(x, j)], slab.at[pl.ds(my_row, images), block_of(j)], 2)
    my_slab = slab.at[pl.ds(my_row, images), :]
    load_o = pltpu.make_async_copy(my_slab, my_slab, local_sem.at[2])
    load_w = load(w_hbm, lw.at[pl.ds(my_row, images), :], 3)
    load_l = load(labels_hbm, labels_ref, 4)
    load_1 = load(m1_hbm, m1_ref, 5)
    load_2 = load(m2_hbm, m2_ref, 6)

    pl.semaphore_wait(barrier, len(friends))

    seat = 2 * yy + z0
    turn = (seat, 3 - seat, seat + 2 - 4 * yy, seat + 1 - 2 * z0)
    strip = images // STRIPS
    strips = range(STRIPS)
    share = images // 2

    def send_strip(p, r):
        send(
            s_hbm.at[pl.ds(r * strip, strip), far_columns(1 - x, turn[p])],
            slab.at[pl.ds(aligned(my_row + r * strip, strip), strip), block_of(turn[p])],
            "slab", ("slab", p, r), XP,
        )

    for r in strips:
        send_strip(0, r)

    def whole(ref, row, columns):
        return ref.at[pl.ds(row, images), columns]

    send(
        s_hbm.at[:, far_columns(1 - x, turn[1])], whole(slab, my_row, block_of(turn[1])), "slab", "slab", XP,
    )
    for j in range(4):
        send(t_hbm.at[:, columns(j, 1 - core)], t_v.at[mine_t, block_of(j)], "targets", "targets", SIB)
    load_1.wait()
    mom[0, z1] = m1_ref[...].astype(bf16)
    here = mom.at[0, z1]
    send(here, here, "moment", "moment", ZF)

    load_s.wait()

    def support_squares(i, acc):
        block = sup_v[:, pl.ds(aligned(i * width, width), width)].astype(f32)
        block = block * block
        for k in range(width // 128):
            acc = acc + block[:, k * 128 : (k + 1) * 128]
        return acc

    sacc = lax.fori_loop(0, pixels // width, support_squares, jnp.zeros((images, 128), f32))
    s_row = to_row(jnp.sum(sacc, axis=1, keepdims=True), x * images, lanes)

    def target_squares(first):
        def body(i, carry):
            where = pl.ds(aligned(first + i * 16, 16), 16)
            sums = []
            for j in range(4):
                block = t_v[where, j * width : (j + 1) * width].astype(f32)
                block = block * block
                acc = block[:, 0:128]
                for k in range(1, width // 128):
                    acc = acc + block[:, k * 128 : (k + 1) * 128]
                sums.append(acc)
            tacc[where, :] = (sums[0] + sums[1]) + (sums[2] + sums[3])
            return carry

        lax.fori_loop(0, rows // 16, body, 0)

    load_t.wait()
    target_squares(core * rows)

    def strip_of(p, r):
        return slab.at[pl.ds(aligned(peer_row + r * strip, strip), strip), block_of(turn[p])]

    for r in strips:
        here = strip_of(0, r)
        arrived(here, ("slab", 0, r), XP)
        send(here, here, "slab", "slab y", YP)
        send(here, here, "slab", "slab z", ZP)

    weight_rows = pl.ds(aligned(my_row + core * share, share), share)
    send(w_hbm.at[pl.ds(aligned(core * share, share), share), :], lw.at[weight_rows, :], "weights", "weights", XP)

    other_t = pl.ds(aligned((1 - core) * rows, rows), rows)
    arrived(t_v.at[other_t, :], "targets", SIB)
    target_squares((1 - core) * rows)

    group = (SIB, XP, XS)
    quarter = 2 * core + x
    theirs = (2 * (1 - core) + x, 2 * core + 1 - x, 2 * (1 - core) + 1 - x)

    def rows_of(q):
        return pl.ds(aligned(q * part, part), part)

    def square_col(q):
        return jnp.sum(tacc[rows_of(q), :], axis=1, keepdims=True)

    for i in range(3):
        dmsg_s[i, 0:8, :] = jnp.broadcast_to(to_row(square_col(theirs[i]), 0, lanes), (8, lanes))
        dmsg_s[i, 8:16, :] = jnp.broadcast_to(s_row, (8, lanes))
        send(dmsg_s.at[i], dmsg_r.at[i], "small", "diag", group[i])
    my_sq = square_col(quarter)
    load_l.wait()
    label_col = to_col(labels_ref[...].astype(f32), part, x * part)

    load_o.wait()

    def cross_piece(p, first=False):
        value = lax.dot_general(
            t_v[:, block_of(turn[p])], slab[:, block_of(turn[p])], (((1,), (1,)), ((), ())),
            preferred_element_type=f32,
        )
        cacc[...] = value if first else cacc[...] + value

    cross_piece(0, True)
    arrived(whole(slab, peer_row, block_of(turn[1])), "slab", XP)
    cross_piece(1)
    arrived(whole(slab, peer_row, block_of(turn[2])), "slab y", YP)
    cross_piece(2)
    arrived(whole(slab, peer_row, block_of(turn[3])), "slab z", ZP)

    def last_piece(q):
        return cacc[rows_of(q), :] + lax.dot_general(
            t_v[rows_of(q), block_of(turn[3])], slab[:, block_of(turn[3])], (((1,), (1,)), ((), ())),
            preferred_element_type=f32,
        )

    for i in (2, 1, 0):
        cmsg_s[i] = last_piece(theirs[i]).astype(bf16)
        send(cmsg_s.at[i], cmsg_r.at[i], "rows", "cross", group[i])
    own_cross = last_piece(quarter)
    half_rows = lw.at[pl.ds(aligned(peer_row + core * share, share), share), :]
    arrived(half_rows, "weights", XP)
    send(half_rows, half_rows, "weights", "weights on", SIB)
    load_2.wait()
    mom[1, z1] = m2_ref[...].astype(bf16)
    here = mom.at[1, z1]
    send(here, here, "moment", "moment", ZF)

    arrived(dmsg_r, "diag", SIB)
    square_row = dmsg_r[0, 0:1, :] + dmsg_r[1, 0:1, :] + dmsg_r[2, 0:1, :]
    roots = target_chain((my_sq + to_col(square_row, part)) / pixels + bias_var)
    factors, rates = support_chain((s_row + dmsg_r[1, 8:9, :]) / pixels + bias_var)
    load_w.wait()
    arrived(lw.at[pl.ds(aligned(peer_row + (1 - core) * share, share), share), :], "weights on", SIB)

    arrived(cmsg_r, "cross", SIB)
    total = own_cross + cmsg_r[0].astype(f32)
    total = total + (cmsg_r[1].astype(f32) + cmsg_r[2].astype(f32))
    kernel, saved = forward(total / pixels + bias_var, roots, factors)
    weights = lw[...]
    predicted = jnp.dot(kernel.astype(bf16), weights, preferred_element_type=f32)
    classes = lax.broadcasted_iota(jnp.int32, predicted.shape, 1)
    onehot = (label_col == classes.astype(f32)).astype(f32)
    residual = (predicted - onehot).astype(bf16)
    kernel_grad = scale * lax.dot_general(
        residual, weights, (((1,), (1,)), ((), ())), preferred_element_type=f32
    )
    cross_grad, norm_grad = backward(kernel_grad, saved, factors, rates)
    mine_low = low.at[rows_of(quarter), :]
    mine_low[...] = cross_grad.astype(bf16)
    for i in (2, 1, 0):
        send(mine_low, mine_low, "rows", "low", group[i])
    nmsg_s[...] = jnp.broadcast_to(norm_grad, nmsg_s.shape)
    for i in (2, 1, 0):
        send(nmsg_s, nmsg_r.at[i], "small", "norm", group[i])
    arrived(low.at[0 : 3 * part, :], "low", SIB)
    arrived(nmsg_r, "norm", SIB)
    norm_row = norm_grad + nmsg_r[0, 0:1, :] + nmsg_r[1, 0:1, :] + nmsg_r[2, 0:1, :]
    norm_col = to_col(2.0 * norm_row, lanes)
    grads = low[...].astype(f32).T.astype(bf16)

    order = ((1, 1), (0, 1), (1, 0), (0, 0))
    first = slice(0, images)
    second = slice(images, 2 * images)

    def at(k, h):
        return (k, slice(None), slice(starts[h], starts[h] + sizes[h]))

    def block_grad(k, h):
        dz, dy = order[k]
        number = (z0 + dz - 2 * dz * z0) * 2 + (yy + dy - 2 * dy * yy)
        where = pl.ds(aligned(number * width + starts[h], 128), sizes[h])
        value = jnp.dot(grads, t_v[:, where], preferred_element_type=f32)
        return value + norm_col * slab[:, where].astype(f32)

    for h in chunks:
        if h in DIRECT:
            for k, device in enumerate((DG, YP, ZP)):
                here = at(k, h)
                ds[here] = block_grad(k, h).astype(bf16)
                send(ds.at[here], dr.at[here], "sum", ("sum", h), device)
            continue
        value = block_grad(0, h)
        sy[at(0, h)] = value[first].astype(bf16)
        send(sy.at[at(0, h)], ry.at[at(0, h)], "sum", ("pair", h), YP)
        sz[at(0, h)] = value[second].astype(bf16)
        send(sz.at[at(0, h)], rz.at[at(0, h)], "sum", ("pair", h), ZP)
        value = block_grad(1, h)
        sy[at(1, h)] = value[first].astype(bf16)
        send(sy.at[at(1, h)], ry.at[at(1, h)], "sum", ("sum", h), YP)
        keep[at(0, h)] = value[second]
        value = block_grad(2, h)
        sz[at(1, h)] = value[second].astype(bf16)
        send(sz.at[at(1, h)], rz.at[at(1, h)], "sum", ("sum", h), ZP)
        keep[at(1, h)] = value[first]
    for h in chunks:
        value = block_grad(3, h)
        keep[at(2, h)] = value[first]
        keep[at(3, h)] = value[second]

    def pieces(count):
        return sup_v.at[:, 0:count]

    def late(h):
        arrived(pieces(2 * sizes[h]), ("pair", h), YP)
        s3[at(0, h)] = (keep[at(1, h)] + ry[at(0, h)].astype(f32)).astype(bf16)
        send(s3.at[at(0, h)], r3.at[at(0, h)], "sum", ("sum", h), ZP)
        s3[at(1, h)] = (keep[at(0, h)] + rz[at(0, h)].astype(f32)).astype(bf16)
        send(s3.at[at(1, h)], r3.at[at(1, h)], "sum", ("sum", h), YP)

    def group_sum(h):
        arrived(pieces((6 if h in DIRECT else 4) * sizes[h]), ("sum", h), YP)
        if h in DIRECT:
            extra = dr[at(0, h)].astype(f32) + dr[at(1, h)].astype(f32) + dr[at(2, h)].astype(f32)
            one = keep[at(2, h)] + extra[first]
            two = keep[at(3, h)] + extra[second]
        else:
            one = (keep[at(2, h)] + ry[at(1, h)].astype(f32)) + r3[at(0, h)].astype(f32)
            two = (keep[at(3, h)] + rz[at(1, h)].astype(f32)) + r3[at(1, h)].astype(f32)
        s4[at(0, h)] = one.astype(bf16)
        s4[at(1, h)] = two.astype(bf16)
        send(s4.at[at(x, h)], r4.at[at(0, h)], "sum", ("last z", h), ZF)
        send(s4.at[at(1 - x, h)], r4.at[at(2, h)], "sum", ("last", h), XP)
        send(s4.at[at(1 - x, h)], r4.at[at(1, h)], "sum", ("last", h), AN)

    for h in chunks:
        if h in DIRECT:
            group_sum(h)
    for h in chunks:
        if h not in DIRECT:
            late(h)
    for h in chunks:
        if h not in DIRECT:
            group_sum(h)

    arrived(mom.at[:, 1 - z1], "moment", ZF)

    def cut(index, h):
        return pl.ds(aligned(index * width + starts[h], 128), sizes[h])

    def pass_on(index, name, device, h):
        here = out_ref.at[:, cut(index, h)]
        send(here, here, "gather", (name, h) if device is not SIB else "sibling", device)

    def came(index, name, device, h):
        arrived(out_ref.at[:, cut(index, h)], (name, h), device)

    def moved(first_in, second_in, gradient):
        new_first = first_decay * first_in + (1.0 - first_decay) * gradient
        new_second = second_decay * second_in + (1.0 - second_decay) * gradient * gradient
        return new_first, new_second

    slabs = (x, 1 - x)
    tgt_in = tgt - 8 * z1
    y_in, z_in, d_in = y_t - 8 * z1, z0_t - 8 * z1, y_t + z0_t - tgt - 8 * z1

    steps = [(h, i) for h in chunks for i in (0, 1)]
    straight_steps = [steps[n] for n in DIRECT_STEPS]

    def adam(h, i):
        here = slice(starts[h], starts[h] + sizes[h])
        side = slabs[i]
        if i == 0:
            arrived(r4.at[at(0, h)], ("last z", h), ZF)
            gradient = (s4[at(x, h)].astype(f32) + r4[at(0, h)].astype(f32)) / pixels
        else:
            arrived(pieces(2 * sizes[h]), ("last", h), XP)
            gradient = (r4[at(1, h)].astype(f32) + r4[at(2, h)].astype(f32)) / pixels
        new_first, new_second = moved(mom[0, side, :, here].astype(f32), mom[1, side, :, here].astype(f32), gradient)
        update = learning_rate * (new_first / first_fix) / (jnp.sqrt(new_second / second_fix) + adam_eps)
        spot = tgt_in + 8 * side
        out_ref[:, cut(spot, h)] = (sup_v[:, cut(spot, h)].astype(f32) - update).astype(bf16)
        pass_on(spot, ("own y", i), YP, h)
        if (h, i) in straight_steps:
            pass_on(spot, ("own d", i), DG, h)
        pass_on(spot, ("own z", i), ZP, h)
        pass_on(spot, ("own s", i), SIB, h)

        @pl.when(side == z1)
        def _():
            new_first, new_second = moved(m1_ref[:, here], m2_ref[:, here], gradient)
            n1_ref[:, here] = new_first
            n2_ref[:, here] = new_second

    def relay(h, i):
        side = 8 * slabs[i]
        turned = steps.index((h, i)) in TURNED
        came(side + z_in, ("own z", i), ZP, h)
        if (h, i) not in straight_steps and not turned:
            pass_on(side + z_in, ("z y", i), YP, h)
        pass_on(side + z_in, ("z s", i), SIB, h)
        came(side + y_in, ("own y", i), YP, h)
        if (h, i) not in straight_steps and turned:
            pass_on(side + y_in, ("z y", i), ZP, h)
        pass_on(side + y_in, ("y s", i), SIB, h)

    def finish(h, i):
        side = 8 * slabs[i]
        if (h, i) in straight_steps:
            came(side + d_in, ("own d", i), DG, h)
        else:
            came(side + d_in, ("z y", i), YP, h)
        pass_on(side + d_in, ("d s", i), SIB, h)

    for n in range(len(steps) + LAG):
        if n < len(steps):
            adam(*steps[n])
        if n >= LAG:
            relay(*steps[n - LAG])
    for step in steps:
        finish(*step)
    arrived(out_ref.at[:, 0 : 8 * width], "sibling", SIB)
    all_sent(sup_v.at[:, 0 : 4 * width], "slab")
    all_sent(t_v.at[other_t, :], "targets")
    all_sent(lw.at[0:images, :], "weights")
    all_sent(t_v.at[0 : 3 * part, 0:256], "rows")
    all_sent(cacc.at[0 : 3 * 24, :], "small")
    all_sent(mom.at[:, 0], "moment")
    all_sent(pieces(counts["sum"]), "sum")
    all_sent(pieces(counts["gather"]), "gather")
    assert len(send_ids) <= SENDS and len(receive_ids) <= RECEIVES


def fused(targets, support, label_weights, labels, first_moment, second_moment):
    rows, _ = targets.shape
    images, pixels = support.shape
    width = first_moment.shape[1]
    classes = label_weights.shape[1]
    target_count = rows * lax.axis_size("tgt")
    support_count = images * lax.axis_size("sup")
    scale = 4.0 * pixels * math.sqrt(classes * support_count / target_count)
    everyone, part = 2 * images, rows // 2
    hbm = pl.BlockSpec(memory_space=pltpu.HBM)
    vmem = pl.BlockSpec(memory_space=pltpu.VMEM)
    slots = pltpu.VMEM((2, images, width), bf16)
    return pl.pallas_call(
        functools.partial(step_kernel, scale, pixels),
        out_shape=(
            pltpu.VMEM(support.shape, bf16),
            pltpu.VMEM(first_moment.shape, f32),
            pltpu.VMEM(first_moment.shape, f32),
        ),
        in_specs=[hbm] * 6,
        out_specs=(vmem, vmem, vmem),
        scratch_shapes=[
            pltpu.VMEM((2 * rows, 4 * width), bf16),
            pltpu.VMEM((everyone, 4 * width), bf16),
            pltpu.VMEM((images, pixels), bf16),
            pltpu.VMEM((everyone, classes), bf16),
            pltpu.VMEM((2 * rows, 128), f32),
            pltpu.VMEM((3, 16, everyone), f32),
            pltpu.VMEM((3, 16, everyone), f32),
            pltpu.VMEM((2 * rows, everyone), f32),
            pltpu.VMEM((3, part, everyone), bf16),
            pltpu.VMEM((3, part, everyone), bf16),
            pltpu.VMEM((2 * rows, everyone), bf16),
            pltpu.VMEM((8, everyone), f32),
            pltpu.VMEM((3, 8, everyone), f32),
            slots,
            slots,
            slots,
            slots,
            pltpu.VMEM((4, images, width), f32),
            slots,
            slots,
            slots,
            pltpu.VMEM((3, images, width), bf16),
            pltpu.VMEM((3, everyone, width), bf16),
            pltpu.VMEM((3, everyone, width), bf16),
            pltpu.VMEM((2, 2, images, width), bf16),
            pltpu.VMEM((1, rows), jnp.int32),
            pltpu.VMEM((images, width), f32),
            pltpu.VMEM((images, width), f32),
            pltpu.SemaphoreType.DMA((SENDS,)),
            pltpu.SemaphoreType.DMA((RECEIVES,)),
            pltpu.SemaphoreType.DMA((LOADS,)),
        ],
        compiler_params=pltpu.CompilerParams(
            collective_id=0, has_side_effects=True, vmem_limit_bytes=60000000
        ),
    )(targets, support, label_weights, labels[None, :], first_moment, second_moment)


def hand_over(a_ref, b_ref, c_ref, x_ref, y_ref, z_ref, sem):
    copies = [
        pltpu.make_async_copy(src, dst, sem.at[i])
        for i, (src, dst) in enumerate(((a_ref, x_ref), (b_ref, y_ref), (c_ref, z_ref)))
    ]
    for copy in copies:
        copy.start()
    for copy in copies:
        copy.wait()


def settle(support, first, second, space):
    return pl.pallas_call(
        hand_over,
        out_shape=tuple(jax.ShapeDtypeStruct(a.shape, a.dtype) for a in (support, first, second)),
        in_specs=[pl.BlockSpec(memory_space=space)] * 3,
        out_specs=(pl.BlockSpec(memory_space=pltpu.HBM),) * 3,
        scratch_shapes=[pltpu.SemaphoreType.DMA((3,))],
    )(support, first, second)


def pick(mesh):
    groups, shares = mesh.shape["sup"], mesh.shape["tgt"]

    def run(targets, support, label_weights, labels, first_moment, second_moment):
        width = first_moment.shape[1]
        fits = groups == 2 and shares == 16 and width == 128 * sum(CUTS)
        fits = fits and targets.shape[0] % 32 == 0 and groups * support.shape[0] == 128
        body = fused if fits else shards
        out = body(targets, support, label_weights, labels, first_moment, second_moment)
        return settle(*[pltpu.with_memory_space_constraint(o, pltpu.VMEM) for o in out], pltpu.VMEM) if fits else out

    return run


def solution(mesh):
    return jax.shard_map(
        pick(mesh),
        mesh=mesh,
        in_specs=(
            P("tgt", "sup"),
            P("sup", None),
            P("sup", None),
            P("tgt"),
            P("sup", "tgt"),
            P("sup", "tgt"),
        ),
        out_specs=(P("sup", None), P("sup", "tgt"), P("sup", "tgt")),
        check_vma=False,
    )
```
